32 devices in a mesh: ctx: 8 (over z, y), wa: 4 (over x, core).
Axes of the slice: x: 2, y: 2, z: 4, core: 2. Of those that a mesh axis runs over, the one named last changes fastest.
Arguments:
- tokens: bfloat16 [4, 8, 2, 128, 1536], P('wa', 'ctx'), may hold values from -6 to 6
- doc_starts: int32 [4, 8], P('wa'), may hold values from 0 to 2047, as said below
- routes: int32 [4, 8, 2, 128, 6], P('wa', 'ctx'), may hold values from 0 to 15, all different within a row; in each aligned block of 256 rows (0 to 255, 256 to 511, ..., all dimensions but the last counted through in order) at most 192 rows name the same one
- norm_gain_1: bfloat16 [1536], P('wa'), may hold values from 0.5 to 1.5
- query_weight: bfloat16 [1536, 1536], P('wa'), may hold values from -0.21875 to 0.21875
- key_matrix: bfloat16 [1536, 512], P('wa'), may hold values from -0.21875 to 0.21875
- value_matrix: bfloat16 [1536, 512], P('wa'), may hold values from -0.15625 to 0.15625
- out_weight: bfloat16 [1536, 1536], P(None, 'wa'), may hold values from -2 to 2
- norm_gain_2: bfloat16 [1536], P('wa'), may hold values from 0.5 to 1.5
- router_weight: bfloat16 [1536, 16], P('wa'), may hold values from -0.078125 to 0.078125
- shared_gate: bfloat16 [1536, 1024], P('wa'), may hold values from -0.15625 to 0.15625
- shared_up: bfloat16 [1536, 1024], P('wa'), may hold values from -0.15625 to 0.15625
- shared_down: bfloat16 [1024, 1536], P(None, 'wa'), may hold values from -0.375 to 0.375
- expert_gate: bfloat16 [16, 1536, 512], P('wa'), may hold values from -0.15625 to 0.15625
- expert_up: bfloat16 [16, 1536, 512], P('wa'), may hold values from -0.15625 to 0.15625
- expert_down: bfloat16 [16, 512, 1536], P('wa'), may hold values from -0.75 to 0.75
- out_grad: bfloat16 [4, 8, 2, 128, 1536], P('wa', 'ctx'), may hold values from -6 to 6
Outputs:
- block_out: bfloat16 [4, 8, 2, 128, 1536], P('wa', 'ctx')
- tokens_grad: bfloat16 [4, 8, 2, 128, 1536], P('wa', 'ctx')
- norm_gain_1_grad: float32 [1536], P(('ctx', 'wa'))
- query_weight_grad: float32 [1536, 1536], P(('ctx', 'wa'))
- key_weight_grad: float32 [1536, 512], P(('ctx', 'wa'))
- value_weight_grad: float32 [1536, 512], P(('ctx', 'wa'))
- out_weight_grad: float32 [1536, 1536], P(None, ('ctx', 'wa'))
- norm_gain_2_grad: float32 [1536], P(('ctx', 'wa'))
- router_weight_grad: float32 [1536, 16], P(('ctx', 'wa'))
- shared_gate_grad: float32 [1536, 1024], P(('ctx', 'wa'))
- shared_up_grad: float32 [1536, 1024], P(('ctx', 'wa'))
- shared_down_grad: float32 [1024, 1536], P(None, ('ctx', 'wa'))
- expert_gate_grad: float32 [16, 1536, 512], P('wa', 'ctx')
- expert_up_grad: float32 [16, 1536, 512], P('wa', 'ctx')
- expert_down_grad: float32 [16, 512, 1536], P('wa', None, 'ctx')
The draws below stay inside these ranges and needn't reach their ends.
Inputs may be any that keep to these rules, and one draw needn't show every extreme that they name: doc_starts[s, 0] is 0 and each row rises strictly; the 8 documents of a stream (the last one ending at the stream's end) have 1 to 1024 tokens, and one of them has exactly 1024. `routes`: the 6 experts of a token are different; among the 256 tokens of one device no expert is chosen more than 192 times, and in every draw some device chooses some expert exactly 192 times.
All inputs are finite; a program needn't handle non-finite values.
Results may differ from the reference program's by a relative error of at most 0.018.
The reference program's roundings to bfloat16 on the way count: a program that leaves them out, or rounds other values in their place, can miss the bound.
Values may be sent and summed in bfloat16 or wider, within the bound.
No kernel may reach another device: no remote copies, remote signals or barrier semaphores. Data moves between devices by JAX's collectives and lax.ppermute only.
A program may use at most 320 MiB of HBM per device.

```python
import math
from functools import partial
import jax
import jax.numpy as jnp
import numpy as np
from jax import lax

MODEL_DIM = 1536
QUERY_HEADS = 12
KEY_VALUE_HEADS = 4
HEAD_DIM = 128
FFE = 512
FFS = 1024
TOP = 6
EXPERTS = 16
TOK_DEV = 256
NDOC = 8
HALF = 128
STREAM_TOKENS = 2048
STREAMS = 4
MOST = 192
DOC_MOST = 1024
N_CTX = 8


def stream_starts(stream_key):
    first_key, second_key = jax.random.split(stream_key)
    longest = jax.random.randint(first_key, (), 0, NDOC)
    remaining = STREAM_TOKENS - DOC_MOST
    cut_points = jnp.sort(jax.random.choice(second_key, remaining - 1, (NDOC - 2,), replace=False) + 1).astype(jnp.int32)
    edges = jnp.concatenate([jnp.zeros((1,), jnp.int32), cut_points, jnp.full((1,), remaining, jnp.int32)])
    others = edges[1:] - edges[:-1]
    placing = jnp.arange(NDOC, dtype=jnp.int32)
    earlier = others[jnp.minimum(placing, NDOC - 2)]
    later_ones = others[jnp.maximum(placing - 1, 0)]
    lengths = jnp.where(placing < longest, earlier, jnp.where(placing == longest, DOC_MOST, later_ones))
    return (jnp.cumsum(lengths) - lengths).astype(jnp.int32)


def draw_doc_starts(key, part):
    stream_keys = jax.vmap(lambda stream_index: jax.random.fold_in(jax.random.fold_in(key, 7), stream_index))(jnp.arange(STREAMS))
    return jax.vmap(stream_starts)(stream_keys)


def steps_of(key, dims, shards, low, high):
    def one(position, blocks):
        steps = jax.random.uniform(jax.random.fold_in(jax.random.fold_in(key, 6), position), (blocks,), jnp.float32, low / len(shards), high / len(shards))
        return jnp.repeat(jnp.exp(steps), dims[position] // blocks).reshape((-1,) + (1,) * (len(dims) - position - 1))

    loudness = one(*shards[0])
    for cut in shards[1:]:
        loudness = loudness * one(*cut)
    return loudness


def assign_block(key, own, number, rows, amount, top, reach, slope):
    ranking = jax.random.permutation(key, amount)
    packed, usual = shares(amount, rows * top, reach, slope, True), shares(amount, rows * top, reach, slope, False)
    places = jnp.arange(amount)

    def named(sizes, offset_by):
        used = int((sizes > 0).sum())
        fixed = max(1, used // 4)
        passed = fixed + (places - fixed + offset_by * (used - fixed)) % max(1, amount - fixed)
        return jnp.zeros((amount,), jnp.int32).at[ranking[jnp.where(places < fixed, places, passed)]].set(jnp.asarray(sizes, jnp.int32))

    sizes = jnp.where(number % 4 == 0, named(packed, number // 4), named(usual, number - number // 4 - 1))
    mixed = jax.random.permutation(jax.random.fold_in(own, 3), amount)
    giver, sink = mixed[0:amount // 2 * 2:2], mixed[1:amount // 2 * 2:2]
    room = jnp.minimum(sizes[giver] - 1, reach - sizes[sink]) // 2
    room = jnp.where((giver == ranking[0]) | (sink == ranking[0]) | (sizes[sink] == 0), 0, jnp.maximum(room, 0))
    passed = jax.random.randint(jax.random.fold_in(own, 4), (amount // 2,), 0, 1 << 20) % (room + 1)
    sizes = sizes.at[giver].add(-passed).at[sink].add(passed)
    labels = jnp.searchsorted(jnp.cumsum(sizes), jnp.arange(rows * top), side="right").astype(jnp.int32)
    table = labels.reshape(top, rows).T
    table = table[jax.random.permutation(jax.random.fold_in(own, 1), rows)]
    offset_by = jax.random.randint(jax.random.fold_in(own, 2), (rows, 1), 0, top)
    return jnp.take_along_axis(table, (jnp.arange(top)[None, :] + offset_by) % top, axis=1)


def shares(count, total, limit, slope, full):
    loads = [(1 << 20) // math.isqrt(standing ** slope) + 1 for standing in range(1, count + 1)]
    largest = limit if full else min(limit, max(-(-total // count), total * loads[0] // sum(loads)))
    least = 1 if total - largest >= count - 1 else 0
    counts, rest = [largest] + [least] * (count - 1), total - largest - least * (count - 1)
    while rest > 0:
        candidates = [i for i in range(1, count) if counts[i] < largest] or [i for i in range(1, count) if counts[i] < limit]
        whole, left = sum([loads[i] for i in candidates]), rest
        for i in candidates:
            extra = min(limit - counts[i], max(1, left * loads[i] // whole), rest)
            counts[i] = counts[i] + extra
            rest = rest - extra
    return np.array(counts)


def centred(rng, shape, scale, reach, pieces=(), kind=jnp.bfloat16):
    drawn = jax.random.normal(rng, shape, jnp.float32) * scale
    if len(pieces) > 0:
        drawn = steps_of(rng, shape, pieces, -0.22, 0.18) * drawn
    return jnp.clip(drawn, min=-reach, max=reach).astype(kind)


def setup_inputs(seed: int = 0) -> dict:
    seeds = jax.random.split(jax.random.key(seed), 18)
    tokens = centred(seeds[0], (STREAMS, N_CTX, 2, HALF, MODEL_DIM), 1.0, 6.0, ((0, 4), (1, 8)))
    doc_starts = draw_doc_starts(jax.random.fold_in(seeds[17], 71), 0)
    routes_keys = jax.random.split(jax.random.fold_in(seeds[2], 1), STREAMS * N_CTX * 2 * HALF // TOK_DEV)
    routes_turns = jax.random.permutation(jax.random.fold_in(seeds[2], 3), STREAMS * N_CTX * 2 * HALF // TOK_DEV)
    routes = jax.vmap(lambda own, number: assign_block(jax.random.fold_in(seeds[2], 2), own, number, TOK_DEV, EXPERTS, TOP, MOST, 1))(routes_keys, routes_turns).reshape((STREAMS, N_CTX, 2, HALF, TOP))
    norm_gain_1 = jnp.clip(1.0 + 0.1 * jax.random.normal(seeds[3], (MODEL_DIM,), jnp.float32), 0.5, 1.5).astype(jnp.bfloat16)
    query_weight = centred(seeds[4], (MODEL_DIM, QUERY_HEADS * HEAD_DIM), (MODEL_DIM // 2) ** -0.5, 0.21875, ((0, 4),))
    key_matrix = centred(seeds[5], (MODEL_DIM, KEY_VALUE_HEADS * HEAD_DIM), (MODEL_DIM // 2) ** -0.5, 0.21875, ((0, 4),))
    value_matrix = centred(seeds[6], (MODEL_DIM, KEY_VALUE_HEADS * HEAD_DIM), MODEL_DIM ** -0.5, 0.15625, ((0, 4),))
    out_weight = centred(seeds[7], (QUERY_HEADS * HEAD_DIM, MODEL_DIM), 8 ** -0.5, 2.0, ((1, 4),))
    norm_gain_2 = jnp.clip(1.0 + 0.1 * jax.random.normal(seeds[8], (MODEL_DIM,), jnp.float32), 0.5, 1.5).astype(jnp.bfloat16)
    router_weight = centred(seeds[9], (MODEL_DIM, EXPERTS), (4 * MODEL_DIM) ** -0.5, 0.078125, ((0, 4),))
    shared_gate = centred(seeds[10], (MODEL_DIM, FFS), MODEL_DIM ** -0.5, 0.15625, ((0, 4),))
    shared_up = centred(seeds[11], (MODEL_DIM, FFS), MODEL_DIM ** -0.5, 0.15625, ((0, 4),))
    shared_down = centred(seeds[12], (FFS, MODEL_DIM), (FFS // 4) ** -0.5, 0.375, ((1, 4),))
    expert_gate = centred(seeds[13], (EXPERTS, MODEL_DIM, FFE), MODEL_DIM ** -0.5, 0.15625, ((0, 4),))
    expert_up = centred(seeds[14], (EXPERTS, MODEL_DIM, FFE), MODEL_DIM ** -0.5, 0.15625, ((0, 4),))
    expert_down = centred(seeds[15], (EXPERTS, FFE, MODEL_DIM), (FFE // 8) ** -0.5, 0.75, ((0, 4),))
    out_grad = centred(seeds[16], (STREAMS, N_CTX, 2, HALF, MODEL_DIM), 1.0, 6.0, ((0, 4), (1, 8)))
    return dict(tokens=tokens, doc_starts=doc_starts, routes=routes, norm_gain_1=norm_gain_1, query_weight=query_weight, key_matrix=key_matrix, value_matrix=value_matrix, out_weight=out_weight, norm_gain_2=norm_gain_2, router_weight=router_weight, shared_gate=shared_gate, shared_up=shared_up, shared_down=shared_down, expert_gate=expert_gate, expert_up=expert_up, expert_down=expert_down, out_grad=out_grad)


epsilon = 1e-05
large_negative = -1e+30
highest = lax.Precision.HIGHEST

@jax.custom_vjp
def low(v):
    return lax.optimization_barrier(v.astype(jnp.bfloat16)).astype(jnp.float32)

@jax.custom_vjp
def low_back(v):
    return v

def low_keep(v):
    return (low(v), None)

def low_pass(kept, grad):
    return (grad,)

def back_keep(v):
    return (v, None)

def back_low(kept, grad):
    return (low(grad),)
low.defvjp(low_keep, low_pass)
low_back.defvjp(back_keep, back_low)

def matmul(left, right):
    return jnp.dot(left, right, precision=highest)

def rms_scaled(values):
    return values * lax.rsqrt(lax.optimization_barrier(jnp.mean(values * values, axis=-1, keepdims=True)) + epsilon)

def silu_of(values):
    return values * jax.nn.sigmoid(values)

def softmax_last(values):
    shifted = jnp.exp(values - lax.optimization_barrier(jnp.max(values, axis=-1, keepdims=True)))
    return shifted / lax.optimization_barrier(jnp.sum(shifted, axis=-1, keepdims=True))

def to_stream(array):
    leading = array.shape[0]
    trailing = array.shape[4:]
    front_part = array[:, :, 0].reshape((leading, -1) + trailing)
    back_part = array[:, ::-1, 1].reshape((leading, -1) + trailing)
    return jnp.concatenate([front_part, back_part], axis=1)

def from_stream(array):
    leading = array.shape[0]
    trailing = array.shape[2:]
    middle = N_CTX * HALF
    front_part = array[:, :middle].reshape((leading, N_CTX, HALF) + trailing)
    back_part = array[:, middle:].reshape((leading, N_CTX, HALF) + trailing)[:, ::-1]
    return jnp.stack([front_part, back_part], axis=2)

def packed_attention(query_rows, key_projected, value_projected, segment):
    heads_ratio = QUERY_HEADS // KEY_VALUE_HEADS
    rows_per_block = math.gcd(512, STREAM_TOKENS)
    count_of_blocks = STREAM_TOKENS // rows_per_block
    heads_of_keys = key_projected.reshape(STREAM_TOKENS, KEY_VALUE_HEADS, HEAD_DIM)
    heads_of_values = value_projected.reshape(STREAM_TOKENS, KEY_VALUE_HEADS, HEAD_DIM)
    key_pos = jnp.arange(STREAM_TOKENS, dtype=jnp.int32)
    blocks_of_queries = query_rows.reshape(count_of_blocks, rows_per_block, KEY_VALUE_HEADS, heads_ratio, HEAD_DIM)
    pos_blocks = key_pos.reshape(count_of_blocks, rows_per_block)
    seg_blocks = segment.reshape(count_of_blocks, rows_per_block)

    def one_block(fragments):
        query_block, pos_block, seg_block = fragments
        scores = jnp.einsum('bgrd,kgd->grbk', query_block, heads_of_keys, precision=highest) * HEAD_DIM ** (-0.5)
        scores = low_back(scores)
        allowed = (key_pos[None, :] <= pos_block[:, None]) & (segment[None, :] == seg_block[:, None])
        scores = jnp.where(allowed[None, None], scores, large_negative)
        weights = low(softmax_last(scores))
        attended_rows = jnp.einsum('grbk,kgd->bgrd', weights, heads_of_values, precision=highest)
        return attended_rows.reshape(rows_per_block, QUERY_HEADS * HEAD_DIM)
    return lax.map(jax.checkpoint(one_block), (blocks_of_queries, pos_blocks, seg_blocks)).reshape(STREAM_TOKENS, QUERY_HEADS * HEAD_DIM)

def expert_tables(route_ids):
    flat_ids = route_ids.reshape(-1)
    assigned = flat_ids.shape[0]
    capacity = STREAMS * N_CTX * MOST
    one_hot = (flat_ids[:, None] == jnp.arange(EXPERTS, dtype=jnp.int32)[None, :]).astype(jnp.int32)
    rank_in_expert = lax.optimization_barrier(jnp.sum((jnp.cumsum(one_hot, axis=0) - 1) * one_hot, axis=1))
    slot_index = (flat_ids * capacity + rank_in_expert).astype(jnp.int32)
    slot_table = jnp.full((EXPERTS * capacity,), assigned, jnp.int32).at[slot_index].set(jnp.arange(assigned, dtype=jnp.int32))
    return (slot_index, slot_table)

def experts_forward(normed_two, gates, slot_index, slot_table, gate_experts, up_experts, down_experts):
    assigned = slot_index.shape[0]
    capacity = slot_table.shape[0] // EXPERTS
    filled = slot_table < assigned
    owners = jnp.minimum(slot_table, assigned - 1) // TOP
    inputs_slots = low_back(jnp.where(filled[:, None], normed_two[owners], jnp.float32(0.0)))
    per_expert = inputs_slots.reshape(EXPERTS, capacity, MODEL_DIM)

    def one_expert(fragments):
        expert_in, gate_matrix, up_matrix, down_matrix = fragments
        gate_pre = low_back(matmul(expert_in, gate_matrix))
        up_pre = low_back(matmul(expert_in, up_matrix))
        hidden = low(silu_of(gate_pre) * up_pre)
        return low_back(low(matmul(hidden, down_matrix)))
    produced = lax.map(jax.checkpoint(one_expert), (per_expert, gate_experts, up_experts, down_experts))
    picked = produced.reshape(EXPERTS * capacity, MODEL_DIM)[slot_index].reshape(-1, TOP, MODEL_DIM)
    return lax.optimization_barrier(jnp.sum(gates[:, :, None] * picked, axis=1))

def block_forward(stream_tokens, gain_one, query_weight, key_matrix, value_matrix, out_weight, gain_two, router_weight, gate_shared, up_shared, down_shared, gate_experts, up_experts, down_experts, document_segments, route_ids, slot_index, slot_table):
    count_of_streams = stream_tokens.shape[0]
    total_rows = count_of_streams * STREAM_TOKENS
    flat_tokens = stream_tokens.reshape(total_rows, MODEL_DIM)
    normed_one = low(rms_scaled(flat_tokens) * gain_one)
    query_projected = low_back(low(matmul(normed_one, query_weight)))
    key_projected = low_back(low(matmul(normed_one, key_matrix)))
    value_projected = low_back(low(matmul(normed_one, value_matrix)))
    attended_rows = lax.map(lambda fragments: packed_attention(*fragments), (query_projected.reshape(count_of_streams, STREAM_TOKENS, QUERY_HEADS * HEAD_DIM), key_projected.reshape(count_of_streams, STREAM_TOKENS, KEY_VALUE_HEADS * HEAD_DIM), value_projected.reshape(count_of_streams, STREAM_TOKENS, KEY_VALUE_HEADS * HEAD_DIM), document_segments))
    attended_rows = low_back(low(attended_rows.reshape(total_rows, QUERY_HEADS * HEAD_DIM)))
    residual = flat_tokens + low_back(matmul(attended_rows, out_weight))
    normed_two = low(rms_scaled(residual) * gain_two)
    logits = matmul(normed_two, router_weight)
    chosen = jnp.take_along_axis(logits, route_ids.reshape(total_rows, TOP), axis=1)
    gates = softmax_last(chosen)
    gate_pre = low_back(matmul(normed_two, gate_shared))
    up_pre = low_back(matmul(normed_two, up_shared))
    shared_out = matmul(low(silu_of(gate_pre) * up_pre), down_shared)
    expert_out = experts_forward(normed_two, gates, slot_index, slot_table, gate_experts, up_experts, down_experts)
    return (residual + shared_out + expert_out).reshape(stream_tokens.shape)

def reference(tokens, doc_starts, routes, norm_gain_1, query_weight, key_matrix, value_matrix, out_weight, norm_gain_2, router_weight, shared_gate, shared_up, shared_down, expert_gate, expert_up, expert_down, out_grad):
    stream_tokens = to_stream(tokens).astype(jnp.float32)
    cotangent = to_stream(out_grad).astype(jnp.float32)
    route_ids = to_stream(routes).reshape(-1).astype(jnp.int32)
    positions = jnp.arange(STREAM_TOKENS, dtype=jnp.int32)
    document_segments = lax.optimization_barrier(jnp.sum((doc_starts[:, None, 1:] <= positions[None, :, None]).astype(jnp.int32), axis=-1))
    slot_index, slot_table = expert_tables(route_ids)
    forward = partial(block_forward, document_segments=document_segments, route_ids=route_ids, slot_index=slot_index, slot_table=slot_table)
    output, pullback = jax.vjp(forward, stream_tokens, norm_gain_1.astype(jnp.float32), query_weight.astype(jnp.float32), key_matrix.astype(jnp.float32), value_matrix.astype(jnp.float32), out_weight.astype(jnp.float32), norm_gain_2.astype(jnp.float32), router_weight.astype(jnp.float32), shared_gate.astype(jnp.float32), shared_up.astype(jnp.float32), shared_down.astype(jnp.float32), expert_gate.astype(jnp.float32), expert_up.astype(jnp.float32), expert_down.astype(jnp.float32))
    grads = pullback(cotangent)
    return (from_stream(output).astype(jnp.bfloat16), from_stream(grads[0]).astype(jnp.bfloat16), grads[1], grads[2], grads[3], grads[4], grads[5], grads[6], grads[7], grads[8], grads[9], grads[10], grads[11], grads[12], grads[13])
```

```python
import jax
import jax.numpy as jnp
from jax import lax
from jax.experimental import pallas as pl
from jax.experimental.pallas import tpu as pltpu
from jax.sharding import PartitionSpec as P

QUERY_HEADS = 12
KEY_VALUE_HEADS = 4
HEAD_DIM = 128
TOP = 6
EXPERTS = 16

epsilon = 1e-05
large_negative = -1e30
highest = lax.Precision.HIGHEST
ORDER = (0, 2, 1, 3)


def dot32(left, right, dims=None):
    if dims is None:
        return jnp.dot(left, right, preferred_element_type=jnp.float32)
    return lax.dot_general(left, right, (dims, ((), ())), preferred_element_type=jnp.float32)


def flip(value, axis, bits):
    count = lax.axis_size(axis)
    return lax.ppermute(value, axis, [(i, i ^ bits) for i in range(count)])


def gather_rows(value):
    across = flip(value, "wa", 2)
    return jnp.concatenate([value, across, flip(value, "wa", 1), flip(across, "wa", 1)], axis=0)


def exchange(pieces, index):
    received = []
    for bits in ORDER:
        piece = lax.dynamic_index_in_dim(pieces, index ^ bits, 0, keepdims=False)
        received.append(piece if bits == 0 else flip(piece, "wa", bits))
    return jnp.concatenate(received, axis=0)


def reduce_rows(partial, kind):
    half = partial.shape[0] // 2
    near = partial[:half] + flip(partial[half:].astype(kind), "wa", 1).astype(jnp.float32)
    quarter = half // 2
    return near[:quarter] + flip(near[quarter:].astype(kind), "wa", 2).astype(jnp.float32)


def scatter_small(value):
    rows, width = value.shape
    contexts, members = lax.axis_size("ctx"), lax.axis_size("wa")
    each = width // (contexts * members)
    spread = value.reshape(rows, contexts, members, each).transpose(2, 0, 1, 3)
    spread = spread.reshape(members, rows, contexts * each)
    first = jnp.sum(lax.all_to_all(spread, "wa", 0, 0, tiled=True), axis=0)
    second = first.reshape(rows, contexts, each).transpose(1, 0, 2)
    return jnp.sum(lax.all_to_all(second, "ctx", 0, 0, tiled=True), axis=0)


def scatter_ctx(value):
    return lax.psum_scatter(value, "ctx", scatter_dimension=0, tiled=True)[0]


def silu_parts(values):
    sigmoid_of = jax.nn.sigmoid(values)
    return (values * sigmoid_of, sigmoid_of * (1.0 + values * (1.0 - sigmoid_of)))


def rms_back(grad_normed, normed, inverse, gain_values):
    scaled = grad_normed * gain_values
    return (
        jnp.sum(grad_normed * normed, axis=0),
        inverse * (scaled - normed * jnp.mean(scaled * normed, axis=-1, keepdims=True)),
    )


def attention_masks(starts_ref, block, half_rows, shape):
    rows = block * half_rows + lax.broadcasted_iota(jnp.int32, shape, 0) % half_rows
    first = jnp.zeros(shape, jnp.int32)
    for document in range(1, starts_ref.shape[0]):
        start = starts_ref[document]
        first = jnp.where(start <= rows, jnp.maximum(first, start), first)
    return first, rows


def block_bounds(starts_ref, block, half_rows):
    top = block * half_rows
    first = jnp.int32(0)
    for document in range(1, starts_ref.shape[0]):
        start = starts_ref[document]
        first = jnp.where(start <= top, jnp.maximum(first, start), first)
    return first // half_rows


def block_place(block, contexts):
    return jnp.where(block < contexts, 2 * block, 4 * contexts - 1 - 2 * block)


def attention_forward_kernel(starts_ref, own_ref, q_ref, k_ref, v_ref, o_ref, lse_ref, s_ref):
    blocks, half_rows, _ = k_ref.shape
    contexts = blocks // 2
    ratio = q_ref.shape[1] // HEAD_DIM
    rows = ratio * half_rows
    scale = HEAD_DIM ** (-0.5)
    for half in range(2):
        block = own_ref[0] if half == 0 else blocks - 1 - own_ref[0]
        queries = jnp.concatenate(
            [
                q_ref[half * half_rows : (half + 1) * half_rows, h * HEAD_DIM : (h + 1) * HEAD_DIM]
                for h in range(ratio)
            ],
            axis=0,
        )
        low = block_bounds(starts_ref, block, half_rows)
        first, position = attention_masks(starts_ref, block, half_rows, (rows, half_rows))
        column = lax.broadcasted_iota(jnp.int32, (rows, half_rows), 1)

        def score_step(step, running):
            keys = k_ref[block_place(step, contexts)]
            scores = dot32(queries, keys, ((1,), (1,))) * scale
            at = column + step * half_rows
            scores = jnp.where((at >= first) & (at <= position), scores, large_negative)
            s_ref[step - low] = scores
            return jnp.maximum(running, scores)

        running = lax.fori_loop(
            low, block + 1, score_step, jnp.full((rows, half_rows), large_negative, jnp.float32)
        )
        row_max = jnp.max(running, axis=1, keepdims=True)

        def sum_step(step, total):
            expo = jnp.exp(s_ref[step - low] - row_max)
            s_ref[step - low] = expo
            return total + expo

        total = lax.fori_loop(
            low, block + 1, sum_step, jnp.zeros((rows, half_rows), jnp.float32)
        )
        row_sum = jnp.sum(total, axis=1, keepdims=True)
        inverse = 1.0 / row_sum

        def value_step(step, accum):
            weights = (s_ref[step - low] * inverse).astype(jnp.bfloat16)
            return accum + dot32(weights, v_ref[block_place(step, contexts)])

        accum = lax.fori_loop(
            low, block + 1, value_step, jnp.zeros((rows, HEAD_DIM), jnp.float32)
        )
        log_sum = row_max + jnp.log(row_sum)
        lse_ref[0, half] = jnp.broadcast_to(log_sum, (rows, half_rows))
        for h in range(ratio):
            o_ref[half * half_rows : (half + 1) * half_rows, h * HEAD_DIM : (h + 1) * HEAD_DIM] = (
                accum[h * half_rows : (h + 1) * half_rows].astype(jnp.bfloat16)
            )


def attention_forward(starts, own, queries, keys, values):
    rows, width = queries.shape
    blocks, half_rows, _ = keys.shape
    ratio = QUERY_HEADS // KEY_VALUE_HEADS
    stacked = ratio * half_rows
    kv_spec = pl.BlockSpec((blocks, half_rows, HEAD_DIM), lambda g, *_: (0, 0, g))
    q_spec = pl.BlockSpec((rows, ratio * HEAD_DIM), lambda g, *_: (0, g))
    return pl.pallas_call(
        attention_forward_kernel,
        grid_spec=pltpu.PrefetchScalarGridSpec(
            num_scalar_prefetch=2,
            grid=(KEY_VALUE_HEADS,),
            in_specs=[q_spec, kv_spec, kv_spec],
            out_specs=[
                q_spec,
                pl.BlockSpec((1, 2, stacked, half_rows), lambda g, *_: (g, 0, 0, 0)),
            ],
            scratch_shapes=[pltpu.VMEM((blocks, stacked, half_rows), jnp.float32)],
        ),
        out_shape=(
            jax.ShapeDtypeStruct((rows, width), jnp.bfloat16),
            jax.ShapeDtypeStruct((KEY_VALUE_HEADS, 2, stacked, half_rows), jnp.float32),
        ),
        compiler_params=pltpu.CompilerParams(vmem_limit_bytes=48 << 20),
        cost_estimate=pl.CostEstimate(
            flops=2 * rows * width * blocks * half_rows * 2,
            bytes_accessed=4 * rows * width + 4 * blocks * half_rows * 512,
            transcendentals=rows * QUERY_HEADS * blocks * half_rows // 2,
        ),
        name="attention_forward",
    )(starts, own, queries, keys, values)


def attention_backward_kernel(
    starts_ref, own_ref, q_ref, do_ref, k_ref, v_ref, lse_ref, dq_ref, dk_ref, dv_ref, p_ref, dp_ref, dka_ref, dva_ref
):
    blocks, half_rows, _ = k_ref.shape
    contexts = blocks // 2
    ratio = q_ref.shape[1] // HEAD_DIM
    rows = ratio * half_rows
    scale = HEAD_DIM ** (-0.5)
    dka_ref[...] = jnp.zeros_like(dka_ref)
    dva_ref[...] = jnp.zeros_like(dva_ref)

    def stack(ref, half):
        return jnp.concatenate(
            [
                ref[half * half_rows : (half + 1) * half_rows, h * HEAD_DIM : (h + 1) * HEAD_DIM]
                for h in range(ratio)
            ],
            axis=0,
        )

    for half in range(2):
        block = own_ref[0] if half == 0 else blocks - 1 - own_ref[0]
        queries = stack(q_ref, half)
        grads = stack(do_ref, half)
        log_sum = lse_ref[0, half]
        low = block_bounds(starts_ref, block, half_rows)
        first, position = attention_masks(starts_ref, block, half_rows, (rows, half_rows))
        column = lax.broadcasted_iota(jnp.int32, (rows, half_rows), 1)

        def prob_step(step, running):
            place = block_place(step, contexts)
            scores = dot32(queries, k_ref[place], ((1,), (1,))) * scale
            at = column + step * half_rows
            probs = jnp.where(
                (at >= first) & (at <= position), jnp.exp(scores - log_sum), 0.0
            )
            prob_grads = dot32(grads, v_ref[place], ((1,), (1,)))
            p_ref[step - low] = probs
            dp_ref[step - low] = prob_grads
            return running + probs * prob_grads

        running = lax.fori_loop(
            low, block + 1, prob_step, jnp.zeros((rows, half_rows), jnp.float32)
        )
        delta = jnp.sum(running, axis=1, keepdims=True)

        def grad_step(step, query_grad):
            place = block_place(step, contexts)
            probs = p_ref[step - low]
            score_low = (probs * (dp_ref[step - low] - delta)).astype(jnp.bfloat16)
            dka_ref[place] += dot32(score_low, queries, ((0,), (0,)))
            dva_ref[place] += dot32(probs.astype(jnp.bfloat16), grads, ((0,), (0,)))
            return query_grad + dot32(score_low, k_ref[place])

        query_grad = lax.fori_loop(
            low, block + 1, grad_step, jnp.zeros((rows, HEAD_DIM), jnp.float32)
        )
        for h in range(ratio):
            dq_ref[half * half_rows : (half + 1) * half_rows, h * HEAD_DIM : (h + 1) * HEAD_DIM] = (
                query_grad[h * half_rows : (h + 1) * half_rows] * scale
            ).astype(jnp.bfloat16)
    dk_ref[...] = (dka_ref[...] * scale).astype(jnp.bfloat16)
    dv_ref[...] = dva_ref[...].astype(jnp.bfloat16)


def attention_backward(starts, own, queries, grads, keys, values, log_sums):
    rows, width = queries.shape
    blocks, half_rows, kv_width = keys.shape
    ratio = QUERY_HEADS // KEY_VALUE_HEADS
    stacked = ratio * half_rows
    kv_spec = pl.BlockSpec((blocks, half_rows, HEAD_DIM), lambda g, *_: (0, 0, g))
    q_spec = pl.BlockSpec((rows, ratio * HEAD_DIM), lambda g, *_: (0, g))
    return pl.pallas_call(
        attention_backward_kernel,
        grid_spec=pltpu.PrefetchScalarGridSpec(
            num_scalar_prefetch=2,
            grid=(KEY_VALUE_HEADS,),
            in_specs=[
                q_spec,
                q_spec,
                kv_spec,
                kv_spec,
                pl.BlockSpec((1, 2, stacked, half_rows), lambda g, *_: (g, 0, 0, 0)),
            ],
            out_specs=[q_spec, kv_spec, kv_spec],
            scratch_shapes=[
                pltpu.VMEM((blocks, stacked, half_rows), jnp.float32),
                pltpu.VMEM((blocks, stacked, half_rows), jnp.float32),
                pltpu.VMEM((blocks, half_rows, HEAD_DIM), jnp.float32),
                pltpu.VMEM((blocks, half_rows, HEAD_DIM), jnp.float32),
            ],
        ),
        out_shape=(
            jax.ShapeDtypeStruct((rows, width), jnp.bfloat16),
            jax.ShapeDtypeStruct((blocks, half_rows, kv_width), jnp.bfloat16),
            jax.ShapeDtypeStruct((blocks, half_rows, kv_width), jnp.bfloat16),
        ),
        compiler_params=pltpu.CompilerParams(vmem_limit_bytes=58 << 20),
        cost_estimate=pl.CostEstimate(
            flops=5 * rows * width * blocks * half_rows * 2,
            bytes_accessed=8 * rows * width + 8 * blocks * half_rows * kv_width,
            transcendentals=rows * QUERY_HEADS * blocks * half_rows // 2,
        ),
        name="attention_backward",
    )(starts, own, queries, grads, keys, values, log_sums)


def experts_kernel(
    base_ref, x_ref, dy_ref, xt_ref, dyt_ref, g_ref, gt_ref, wg_ref, wu_ref, wd_ref,
    out_ref, dx_ref, dg_ref, dw_ref, he_ref, da_ref, db_ref,
):
    local = pl.program_id(0)
    expert = base_ref[0] + local
    total_rows = x_ref.shape[0]
    step_rows = 256
    per = dw_ref.shape[3]
    tall = 384

    @pl.when(local == 0)
    def _():
        out_ref[...] = jnp.zeros_like(out_ref)
        dx_ref[...] = jnp.zeros_like(dx_ref)
        dg_ref[...] = jnp.zeros_like(dg_ref)

    @pl.loop(0, total_rows // step_rows)
    def _(step):
        rows = pl.ds(pl.multiple_of(step * step_rows, step_rows), step_rows)
        x = x_ref[rows, :]
        dy = dy_ref[rows, :].astype(jnp.float32)
        lane = lax.broadcasted_iota(jnp.int32, (step_rows, g_ref.shape[1]), 1)
        mine = lane == expert
        gate = jnp.sum(jnp.where(mine, g_ref[rows, :], 0.0), axis=1, keepdims=True)
        pre = dot32(x, wg_ref[0])
        up = dot32(x, wu_ref[0])
        silu, slope = silu_parts(pre)
        hidden = (silu * up).astype(jnp.bfloat16)
        he_ref[rows, :] = hidden
        made = dot32(hidden, wd_ref[0]).astype(jnp.bfloat16).astype(jnp.float32)
        out_ref[rows, :] += gate * made
        dg_ref[rows, :] += jnp.where(mine, jnp.sum(dy * made, axis=1, keepdims=True), 0.0)
        scaled = (gate * dy).astype(jnp.bfloat16)
        back = dot32(scaled, wd_ref[0], ((1,), (1,)))
        pre_low = (back * up * slope).astype(jnp.bfloat16)
        up_low = (back * silu).astype(jnp.bfloat16)
        da_ref[rows, :] = pre_low
        db_ref[rows, :] = up_low
        moved = dot32(pre_low, wg_ref[0], ((1,), (1,))) + dot32(up_low, wu_ref[0], ((1,), (1,)))
        dx_ref[rows, :] += moved.astype(jnp.bfloat16).astype(jnp.float32)

    gate_row = gt_ref[pl.ds(expert, 1), :]

    @pl.loop(0, xt_ref.shape[0] // tall)
    def _(step):
        rows = pl.ds(pl.multiple_of(step * tall, tall), tall)
        xt = xt_ref[rows, :]
        scaled = (dyt_ref[rows, :].astype(jnp.float32) * gate_row).astype(jnp.bfloat16)
        for number, term in enumerate(
            (dot32(xt, da_ref[...]), dot32(xt, db_ref[...]), dot32(scaled, he_ref[...]))
        ):
            low = term.astype(jnp.bfloat16)
            for part in range(tall // per):
                dw_ref[step * (tall // per) + part, 0, number] = low[part * per : (part + 1) * per]


def experts_call(base, x, dy, xt, dyt, gates, gates_t, gate_w, up_w, down_w, contexts):
    rows, width = x.shape
    count, _, hidden = gate_w.shape
    per = width // contexts
    once = pl.Buffered(1)
    whole = lambda shape: pl.BlockSpec(shape, lambda e, *_: (0,) * len(shape), pipeline_mode=once)
    weight = lambda shape: pl.BlockSpec((1,) + shape, lambda e, *_: (e, 0, 0))
    return pl.pallas_call(
        experts_kernel,
        grid_spec=pltpu.PrefetchScalarGridSpec(
            num_scalar_prefetch=1,
            grid=(count,),
            in_specs=[
                whole((rows, width)),
                whole((rows, width)),
                whole((width, rows)),
                whole((width, rows)),
                whole((rows, EXPERTS)),
                whole((EXPERTS, rows)),
                weight((width, hidden)),
                weight((width, hidden)),
                weight((hidden, width)),
            ],
            out_specs=[
                whole((rows, width)),
                whole((rows, width)),
                whole((rows, EXPERTS)),
                pl.BlockSpec((contexts, 1, 3, per, hidden), lambda e, *_: (0, e, 0, 0, 0)),
            ],
            scratch_shapes=[pltpu.VMEM((rows, hidden), jnp.bfloat16)] * 3,
        ),
        out_shape=(
            jax.ShapeDtypeStruct((rows, width), jnp.float32),
            jax.ShapeDtypeStruct((rows, width), jnp.float32),
            jax.ShapeDtypeStruct((rows, EXPERTS), jnp.float32),
            jax.ShapeDtypeStruct((contexts, count, 3, per, hidden), jnp.bfloat16),
        ),
        compiler_params=pltpu.CompilerParams(vmem_limit_bytes=60 << 20),
        cost_estimate=pl.CostEstimate(
            flops=18 * count * rows * width * hidden,
            bytes_accessed=16 * rows * width + 12 * count * width * hidden,
            transcendentals=count * rows * hidden,
        ),
        name="experts",
    )(base, x, dy, xt, dyt, gates, gates_t, gate_w, up_w, down_w)


def dense_gates(logits, routes):
    chosen = jnp.any(
        routes[:, :, None] == jnp.arange(EXPERTS, dtype=jnp.int32)[None, None, :], axis=1
    )
    top = jnp.max(jnp.where(chosen, logits, large_negative), axis=-1, keepdims=True)
    expo = jnp.where(chosen, jnp.exp(logits - top), 0.0)
    return expo / jnp.sum(expo, axis=-1, keepdims=True)


def shards(
    tokens, doc_starts, routes, norm_gain_1, query_weight, key_matrix, value_matrix, out_weight,
    norm_gain_2, router_weight, shared_gate, shared_up, shared_down, expert_gate, expert_up,
    expert_down, out_grad,
):
    contexts, members = lax.axis_size("ctx"), lax.axis_size("wa")
    context, member = lax.axis_index("ctx"), lax.axis_index("wa")
    half_rows, width = tokens.shape[3], tokens.shape[4]
    rows = 2 * half_rows
    share = width // members
    each = share // contexts
    kv_width = key_matrix.shape[1]
    blocks = 2 * contexts
    starts = doc_starts[0]
    own = context[None].astype(jnp.int32)
    inputs = tokens.reshape(rows, width).astype(jnp.float32)
    grad_low = out_grad.reshape(rows, width)
    grad_rows = grad_low.astype(jnp.float32)

    small = jnp.concatenate([norm_gain_1[:, None], norm_gain_2[:, None], router_weight], axis=1)
    small = lax.all_gather(small, "wa", axis=0, tiled=True)
    gain_one = small[:, 0].astype(jnp.float32)
    gain_two = small[:, 1].astype(jnp.float32)
    router_full = small[:, 2:]

    kv_full = lax.all_gather(
        jnp.concatenate([key_matrix, value_matrix], axis=1), "wa", axis=0, tiled=True
    )
    query_full = lax.all_gather(query_weight, "wa", axis=0, tiled=True)
    out_full = lax.all_gather(out_weight, "wa", axis=0, tiled=False)
    hidden_share = shared_gate.shape[1] // members
    pair = jnp.concatenate(
        [
            shared_gate.reshape(share, members, hidden_share),
            shared_up.reshape(share, members, hidden_share),
        ],
        axis=2,
    ).transpose(1, 0, 2)
    pair = lax.all_to_all(pair, "wa", 0, 0, tiled=True).reshape(width, 2 * hidden_share)
    down_share = lax.all_to_all(
        shared_down.reshape(members, hidden_share, share), "wa", 0, 0, tiled=True
    )
    down_share = down_share.transpose(1, 0, 2).reshape(hidden_share, width)

    inverse_one = lax.rsqrt(jnp.mean(inputs * inputs, axis=-1, keepdims=True) + epsilon)
    normed_one = inputs * inverse_one
    normed_low = (normed_one * gain_one).astype(jnp.bfloat16)
    kv_own = dot32(normed_low, kv_full).astype(jnp.bfloat16)
    kv_all = lax.all_gather(kv_own.reshape(2, half_rows, 2 * kv_width), "ctx", axis=0, tiled=True)
    keys, values = kv_all[:, :, :kv_width], kv_all[:, :, kv_width:]
    queries = dot32(normed_low, query_full).astype(jnp.bfloat16)
    by_share = lambda value: value.reshape(rows, contexts, members, each).transpose(2, 0, 1, 3).reshape(
        members, rows, share
    )
    normed_share = exchange(by_share(normed_low), member)
    routes_all = gather_rows(routes.reshape(rows, TOP))
    grad_all = gather_rows(grad_low)

    attended, log_sums = attention_forward(starts, own, queries, keys, values)
    attended_all = gather_rows(attended)
    mixed = jnp.concatenate([dot32(attended, out_full[m]) for m in range(members)], axis=1)
    residual = inputs + mixed
    inverse_two = lax.rsqrt(jnp.mean(residual * residual, axis=-1, keepdims=True) + epsilon)
    normed_two = residual * inverse_two
    second_low = (normed_two * gain_two).astype(jnp.bfloat16)

    second_all = gather_rows(second_low)
    gates_all = dense_gates(dot32(second_all, router_full), routes_all)
    out_part, dx_part, gate_back, expert_terms = experts_call(
        (member * expert_gate.shape[0])[None].astype(jnp.int32),
        second_all, grad_all, second_all.T, grad_all.T, gates_all, gates_all.T,
        expert_gate, expert_up, expert_down, contexts,
    )
    shared_pre = dot32(second_all, pair)
    shared_silu, shared_slope = silu_parts(shared_pre[:, :hidden_share])
    shared_up_pre = shared_pre[:, hidden_share:]
    shared_hidden = (shared_silu * shared_up_pre).astype(jnp.bfloat16)
    shared_back = dot32(grad_all, down_share, ((1,), (1,)))
    pair_low = jnp.concatenate(
        [
            (shared_back * shared_up_pre * shared_slope).astype(jnp.bfloat16),
            (shared_back * shared_silu).astype(jnp.bfloat16),
        ],
        axis=1,
    )
    out_part = out_part + dot32(shared_hidden, down_share)
    dx_part = dx_part + dot32(pair_low, pair, ((1,), (1,)))
    dx_own = reduce_rows(dx_part, jnp.bfloat16)
    out_own = reduce_rows(out_part, jnp.bfloat16)
    gate_back = reduce_rows(gate_back, jnp.float32)
    block_out = (residual + out_own).astype(jnp.bfloat16).reshape(tokens.shape)

    expert_sum = scatter_ctx(expert_terms).astype(jnp.float32)
    expert_gate_grad = expert_sum[:, 0]
    expert_up_grad = expert_sum[:, 1]
    expert_down_grad = expert_sum[:, 2].transpose(0, 2, 1)
    pair_term = dot32(second_all, pair_low, ((0,), (0,)))
    down_term = dot32(grad_all, shared_hidden, ((0,), (0,)))
    shared_term = jnp.concatenate([pair_term, down_term], axis=1).astype(jnp.bfloat16)
    shared_sum = scatter_ctx(shared_term.reshape(contexts, share // contexts * members, 3 * hidden_share))
    shared_sum = lax.all_to_all(
        shared_sum.reshape(members, each, 3 * hidden_share), "wa", 0, 0, tiled=True
    ).astype(jnp.float32)
    units = lambda part: (
        shared_sum[:, :, part * hidden_share : (part + 1) * hidden_share]
    )
    shared_gate_grad = units(0).transpose(1, 0, 2).reshape(each, members * hidden_share)
    shared_up_grad = units(1).transpose(1, 0, 2).reshape(each, members * hidden_share)
    shared_down_grad = units(2).transpose(0, 2, 1).reshape(members * hidden_share, each)

    gates = gates_all[:rows]
    logit_grad = gates * (gate_back - jnp.sum(gates * gate_back, axis=-1, keepdims=True))
    router_term = lax.dot_general(
        logit_grad, second_low.astype(jnp.float32), (((0,), (0,)), ((), ())), precision=highest
    )
    second_grad = dx_own + jnp.dot(logit_grad, router_full.astype(jnp.float32).T, precision=highest)
    gain_two_term, residual_back = rms_back(second_grad, normed_two, inverse_two, gain_two)
    residual_grad = grad_rows + residual_back
    mix_low = residual_grad.astype(jnp.bfloat16)

    mix_share = exchange(by_share(mix_low), member)
    attended_grad = sum(
        dot32(mix_low[:, m * share : (m + 1) * share], out_full[m], ((1,), (1,)))
        for m in range(members)
    ).astype(jnp.bfloat16)
    query_low, key_parts, value_parts = attention_backward(
        starts, own, queries, attended_grad, keys, values, log_sums
    )
    kv_parts = jnp.concatenate([key_parts, value_parts], axis=2)
    kv_low = scatter_ctx(kv_parts.reshape(contexts, rows, 2 * kv_width))
    out_term = dot32(mix_share, attended_all, ((0,), (0,))).astype(jnp.bfloat16)
    query_all = gather_rows(query_low)
    query_term = dot32(normed_share, query_all, ((0,), (0,))).astype(jnp.bfloat16)
    early = jnp.concatenate([out_term, query_term], axis=1).reshape(contexts, each, 2 * width)
    early = scatter_ctx(early).astype(jnp.float32)
    out_weight_grad = early[:, :width].T
    query_weight_grad = early[:, width:]
    kv_low_all = gather_rows(kv_low)
    kv_term = dot32(normed_share, kv_low_all, ((0,), (0,))).astype(jnp.bfloat16)
    late = scatter_ctx(kv_term.reshape(contexts, each, 2 * kv_width)).astype(jnp.float32)
    key_weight_grad = late[:, :kv_width]
    value_weight_grad = late[:, kv_width:]
    first_grad = dot32(query_low, query_full, ((1,), (1,))) + dot32(kv_low, kv_full, ((1,), (1,)))
    gain_one_term, input_back = rms_back(first_grad, normed_one, inverse_one, gain_one)
    tokens_grad = (residual_grad + input_back).astype(jnp.bfloat16).reshape(tokens.shape)

    tiny = scatter_small(jnp.concatenate([router_term, gain_two_term[None], gain_one_term[None]], axis=0))
    return (
        block_out,
        tokens_grad,
        tiny[EXPERTS + 1],
        query_weight_grad,
        key_weight_grad,
        value_weight_grad,
        out_weight_grad,
        tiny[EXPERTS],
        tiny[:EXPERTS].T,
        shared_gate_grad,
        shared_up_grad,
        shared_down_grad,
        expert_gate_grad,
        expert_up_grad,
        expert_down_grad,
    )


def solution(mesh):
    return jax.shard_map(
        shards,
        mesh=mesh,
        in_specs=(
            P("wa", "ctx", None, None, None),
            P("wa", None),
            P("wa", "ctx", None, None, None),
            P("wa"),
            P("wa", None),
            P("wa", None),
            P("wa", None),
            P(None, "wa"),
            P("wa"),
            P("wa", None),
            P("wa", None),
            P("wa", None),
            P(None, "wa"),
            P("wa", None, None),
            P("wa", None, None),
            P("wa", None, None),
            P("wa", "ctx", None, None, None),
        ),
        out_specs=(
            P("wa", "ctx", None, None, None),
            P("wa", "ctx", None, None, None),
            P(("ctx", "wa")),
            P(("ctx", "wa"), None),
            P(("ctx", "wa"), None),
            P(("ctx", "wa"), None),
            P(None, ("ctx", "wa")),
            P(("ctx", "wa")),
            P(("ctx", "wa"), None),
            P(("ctx", "wa"), None),
            P(("ctx", "wa"), None),
            P(None, ("ctx", "wa")),
            P("wa", "ctx", None),
            P("wa", "ctx", None),
            P("wa", None, "ctx"),
        ),
        check_vma=False,
    )
```

```python
import jax
import jax.numpy as jnp
from jax import lax
from jax.experimental import pallas as pl
from jax.experimental.pallas import tpu as pltpu
from jax.sharding import PartitionSpec as P

QUERY_HEADS = 12
KEY_VALUE_HEADS = 4
HEAD_DIM = 128
TOP = 6
EXPERTS = 16

epsilon = 1e-05
large_negative = -1e30
highest = lax.Precision.HIGHEST
ORDER = (0, 2, 1, 3)


def dot32(left, right, dims=None):
    if dims is None:
        return jnp.dot(left, right, preferred_element_type=jnp.float32)
    return lax.dot_general(left, right, (dims, ((), ())), preferred_element_type=jnp.float32)


def flip(value, axis, bits):
    count = lax.axis_size(axis)
    return lax.ppermute(value, axis, [(i, i ^ bits) for i in range(count)])


def shift(value, steps):
    count = lax.axis_size("ctx")
    return lax.ppermute(value, "ctx", [(i, (i + 2 * steps) % count) for i in range(count)])


def after(value, *earlier):
    return lax.optimization_barrier((value,) + earlier)[0]


def gather_pieces(value):
    across = flip(value, "wa", 2)
    return [value, across, flip(value, "wa", 1), flip(across, "wa", 1)]


def ordered(pieces, index):
    chip, core = index // 2, index % 2
    near = [jnp.where(core == i, pieces[0], pieces[2]) for i in range(2)]
    far = [jnp.where(core == i, pieces[1], pieces[3]) for i in range(2)]
    return jnp.concatenate(
        [jnp.where(chip == i // 2, near[i % 2], far[i % 2]) for i in range(4)], axis=0
    )


def exchange(pieces, index):
    received = []
    for bits in ORDER:
        piece = lax.dynamic_index_in_dim(pieces, index ^ bits, 0, keepdims=False)
        received.append(piece if bits == 0 else flip(piece, "wa", bits))
    return jnp.concatenate(received, axis=0)


def reduce_rows(keep, send, kind):
    near = keep + flip(send, "wa", 1).astype(jnp.float32)
    quarter = keep.shape[0] // 2
    return near[:quarter] + flip(near[quarter:].astype(kind), "wa", 2).astype(jnp.float32)


def scatter_small(value):
    rows, width = value.shape
    contexts, members = lax.axis_size("ctx"), lax.axis_size("wa")
    each = width // (contexts * members)
    spread = value.reshape(rows, contexts, members, each).transpose(2, 0, 1, 3)
    spread = spread.reshape(members, rows, contexts * each)
    first = jnp.sum(lax.all_to_all(spread, "wa", 0, 0, tiled=True), axis=0)
    second = first.reshape(rows, contexts, each).transpose(1, 0, 2)
    return jnp.sum(lax.all_to_all(second, "ctx", 0, 0, tiled=True), axis=0)


def sides():
    count = lax.axis_size("ctx")
    return [list(range(side, count, 2)) for side in range(2)]


def scatter_ctx(value, index):
    lines = value.shape[0] // 2
    line, side = index // 2, index % 2
    pairs = value.reshape((lines, 2) + value.shape[1:])
    keep = lax.dynamic_index_in_dim(pairs, side, 1, keepdims=False)
    send = lax.dynamic_index_in_dim(pairs, 1 - side, 1, keepdims=False)
    near = keep.astype(jnp.float32) + flip(send, "ctx", 1).astype(jnp.float32)
    low = near.astype(jnp.bfloat16)
    total = lax.dynamic_index_in_dim(near, line, 0, keepdims=False)
    for steps in range(1, lines):
        piece = lax.dynamic_index_in_dim(low, (line + lines - steps) % lines, 0, keepdims=False)
        total = total + shift(piece, -steps).astype(jnp.float32)
    return total


def scatter_lines(value):
    return lax.psum_scatter(
        value, "ctx", scatter_dimension=0, axis_index_groups=sides(), tiled=True
    )[0]


def silu_parts(values):
    sigmoid_of = jax.nn.sigmoid(values)
    return (values * sigmoid_of, sigmoid_of * (1.0 + values * (1.0 - sigmoid_of)))


def rms_back(grad_normed, normed, inverse, gain_values):
    scaled = grad_normed * gain_values
    return (
        jnp.sum(grad_normed * normed, axis=0),
        inverse * (scaled - normed * jnp.mean(scaled * normed, axis=-1, keepdims=True)),
    )


def attention_masks(starts_ref, block, half_rows, shape):
    rows = block * half_rows + lax.broadcasted_iota(jnp.int32, shape, 0) % half_rows
    first = jnp.zeros(shape, jnp.int32)
    for document in range(1, starts_ref.shape[0]):
        start = starts_ref[document]
        first = jnp.where(start <= rows, jnp.maximum(first, start), first)
    return first, rows


def block_bounds(starts_ref, block, half_rows):
    top = block * half_rows
    first = jnp.int32(0)
    for document in range(1, starts_ref.shape[0]):
        start = starts_ref[document]
        first = jnp.where(start <= top, jnp.maximum(first, start), first)
    return first // half_rows


def block_place(block, own, contexts):
    late = (block >= contexts).astype(jnp.int32)
    device = jnp.where(block < contexts, block, 2 * contexts - 1 - block)
    lines = contexts // 2
    behind = own // 2 - device // 2
    behind = jnp.where(behind < 0, behind + lines, behind)
    return (((own + device) % 2) * lines + behind) * 2 + late


def attention_forward_kernel(starts_ref, own_ref, q_ref, kv_ref, o_ref, lse_ref, s_ref):
    blocks, half_rows, _ = kv_ref.shape
    contexts = blocks // 2
    ratio = q_ref.shape[1] // HEAD_DIM
    rows = ratio * half_rows
    scale = HEAD_DIM ** (-0.5)
    for half in range(2):
        block = own_ref[0] if half == 0 else blocks - 1 - own_ref[0]
        queries = jnp.concatenate(
            [
                q_ref[half * half_rows : (half + 1) * half_rows, h * HEAD_DIM : (h + 1) * HEAD_DIM]
                for h in range(ratio)
            ],
            axis=0,
        )
        low = block_bounds(starts_ref, block, half_rows)
        first, position = attention_masks(starts_ref, block, half_rows, (rows, half_rows))
        column = lax.broadcasted_iota(jnp.int32, (rows, half_rows), 1)

        def score_step(step, running):
            keys = kv_ref[block_place(step, own_ref[0], contexts), :, :HEAD_DIM]
            scores = dot32(queries, keys, ((1,), (1,))) * scale
            at = column + step * half_rows
            scores = jnp.where((at >= first) & (at <= position), scores, large_negative)
            s_ref[step - low] = scores
            return jnp.maximum(running, scores)

        running = lax.fori_loop(
            low, block + 1, score_step, jnp.full((rows, half_rows), large_negative, jnp.float32)
        )
        row_max = jnp.max(running, axis=1, keepdims=True)

        def sum_step(step, total):
            expo = jnp.exp(s_ref[step - low] - row_max)
            s_ref[step - low] = expo
            return total + expo

        total = lax.fori_loop(
            low, block + 1, sum_step, jnp.zeros((rows, half_rows), jnp.float32)
        )
        row_sum = jnp.sum(total, axis=1, keepdims=True)
        inverse = 1.0 / row_sum

        def value_step(step, accum):
            weights = (s_ref[step - low] * inverse).astype(jnp.bfloat16)
            return accum + dot32(weights, kv_ref[block_place(step, own_ref[0], contexts), :, HEAD_DIM:])

        accum = lax.fori_loop(
            low, block + 1, value_step, jnp.zeros((rows, HEAD_DIM), jnp.float32)
        )
        log_sum = row_max + jnp.log(row_sum)
        lse_ref[0, half] = jnp.broadcast_to(log_sum, (rows, half_rows))
        for h in range(ratio):
            o_ref[half * half_rows : (half + 1) * half_rows, h * HEAD_DIM : (h + 1) * HEAD_DIM] = (
                accum[h * half_rows : (h + 1) * half_rows].astype(jnp.bfloat16)
            )


def attention_forward(starts, own, queries, kv):
    rows, width = queries.shape
    blocks, half_rows, _ = kv.shape
    ratio = QUERY_HEADS // KEY_VALUE_HEADS
    stacked = ratio * half_rows
    kv_spec = pl.BlockSpec((blocks, half_rows, 2 * HEAD_DIM), lambda g, *_: (0, 0, g))
    q_spec = pl.BlockSpec((rows, ratio * HEAD_DIM), lambda g, *_: (0, g))
    return pl.pallas_call(
        attention_forward_kernel,
        grid_spec=pltpu.PrefetchScalarGridSpec(
            num_scalar_prefetch=2,
            grid=(KEY_VALUE_HEADS,),
            in_specs=[q_spec, kv_spec],
            out_specs=[
                q_spec,
                pl.BlockSpec((1, 2, stacked, half_rows), lambda g, *_: (g, 0, 0, 0)),
            ],
            scratch_shapes=[pltpu.VMEM((blocks, stacked, half_rows), jnp.float32)],
        ),
        out_shape=(
            jax.ShapeDtypeStruct((rows, width), jnp.bfloat16),
            jax.ShapeDtypeStruct((KEY_VALUE_HEADS, 2, stacked, half_rows), jnp.float32),
        ),
        compiler_params=pltpu.CompilerParams(vmem_limit_bytes=48 << 20),
        cost_estimate=pl.CostEstimate(
            flops=2 * rows * width * blocks * half_rows * 2,
            bytes_accessed=4 * rows * width + 4 * blocks * half_rows * 512,
            transcendentals=rows * QUERY_HEADS * blocks * half_rows // 2,
        ),
        name="attention_forward",
    )(starts, own, queries, kv)


def attention_backward_kernel(
    starts_ref, own_ref, q_ref, do_ref, kv_ref, lse_ref, dq_ref, keep_ref, send_ref, p_ref, dp_ref, dka_ref, dva_ref
):
    blocks, half_rows, _ = kv_ref.shape
    contexts = blocks // 2
    ratio = q_ref.shape[1] // HEAD_DIM
    rows = ratio * half_rows
    scale = HEAD_DIM ** (-0.5)
    dka_ref[...] = jnp.zeros_like(dka_ref)
    dva_ref[...] = jnp.zeros_like(dva_ref)

    def stack(ref, half):
        return jnp.concatenate(
            [
                ref[half * half_rows : (half + 1) * half_rows, h * HEAD_DIM : (h + 1) * HEAD_DIM]
                for h in range(ratio)
            ],
            axis=0,
        )

    for half in range(2):
        block = own_ref[0] if half == 0 else blocks - 1 - own_ref[0]
        queries = stack(q_ref, half)
        grads = stack(do_ref, half)
        log_sum = lse_ref[0, half]
        low = block_bounds(starts_ref, block, half_rows)
        first, position = attention_masks(starts_ref, block, half_rows, (rows, half_rows))
        column = lax.broadcasted_iota(jnp.int32, (rows, half_rows), 1)

        def prob_step(step, running):
            place = block_place(step, own_ref[0], contexts)
            scores = dot32(queries, kv_ref[place, :, :HEAD_DIM], ((1,), (1,))) * scale
            at = column + step * half_rows
            probs = jnp.where(
                (at >= first) & (at <= position), jnp.exp(scores - log_sum), 0.0
            )
            prob_grads = dot32(grads, kv_ref[place, :, HEAD_DIM:], ((1,), (1,)))
            p_ref[step - low] = probs
            dp_ref[step - low] = prob_grads
            return running + probs * prob_grads

        running = lax.fori_loop(
            low, block + 1, prob_step, jnp.zeros((rows, half_rows), jnp.float32)
        )
        delta = jnp.sum(running, axis=1, keepdims=True)

        def grad_step(step, query_grad):
            place = block_place(step, own_ref[0], contexts)
            probs = p_ref[step - low]
            score_low = (probs * (dp_ref[step - low] - delta)).astype(jnp.bfloat16)
            dka_ref[place] += dot32(score_low, queries, ((0,), (0,)))
            dva_ref[place] += dot32(probs.astype(jnp.bfloat16), grads, ((0,), (0,)))
            return query_grad + dot32(score_low, kv_ref[place, :, :HEAD_DIM])

        query_grad = lax.fori_loop(
            low, block + 1, grad_step, jnp.zeros((rows, HEAD_DIM), jnp.float32)
        )
        for h in range(ratio):
            dq_ref[half * half_rows : (half + 1) * half_rows, h * HEAD_DIM : (h + 1) * HEAD_DIM] = (
                query_grad[h * half_rows : (h + 1) * half_rows] * scale
            ).astype(jnp.bfloat16)
    for out_ref, places in ((keep_ref, slice(0, contexts)), (send_ref, slice(contexts, blocks))):
        out_ref[:, :, :HEAD_DIM] = (dka_ref[places] * scale).astype(jnp.bfloat16)
        out_ref[:, :, HEAD_DIM:] = dva_ref[places].astype(jnp.bfloat16)


def attention_backward(starts, own, queries, grads, kv, log_sums):
    rows, width = queries.shape
    blocks, half_rows, kv_width = kv.shape
    ratio = QUERY_HEADS // KEY_VALUE_HEADS
    stacked = ratio * half_rows
    kv_spec = pl.BlockSpec((blocks, half_rows, 2 * HEAD_DIM), lambda g, *_: (0, 0, g))
    part_spec = pl.BlockSpec((blocks // 2, half_rows, 2 * HEAD_DIM), lambda g, *_: (0, 0, g))
    q_spec = pl.BlockSpec((rows, ratio * HEAD_DIM), lambda g, *_: (0, g))
    return pl.pallas_call(
        attention_backward_kernel,
        grid_spec=pltpu.PrefetchScalarGridSpec(
            num_scalar_prefetch=2,
            grid=(KEY_VALUE_HEADS,),
            in_specs=[
                q_spec,
                q_spec,
                kv_spec,
                pl.BlockSpec((1, 2, stacked, half_rows), lambda g, *_: (g, 0, 0, 0)),
            ],
            out_specs=[q_spec, part_spec, part_spec],
            scratch_shapes=[
                pltpu.VMEM((blocks, stacked, half_rows), jnp.float32),
                pltpu.VMEM((blocks, stacked, half_rows), jnp.float32),
                pltpu.VMEM((blocks, half_rows, HEAD_DIM), jnp.float32),
                pltpu.VMEM((blocks, half_rows, HEAD_DIM), jnp.float32),
            ],
        ),
        out_shape=(
            jax.ShapeDtypeStruct((rows, width), jnp.bfloat16),
            jax.ShapeDtypeStruct((blocks // 2, half_rows, kv_width), jnp.bfloat16),
            jax.ShapeDtypeStruct((blocks // 2, half_rows, kv_width), jnp.bfloat16),
        ),
        compiler_params=pltpu.CompilerParams(vmem_limit_bytes=58 << 20),
        cost_estimate=pl.CostEstimate(
            flops=5 * rows * width * blocks * half_rows * 2,
            bytes_accessed=8 * rows * width + 8 * blocks * half_rows * kv_width,
            transcendentals=rows * QUERY_HEADS * blocks * half_rows // 2,
        ),
        name="attention_backward",
    )(starts, own, queries, grads, kv, log_sums)


def experts_kernel(
    at_ref, x0, x1, x2, x3, dy0, dy1, dy2, dy3, g_ref, wg_ref, wu_ref, wd_ref, shared_ref,
    out_ref, dx_ref, out_low_ref, dx_low_ref, dg_ref, term_ref, pair_term_ref,
    x_ref, dy_ref, he_ref, da_ref, db_ref, tail_ref, sem,
):
    local = pl.program_id(0)
    last = pl.num_programs(0) - 1
    expert = at_ref[0] + local
    side = at_ref[1]
    total_rows, width = x_ref.shape
    step_rows = 256
    per = term_ref.shape[4]
    tall = 384
    shared = shared_ref.shape[1] // 3

    @pl.when(local == 0)
    def _():
        copies = []
        for number, (whole, parts) in enumerate(((x_ref, (x0, x1, x2, x3)), (dy_ref, (dy0, dy1, dy2, dy3)))):
            size = total_rows // 4
            for part, source in enumerate(parts):
                copies.append(
                    pltpu.make_async_copy(
                        source, whole.at[pl.ds(part * size, size), :], sem.at[number * 4 + part]
                    )
                )
        for copy in copies:
            copy.start()
        out_ref[...] = jnp.zeros_like(out_ref)
        dx_ref[...] = jnp.zeros_like(dx_ref)
        tail_ref[...] = jnp.zeros_like(tail_ref)
        dg_ref[...] = jnp.zeros_like(dg_ref)
        for copy in copies:
            copy.wait()

    half = total_rows // 2

    def add(number, rows, value):
        if rows.start < half:
            (out_ref, dx_ref)[number][rows, :] += value
        else:
            tail_ref[number, slice(rows.start - half, rows.stop - half), :] += value

    def store(low, begin, target, number):
        for part in range(low.shape[0] // per):
            device = begin // per + part
            target[(side + device) % 2, device // 2, number] = low[part * per : (part + 1) * per]

    for begin in range(0, total_rows, step_rows):
        rows = slice(begin, begin + step_rows)
        x = x_ref[rows, :]
        lane = lax.broadcasted_iota(jnp.int32, (step_rows, g_ref.shape[1]), 1)
        mine = lane == expert
        gate = jnp.sum(jnp.where(mine, g_ref[rows, :], 0.0), axis=1, keepdims=True)
        pre = dot32(x, wg_ref[0])
        up = dot32(x, wu_ref[0])
        back = dot32(dy_ref[rows, :], wd_ref[0], ((1,), (1,)))
        silu, slope = silu_parts(pre)
        hidden = (silu * up).astype(jnp.bfloat16).astype(jnp.float32)
        dg_ref[rows, :] += jnp.where(mine, jnp.sum(hidden * back, axis=1, keepdims=True), 0.0)
        hidden_low = (gate * hidden).astype(jnp.bfloat16)
        he_ref[rows, :] = hidden_low
        add(0, rows, dot32(hidden_low, wd_ref[0]))
        back = gate * back
        pre_low = (back * up * slope).astype(jnp.bfloat16)
        up_low = (back * silu).astype(jnp.bfloat16)
        da_ref[rows, :] = pre_low
        db_ref[rows, :] = up_low
        add(1, rows, dot32(pre_low, wg_ref[0], ((1,), (1,))) + dot32(up_low, wu_ref[0], ((1,), (1,))))

    for begin in range(0, width, tall):
        columns = slice(begin, begin + tall)
        for number, (left, right) in enumerate(((x_ref, da_ref), (x_ref, db_ref), (dy_ref, he_ref))):
            low = dot32(left[:, columns], right[...], ((0,), (0,))).astype(jnp.bfloat16)
            store(low, begin, term_ref.at[0], number)

    @pl.when(local == last)
    def _():
        for begin in range(0, total_rows, step_rows):
            rows = slice(begin, begin + step_rows)
            x = x_ref[rows, :]
            both = dot32(x, shared_ref[:, : 2 * shared])
            pre, up = both[:, :shared], both[:, shared:]
            silu, slope = silu_parts(pre)
            hidden = (silu * up).astype(jnp.bfloat16)
            he_ref[rows, :shared] = hidden
            add(0, rows, dot32(hidden, shared_ref[:, 2 * shared :], ((1,), (1,))))
            back = dot32(dy_ref[rows, :], shared_ref[:, 2 * shared :])
            da_ref[rows, :shared] = (back * up * slope).astype(jnp.bfloat16)
            da_ref[rows, shared:] = (back * silu).astype(jnp.bfloat16)
            add(1, rows, dot32(da_ref[rows, :], shared_ref[:, : 2 * shared], ((1,), (1,))))
        out_low_ref[...] = tail_ref[0].astype(jnp.bfloat16)
        dx_low_ref[...] = tail_ref[1].astype(jnp.bfloat16)
        for begin in range(0, width, tall):
            columns = slice(begin, begin + tall)
            low = dot32(x_ref[:, columns], da_ref[...], ((0,), (0,))).astype(jnp.bfloat16)
            store(low[:, :shared], begin, pair_term_ref, 0)
            store(low[:, shared:], begin, pair_term_ref, 1)
            low = dot32(dy_ref[:, columns], he_ref[:, :shared], ((0,), (0,))).astype(jnp.bfloat16)
            store(low, begin, pair_term_ref, 2)


def experts_call(at, x, dy, gates, gate_w, up_w, down_w, shared_w, contexts):
    rows, width = 4 * x[0].shape[0], x[0].shape[1]
    count, _, hidden = gate_w.shape
    shared = shared_w.shape[1] // 3
    per = width // contexts
    lines = contexts // 2
    once = pl.Buffered(1)
    whole = lambda shape: pl.BlockSpec(shape, lambda e, *_: (0,) * len(shape), pipeline_mode=once)
    weight = lambda shape: pl.BlockSpec((1,) + shape, lambda e, *_: (e, 0, 0))
    term = pl.BlockSpec((1, 2, lines, 3, per, hidden), lambda e, *_: (e, 0, 0, 0, 0, 0))
    term_shape = jax.ShapeDtypeStruct((count, 2, lines, 3, per, hidden), jnp.bfloat16)
    pair_shape = jax.ShapeDtypeStruct((2, lines, 3, per, shared), jnp.bfloat16)
    return pl.pallas_call(
        experts_kernel,
        grid_spec=pltpu.PrefetchScalarGridSpec(
            num_scalar_prefetch=1,
            grid=(count,),
            in_specs=[pl.BlockSpec(memory_space=pl.ANY)] * 8
            + [
                whole((rows, EXPERTS)),
                weight((width, hidden)),
                weight((width, hidden)),
                weight((hidden, width)),
                whole(shared_w.shape),
            ],
            out_specs=[
                whole((rows // 2, width)),
                whole((rows // 2, width)),
                whole((rows // 2, width)),
                whole((rows // 2, width)),
                whole((rows, EXPERTS)),
                term,
                whole(pair_shape.shape),
            ],
            scratch_shapes=[pltpu.VMEM((rows, width), jnp.bfloat16)] * 2
            + [pltpu.VMEM((rows, hidden), jnp.bfloat16)] * 3
            + [pltpu.VMEM((2, rows // 2, width), jnp.float32), pltpu.SemaphoreType.DMA((8,))],
        ),
        out_shape=(
            jax.ShapeDtypeStruct((rows // 2, width), jnp.float32),
            jax.ShapeDtypeStruct((rows // 2, width), jnp.float32),
            jax.ShapeDtypeStruct((rows // 2, width), jnp.bfloat16),
            jax.ShapeDtypeStruct((rows // 2, width), jnp.bfloat16),
            jax.ShapeDtypeStruct((rows, EXPERTS), jnp.float32),
            term_shape,
            pair_shape,
        ),
        compiler_params=pltpu.CompilerParams(vmem_limit_bytes=60 << 20),
        cost_estimate=pl.CostEstimate(
            flops=18 * count * rows * width * hidden + 18 * rows * width * shared,
            bytes_accessed=16 * rows * width + 12 * count * width * hidden,
            transcendentals=count * rows * hidden,
        ),
        name="experts",
    )(at, *x, *dy, gates, gate_w, up_w, down_w, shared_w)


def dense_gates(logits, routes):
    chosen = jnp.any(
        routes[:, :, None] == jnp.arange(EXPERTS, dtype=jnp.int32)[None, None, :], axis=1
    )
    top = jnp.max(jnp.where(chosen, logits, large_negative), axis=-1, keepdims=True)
    expo = jnp.where(chosen, jnp.exp(logits - top), 0.0)
    return expo / jnp.sum(expo, axis=-1, keepdims=True)


def shards(
    tokens, doc_starts, routes, norm_gain_1, query_weight, key_matrix, value_matrix, out_weight,
    norm_gain_2, router_weight, shared_gate, shared_up, shared_down, expert_gate, expert_up,
    expert_down, out_grad,
):
    contexts, members = lax.axis_size("ctx"), lax.axis_size("wa")
    context, member = lax.axis_index("ctx"), lax.axis_index("wa")
    half_rows, width = tokens.shape[3], tokens.shape[4]
    rows = 2 * half_rows
    share = width // members
    each = share // contexts
    lines = contexts // 2
    kv_width = 2 * key_matrix.shape[1]
    starts = doc_starts[0]
    own = context[None].astype(jnp.int32)
    inputs = tokens.reshape(rows, width).astype(jnp.float32)
    grad_low = out_grad.reshape(rows, width)
    grad_rows = grad_low.astype(jnp.float32)

    beside = lambda k, v: jnp.stack(
        [k.reshape(-1, KEY_VALUE_HEADS, HEAD_DIM), v.reshape(-1, KEY_VALUE_HEADS, HEAD_DIM)], axis=2
    ).reshape(-1, kv_width)
    apart = lambda kv: jnp.moveaxis(
        kv.reshape(-1, KEY_VALUE_HEADS, 2, HEAD_DIM), 2, 0
    ).reshape(2, -1, kv_width // 2)
    small = jnp.concatenate([router_weight, norm_gain_1[:, None], norm_gain_2[:, None]], axis=1)
    small = jnp.pad(small, ((0, 0), (0, 128 - EXPERTS - 2)))
    kv_pieces = gather_pieces(jnp.concatenate([beside(key_matrix, value_matrix), small], axis=1))
    kv_across = kv_pieces[1]
    kv_full = ordered(kv_pieces, member)
    router_full = kv_full[:, kv_width : kv_width + EXPERTS]
    gain_one = kv_full[:, kv_width + EXPERTS].astype(jnp.float32)
    gain_two = kv_full[:, kv_width + EXPERTS + 1].astype(jnp.float32)
    kv_full = kv_full[:, :kv_width]
    query_full = lax.all_gather(after(query_weight, kv_across), "wa", axis=0, tiled=True)
    out_full = lax.all_gather(after(out_weight, kv_across), "wa", axis=0, tiled=False)

    inverse_one = lax.rsqrt(jnp.mean(inputs * inputs, axis=-1, keepdims=True) + epsilon)
    normed_one = inputs * inverse_one
    normed_low = (normed_one * gain_one).astype(jnp.bfloat16)
    kv_own = dot32(normed_low, kv_full).astype(jnp.bfloat16).reshape(2, half_rows, kv_width)
    ring, other = [kv_own], []
    for step in range(lines - 1):
        ring.append(shift(after(ring[-1], *other), 1))
        other.append(flip(ring[step], "ctx", 1))
    other.append(flip(ring[-1], "ctx", 1))
    kv_all = jnp.concatenate(ring + other, axis=0)
    queries = dot32(normed_low, query_full).astype(jnp.bfloat16)

    hidden_share = shared_gate.shape[1] // members
    routes_all = jnp.concatenate(gather_pieces(after(routes.reshape(rows, TOP), ring[1])), axis=0)
    grad_pieces = gather_pieces(after(grad_low, ring[2]))
    queries = after(queries, routes_all, *grad_pieces)
    shared_w = jnp.concatenate(
        [
            shared_gate.reshape(share, members, hidden_share),
            shared_up.reshape(share, members, hidden_share),
            shared_down.T.reshape(share, members, hidden_share),
        ],
        axis=2,
    ).transpose(1, 0, 2)
    shared_w = lax.all_to_all(after(shared_w, ring[-1]), "wa", 0, 0, tiled=True)
    shared_w = shared_w.reshape(width, 3 * hidden_share)
    by_share = lambda value: value.reshape(rows, contexts, members, each).transpose(2, 0, 1, 3).reshape(
        members, rows, share
    )

    attended, log_sums = attention_forward(starts, own, queries, kv_all)
    mixed = jnp.concatenate([dot32(attended, out_full[m]) for m in range(members)], axis=1)
    residual = inputs + mixed
    inverse_two = lax.rsqrt(jnp.mean(residual * residual, axis=-1, keepdims=True) + epsilon)
    normed_two = residual * inverse_two
    second_low = after((normed_two * gain_two).astype(jnp.bfloat16), shared_w)

    second_pieces = gather_pieces(second_low)
    logits = jnp.concatenate([dot32(piece, router_full) for piece in second_pieces], axis=0)
    gates_all = dense_gates(logits, routes_all)
    at = jnp.stack([member * expert_gate.shape[0], context % 2]).astype(jnp.int32)
    out_keep, dx_keep, out_send, dx_send, gate_back, terms, pair_terms = experts_call(
        at, second_pieces, grad_pieces, gates_all, expert_gate, expert_up, expert_down,
        shared_w, contexts,
    )
    half = 2 * rows
    first_other = flip(terms[1, 1], "ctx", 1)
    second_other = flip(terms[2, 1], "ctx", 1)
    dx_own = reduce_rows(dx_keep, dx_send, jnp.bfloat16)
    gate_back = reduce_rows(gate_back[:half], gate_back[half:], jnp.float32)
    line_sums = scatter_lines(terms[0].swapaxes(0, 1))

    gates = gates_all[:rows]
    logit_grad = gates * (gate_back - jnp.sum(gates * gate_back, axis=-1, keepdims=True))
    router_term = lax.dot_general(
        logit_grad, second_low.astype(jnp.float32), (((0,), (0,)), ((), ())), precision=highest
    )
    second_grad = dx_own + jnp.dot(logit_grad, router_full.astype(jnp.float32).T, precision=highest)
    gain_two_term, residual_back = rms_back(second_grad, normed_two, inverse_two, gain_two)
    residual_grad = grad_rows + residual_back
    mix_low = residual_grad.astype(jnp.bfloat16)

    attended_grad = sum(
        dot32(mix_low[:, m * share : (m + 1) * share], out_full[m], ((1,), (1,)))
        for m in range(members)
    ).astype(jnp.bfloat16)
    query_low, kv_keep, kv_send = attention_backward(starts, own, queries, attended_grad, kv_all, log_sums)
    by_line = lambda parts: parts.reshape(lines, rows, kv_width)
    kv_near = by_line(kv_keep).astype(jnp.float32) + flip(by_line(kv_send), "ctx", 1).astype(jnp.float32)
    kv_parts = kv_near.astype(jnp.bfloat16)
    kv_low = kv_near[0]
    for steps in range(1, lines):
        kv_low = kv_low + shift(kv_parts[steps], -steps).astype(jnp.float32)
    kv_low = kv_low.astype(jnp.bfloat16)

    by_units = lambda value: value.reshape(-1, contexts, members, each).transpose(2, 0, 1, 3).reshape(
        members, -1, share
    )

    def widened(term, extra):
        count = extra.shape[0]
        total = jnp.sum(exchange(by_units(extra), member).reshape(members, count, share), axis=0)
        columns = jnp.pad(total, ((0, 128 - count), (0, 0))).T
        return jnp.concatenate([term, columns], axis=1).astype(jnp.bfloat16).reshape(contexts, each, -1)

    def side_sum(expert, received):
        near = terms[expert, 0].astype(jnp.float32) + received.astype(jnp.float32)
        return near.astype(jnp.bfloat16)

    near_one = side_sum(1, after(first_other, query_low))
    sum_one = scatter_lines(near_one)
    third_other = flip(after(terms[3, 1], near_one), "ctx", 1)

    normed_share = exchange(after(by_share(normed_low), query_low), member)
    query_all = jnp.concatenate(gather_pieces(query_low), axis=0)
    query_term = dot32(normed_share, query_all, ((0,), (0,))).astype(jnp.bfloat16)
    attended_all = jnp.concatenate(gather_pieces(after(attended, query_low)), axis=0)
    mix_share = exchange(after(by_share(mix_low), query_low), member)
    out_term = dot32(mix_share, attended_all, ((0,), (0,)))
    out_term = widened(out_term, jnp.concatenate([router_term, gain_two_term[None]], axis=0))
    out_own = reduce_rows(out_keep, after(out_send, out_term), jnp.bfloat16)
    block_out = (residual + out_own).astype(jnp.bfloat16).reshape(tokens.shape)

    near_two = side_sum(2, after(second_other, near_one))
    sum_two = scatter_lines(near_two)
    query_weight_grad = scatter_ctx(
        after(query_term.reshape(contexts, each, width), kv_near), context
    )
    out_sum = scatter_ctx(after(out_term, kv_near), context)
    out_weight_grad = out_sum[:, :width].T
    router_weight_grad = out_sum[:, width : width + EXPERTS]
    norm_gain_2_grad = out_sum[:, width + EXPERTS]

    kv_low_all = jnp.concatenate(gather_pieces(kv_low), axis=0)
    kv_term = dot32(normed_share, kv_low_all, ((0,), (0,)))
    first_grad = dot32(query_low, query_full, ((1,), (1,))) + dot32(kv_low, kv_full, ((1,), (1,)))
    gain_one_term, input_back = rms_back(first_grad, normed_one, inverse_one, gain_one)
    tokens_grad = (residual_grad + input_back).astype(jnp.bfloat16).reshape(tokens.shape)
    kv_sum = scatter_ctx(widened(kv_term, gain_one_term[None]), context)
    key_weight_grad, value_weight_grad = apart(kv_sum[:, :kv_width])
    norm_gain_1_grad = kv_sum[:, kv_width]

    near_three = side_sum(3, after(third_other, kv_low))
    sum_three = scatter_lines(near_three)
    sum_zero = line_sums[0].astype(jnp.float32) + flip(line_sums[1], "ctx", 1).astype(jnp.float32)
    expert_sums = [sum_zero, sum_one, sum_two, sum_three]
    expert_gate_grad = jnp.stack([total[0] for total in expert_sums]).astype(jnp.float32)
    expert_up_grad = jnp.stack([total[1] for total in expert_sums]).astype(jnp.float32)
    expert_down_grad = jnp.stack([total[2].T for total in expert_sums]).astype(jnp.float32)

    received = flip(after(pair_terms[1], near_two), "ctx", 1)
    near = pair_terms[0].astype(jnp.float32) + received.astype(jnp.float32)
    low = near.astype(jnp.bfloat16)
    line = context // 2
    shared_sum = lax.dynamic_index_in_dim(near, line, 0, keepdims=False)
    for steps in range(1, lines):
        piece = lax.dynamic_index_in_dim(low, (line + lines - steps) % lines, 0, keepdims=False)
        shared_sum = shared_sum + shift(piece, -steps).astype(jnp.float32)
    shared_sum = shared_sum.reshape(3, members, each, hidden_share).transpose(1, 0, 2, 3)
    shared_sum = lax.all_to_all(shared_sum, "wa", 0, 0, tiled=True)
    shared_gate_grad = shared_sum[:, 0].transpose(1, 0, 2).reshape(each, members * hidden_share)
    shared_up_grad = shared_sum[:, 1].transpose(1, 0, 2).reshape(each, members * hidden_share)
    shared_down_grad = shared_sum[:, 2].transpose(0, 2, 1).reshape(members * hidden_share, each)
    return (
        block_out,
        tokens_grad,
        norm_gain_1_grad,
        query_weight_grad,
        key_weight_grad,
        value_weight_grad,
        out_weight_grad,
        norm_gain_2_grad,
        router_weight_grad,
        shared_gate_grad,
        shared_up_grad,
        shared_down_grad,
        expert_gate_grad,
        expert_up_grad,
        expert_down_grad,
    )


def solution(mesh):
    return jax.shard_map(
        shards,
        mesh=mesh,
        in_specs=(
            P("wa", "ctx", None, None, None),
            P("wa", None),
            P("wa", "ctx", None, None, None),
            P("wa"),
            P("wa", None),
            P("wa", None),
            P("wa", None),
            P(None, "wa"),
            P("wa"),
            P("wa", None),
            P("wa", None),
            P("wa", None),
            P(None, "wa"),
            P("wa", None, None),
            P("wa", None, None),
            P("wa", None, None),
            P("wa", "ctx", None, None, None),
        ),
        out_specs=(
            P("wa", "ctx", None, None, None),
            P("wa", "ctx", None, None, None),
            P(("ctx", "wa")),
            P(("ctx", "wa"), None),
            P(("ctx", "wa"), None),
            P(("ctx", "wa"), None),
            P(None, ("ctx", "wa")),
            P(("ctx", "wa")),
            P(("ctx", "wa"), None),
            P(("ctx", "wa"), None),
            P(("ctx", "wa"), None),
            P(None, ("ctx", "wa")),
            P("wa", "ctx", None),
            P("wa", "ctx", None),
            P("wa", None, "ctx"),
        ),
        check_vma=False,
    )
```

```python
import functools

import jax
import jax.numpy as jnp
from jax import lax
from jax.experimental import pallas as pl
from jax.experimental.pallas import tpu as pltpu
from jax.sharding import PartitionSpec as P

QUERY_HEADS = 12
KEY_VALUE_HEADS = 4
HEAD_DIM = 128
TOP = 6
EXPERTS = 16

epsilon = 1e-05
large_negative = -1e30
highest = lax.Precision.HIGHEST
ORDER = (0, 2, 1, 3)


def dot32(left, right, dims=None):
    if dims is None:
        return jnp.dot(left, right, preferred_element_type=jnp.float32)
    return lax.dot_general(left, right, (dims, ((), ())), preferred_element_type=jnp.float32)


def flip(value, axis, bits):
    count = lax.axis_size(axis)
    return lax.ppermute(value, axis, [(i, i ^ bits) for i in range(count)])


def shift(value, steps):
    count = lax.axis_size("ctx")
    return lax.ppermute(value, "ctx", [(i, (i + 2 * steps) % count) for i in range(count)])


def after(value, *earlier):
    return lax.optimization_barrier((value,) + earlier)[0]


def gather_pieces(value):
    across = flip(value, "wa", 2)
    return [value, across, flip(value, "wa", 1), flip(across, "wa", 1)]


def ordered(pieces, index):
    chip, core = index // 2, index % 2
    near = [jnp.where(core == i, pieces[0], pieces[2]) for i in range(2)]
    far = [jnp.where(core == i, pieces[1], pieces[3]) for i in range(2)]
    return jnp.concatenate(
        [jnp.where(chip == i // 2, near[i % 2], far[i % 2]) for i in range(4)], axis=0
    )


def exchange(pieces, index):
    received = []
    for bits in ORDER:
        piece = lax.dynamic_index_in_dim(pieces, index ^ bits, 0, keepdims=False)
        received.append(piece if bits == 0 else flip(piece, "wa", bits))
    return received


def reduce_rows(keep, send, kind):
    near = keep + flip(send, "wa", 1).astype(jnp.float32)
    quarter = keep.shape[0] // 2
    return near[:quarter] + flip(near[quarter:].astype(kind), "wa", 2).astype(jnp.float32)


def scatter_small(value):
    rows, width = value.shape
    contexts, members = lax.axis_size("ctx"), lax.axis_size("wa")
    each = width // (contexts * members)
    spread = value.reshape(rows, contexts, members, each).transpose(2, 0, 1, 3)
    spread = spread.reshape(members, rows, contexts * each)
    first = jnp.sum(lax.all_to_all(spread, "wa", 0, 0, tiled=True), axis=0)
    second = first.reshape(rows, contexts, each).transpose(1, 0, 2)
    return jnp.sum(lax.all_to_all(second, "ctx", 0, 0, tiled=True), axis=0)


def sides():
    count = lax.axis_size("ctx")
    return [list(range(side, count, 2)) for side in range(2)]


def to_side(value, index):
    pairs = value.reshape((value.shape[0] // 2, 2) + value.shape[1:])
    keep = lax.dynamic_index_in_dim(pairs, index % 2, 1, keepdims=False)
    return keep, flip(lax.dynamic_index_in_dim(pairs, 1 - index % 2, 1, keepdims=False), "ctx", 1)


def line_sum(near, index):
    lines, line = near.shape[0], index // 2
    low = near.astype(jnp.bfloat16)
    total = lax.dynamic_index_in_dim(near, line, 0, keepdims=False)
    for steps in range(1, lines):
        piece = lax.dynamic_index_in_dim(low, (line + lines - steps) % lines, 0, keepdims=False)
        total = total + shift(piece, -steps).astype(jnp.float32)
    return total


def scatter_lines(value):
    return lax.psum_scatter(
        value, "ctx", scatter_dimension=0, axis_index_groups=sides(), tiled=True
    )[0]


def silu_parts(values):
    sigmoid_of = jax.nn.sigmoid(values)
    return (values * sigmoid_of, sigmoid_of * (1.0 + values * (1.0 - sigmoid_of)))


def rms_back(grad_normed, normed, inverse, gain_values):
    scaled = grad_normed * gain_values
    return (
        jnp.sum(grad_normed * normed, axis=0),
        inverse * (scaled - normed * jnp.mean(scaled * normed, axis=-1, keepdims=True)),
    )


TOGETHER = 3


def attention_masks(starts_ref, block, half_rows, shape):
    rows = block * half_rows + lax.broadcasted_iota(jnp.int32, shape, 0) % half_rows
    first = jnp.zeros(shape, jnp.int32)
    for document in range(1, starts_ref.shape[0]):
        start = starts_ref[document]
        first = jnp.where(start <= rows, jnp.maximum(first, start), first)
    return first, rows


def block_bounds(starts_ref, block, half_rows):
    top = block * half_rows
    first = jnp.int32(0)
    for document in range(1, starts_ref.shape[0]):
        start = starts_ref[document]
        first = jnp.where(start <= top, jnp.maximum(first, start), first)
    return first // half_rows


def block_place(block, own, contexts):
    late = (block >= contexts).astype(jnp.int32)
    device = jnp.where(block < contexts, block, 2 * contexts - 1 - block)
    lines = contexts // 2
    behind = own // 2 - device // 2
    behind = jnp.where(behind < 0, behind + lines, behind)
    return (((own + device) % 2) * lines + behind) * 2 + late


def attention_forward_kernel(starts_ref, own_ref, q_ref, kv_ref, o_ref, lse_ref, s_ref):
    blocks, half_rows, _ = kv_ref.shape
    contexts = blocks // 2
    ratio = q_ref.shape[1] // HEAD_DIM
    rows = ratio * half_rows
    scale = HEAD_DIM ** (-0.5)
    for half in range(2):
        block = own_ref[0] if half == 0 else blocks - 1 - own_ref[0]
        queries = jnp.concatenate(
            [
                q_ref[half * half_rows : (half + 1) * half_rows, h * HEAD_DIM : (h + 1) * HEAD_DIM]
                for h in range(ratio)
            ],
            axis=0,
        )
        low = block_bounds(starts_ref, block, half_rows)
        first, position = attention_masks(starts_ref, block, half_rows, (rows, half_rows))
        column = lax.broadcasted_iota(jnp.int32, (rows, half_rows), 1)

        trips = (block - low + TOGETHER) // TOGETHER

        def score_step(trip, running):
            for part in range(TOGETHER):
                step = trip * TOGETHER + part
                place = block_place(jnp.minimum(low + step, block), own_ref[0], contexts)
                scores = dot32(queries, kv_ref[place, :, :HEAD_DIM], ((1,), (1,))) * scale
                at = column + (low + step) * half_rows
                scores = jnp.where((at >= first) & (at <= position), scores, large_negative)
                s_ref[step] = scores
                running = jnp.maximum(running, scores)
            return running

        running = lax.fori_loop(
            0, trips, score_step, jnp.full((rows, half_rows), large_negative, jnp.float32)
        )
        row_max = jnp.max(running, axis=1, keepdims=True)

        def sum_step(trip, total):
            for part in range(TOGETHER):
                step = trip * TOGETHER + part
                expo = jnp.exp(s_ref[step] - row_max)
                s_ref[step] = expo
                total = total + expo
            return total

        total = lax.fori_loop(0, trips, sum_step, jnp.zeros((rows, half_rows), jnp.float32))
        row_sum = jnp.sum(total, axis=1, keepdims=True)
        inverse = 1.0 / row_sum

        def value_step(trip, accum):
            for part in range(TOGETHER):
                step = trip * TOGETHER + part
                place = block_place(jnp.minimum(low + step, block), own_ref[0], contexts)
                weights = (s_ref[step] * inverse).astype(jnp.bfloat16)
                accum = accum + dot32(weights, kv_ref[place, :, HEAD_DIM:])
            return accum

        accum = lax.fori_loop(0, trips, value_step, jnp.zeros((rows, HEAD_DIM), jnp.float32))
        log_sum = row_max + jnp.log(row_sum)
        lse_ref[0, half] = jnp.broadcast_to(log_sum, (rows, half_rows))
        for h in range(ratio):
            o_ref[half * half_rows : (half + 1) * half_rows, h * HEAD_DIM : (h + 1) * HEAD_DIM] = (
                accum[h * half_rows : (h + 1) * half_rows].astype(jnp.bfloat16)
            )


def attention_forward(starts, own, queries, kv):
    rows, width = queries.shape
    blocks, half_rows, _ = kv.shape
    ratio = QUERY_HEADS // KEY_VALUE_HEADS
    stacked = ratio * half_rows
    kv_spec = pl.BlockSpec((blocks, half_rows, 2 * HEAD_DIM), lambda g, *_: (0, 0, g))
    q_spec = pl.BlockSpec((rows, ratio * HEAD_DIM), lambda g, *_: (0, g))
    return pl.pallas_call(
        attention_forward_kernel,
        grid_spec=pltpu.PrefetchScalarGridSpec(
            num_scalar_prefetch=2,
            grid=(KEY_VALUE_HEADS,),
            in_specs=[q_spec, kv_spec],
            out_specs=[
                q_spec,
                pl.BlockSpec((1, 2, stacked, half_rows), lambda g, *_: (g, 0, 0, 0)),
            ],
            scratch_shapes=[pltpu.VMEM((blocks + TOGETHER - 1, stacked, half_rows), jnp.float32)],
        ),
        out_shape=(
            jax.ShapeDtypeStruct((rows, width), jnp.bfloat16),
            jax.ShapeDtypeStruct((KEY_VALUE_HEADS, 2, stacked, half_rows), jnp.float32),
        ),
        compiler_params=pltpu.CompilerParams(vmem_limit_bytes=48 << 20),
        cost_estimate=pl.CostEstimate(flops=0, bytes_accessed=1 << 20, transcendentals=0),
        name="attention_forward",
    )(starts, own, queries, kv)


def attention_backward_kernel(
    starts_ref, own_ref, q_ref, do_ref, kv_ref, lse_ref, dq_ref, keep_ref, send_ref, p_ref, dp_ref, dka_ref, dva_ref
):
    blocks, half_rows, _ = kv_ref.shape
    contexts = blocks // 2
    ratio = q_ref.shape[1] // HEAD_DIM
    rows = ratio * half_rows
    scale = HEAD_DIM ** (-0.5)
    dka_ref[...] = jnp.zeros_like(dka_ref)
    dva_ref[...] = jnp.zeros_like(dva_ref)

    def stack(ref, half):
        return jnp.concatenate(
            [
                ref[half * half_rows : (half + 1) * half_rows, h * HEAD_DIM : (h + 1) * HEAD_DIM]
                for h in range(ratio)
            ],
            axis=0,
        )

    for half in range(2):
        block = own_ref[0] if half == 0 else blocks - 1 - own_ref[0]
        queries = stack(q_ref, half)
        grads = stack(do_ref, half)
        log_sum = lse_ref[0, half]
        low = block_bounds(starts_ref, block, half_rows)
        first, position = attention_masks(starts_ref, block, half_rows, (rows, half_rows))
        column = lax.broadcasted_iota(jnp.int32, (rows, half_rows), 1)

        trips = (block - low + TOGETHER) // TOGETHER

        def prob_step(trip, running):
            for part in range(TOGETHER):
                step = trip * TOGETHER + part
                place = block_place(jnp.minimum(low + step, block), own_ref[0], contexts)
                scores = dot32(queries, kv_ref[place, :, :HEAD_DIM], ((1,), (1,))) * scale
                at = column + (low + step) * half_rows
                probs = jnp.where(
                    (at >= first) & (at <= position), jnp.exp(scores - log_sum), 0.0
                )
                prob_grads = dot32(grads, kv_ref[place, :, HEAD_DIM:], ((1,), (1,)))
                p_ref[step] = probs
                dp_ref[step] = prob_grads
                running = running + probs * prob_grads
            return running

        running = lax.fori_loop(0, trips, prob_step, jnp.zeros((rows, half_rows), jnp.float32))
        delta = jnp.sum(running, axis=1, keepdims=True)

        def grad_step(trip, query_grad):
            for part in range(TOGETHER):
                step = trip * TOGETHER + part
                place = block_place(jnp.minimum(low + step, block), own_ref[0], contexts)
                probs = p_ref[step]
                score_low = (probs * (dp_ref[step] - delta)).astype(jnp.bfloat16)
                dka_ref[place] += dot32(score_low, queries, ((0,), (0,)))
                dva_ref[place] += dot32(probs.astype(jnp.bfloat16), grads, ((0,), (0,)))
                query_grad = query_grad + dot32(score_low, kv_ref[place, :, :HEAD_DIM])
            return query_grad

        query_grad = lax.fori_loop(0, trips, grad_step, jnp.zeros((rows, HEAD_DIM), jnp.float32))
        for h in range(ratio):
            dq_ref[half * half_rows : (half + 1) * half_rows, h * HEAD_DIM : (h + 1) * HEAD_DIM] = (
                query_grad[h * half_rows : (h + 1) * half_rows] * scale
            ).astype(jnp.bfloat16)
    for out_ref, places in ((keep_ref, slice(0, contexts)), (send_ref, slice(contexts, blocks))):
        out_ref[:, :, :HEAD_DIM] = (dka_ref[places] * scale).astype(jnp.bfloat16)
        out_ref[:, :, HEAD_DIM:] = dva_ref[places].astype(jnp.bfloat16)


def attention_backward(starts, own, queries, grads, kv, log_sums):
    rows, width = queries.shape
    blocks, half_rows, kv_width = kv.shape
    ratio = QUERY_HEADS // KEY_VALUE_HEADS
    stacked = ratio * half_rows
    kv_spec = pl.BlockSpec((blocks, half_rows, 2 * HEAD_DIM), lambda g, *_: (0, 0, g))
    part_spec = pl.BlockSpec((blocks // 2, half_rows, 2 * HEAD_DIM), lambda g, *_: (0, 0, g))
    q_spec = pl.BlockSpec((rows, ratio * HEAD_DIM), lambda g, *_: (0, g))
    return pl.pallas_call(
        attention_backward_kernel,
        grid_spec=pltpu.PrefetchScalarGridSpec(
            num_scalar_prefetch=2,
            grid=(KEY_VALUE_HEADS,),
            in_specs=[
                q_spec,
                q_spec,
                kv_spec,
                pl.BlockSpec((1, 2, stacked, half_rows), lambda g, *_: (g, 0, 0, 0)),
            ],
            out_specs=[q_spec, part_spec, part_spec],
            scratch_shapes=[
                pltpu.VMEM((blocks + TOGETHER - 1, stacked, half_rows), jnp.float32),
                pltpu.VMEM((blocks + TOGETHER - 1, stacked, half_rows), jnp.float32),
                pltpu.VMEM((blocks, half_rows, HEAD_DIM), jnp.float32),
                pltpu.VMEM((blocks, half_rows, HEAD_DIM), jnp.float32),
            ],
        ),
        out_shape=(
            jax.ShapeDtypeStruct((rows, width), jnp.bfloat16),
            jax.ShapeDtypeStruct((blocks // 2, half_rows, kv_width), jnp.bfloat16),
            jax.ShapeDtypeStruct((blocks // 2, half_rows, kv_width), jnp.bfloat16),
        ),
        compiler_params=pltpu.CompilerParams(vmem_limit_bytes=58 << 20),
        cost_estimate=pl.CostEstimate(flops=0, bytes_accessed=1 << 20, transcendentals=0),
        name="attention_backward",
    )(starts, own, queries, grads, kv, log_sums)


def experts_kernel(final, *refs):
    at_ref, *refs = refs
    parts, refs = refs[:8], refs[8:]
    g_ref, wg_ref, wu_ref, wd_ref, *refs = refs
    if final:
        shared_ref, out_in, dx_in, tail_in, dg_in, *refs = refs
        out_ref, dx_ref, out_low_ref, dx_low_ref, dg_ref, *refs = refs
        targets = tuple((refs[0].at[:, number], refs[1].at[:, number]) for number in range(2))
        pair_target, refs = (refs[2], refs[3]), refs[4:]
        x_ref, dy_ref, he_ref, da_ref, db_ref, tail_ref, sem = refs
    else:
        out_ref, dx_ref, tail_ref, dg_ref, *refs = refs
        targets, refs = (refs[0], (refs[1], refs[2])), refs[3:]
        x_ref, dy_ref, he_ref, da_ref, db_ref, sem = refs
    local = pl.program_id(0)
    expert = at_ref[0] + local
    side = at_ref[1]
    total_rows, width = x_ref.shape
    half = total_rows // 2
    step_rows = 256
    tall = 384

    @pl.when(local == 0)
    def _():
        size = total_rows // 4
        moves = []
        for number, source in enumerate(parts):
            whole = (x_ref, dy_ref)[number // 4]
            moves.append((source, whole.at[pl.ds(number % 4 * size, size), :]))
        if final:
            moves += [(out_in, out_ref), (dx_in, dx_ref), (tail_in, tail_ref), (dg_in, dg_ref)]
        copies = [
            pltpu.make_async_copy(source, target, sem.at[number])
            for number, (source, target) in enumerate(moves)
        ]
        for copy in copies:
            copy.start()
        if not final:
            for ref in (out_ref, dx_ref, tail_ref, dg_ref):
                ref[...] = jnp.zeros_like(ref)
        for copy in copies:
            copy.wait()

    def add(number, rows, value):
        if rows.start < half:
            (out_ref, dx_ref)[number][rows, :] += value
        else:
            tail_ref[number, slice(rows.start - half, rows.stop - half), :] += value

    def store_sides(lows, begin, pair):
        per = pair[0].shape[2]
        for parity in range(2):

            @pl.when(side == parity)
            def _():
                for part in range(tall // per):
                    line = begin // (2 * per) + part // 2
                    for number, low in enumerate(lows):
                        pair[(part + parity) % 2][line, number] = low[part * per : (part + 1) * per]

    def store_lines(lows, begin, target):
        per = target.shape[3]
        for part in range(tall // per):
            line = begin // (2 * per) + part // 2
            for number, low in enumerate(lows):
                target[line, (side + part) % 2, number] = low[part * per : (part + 1) * per]

    for begin in range(0, total_rows, step_rows):
        rows = slice(begin, begin + step_rows)
        x = x_ref[rows, :]
        lane = lax.broadcasted_iota(jnp.int32, (step_rows, g_ref.shape[1]), 1)
        mine = lane == expert
        gate = jnp.sum(jnp.where(mine, g_ref[rows, :], 0.0), axis=1, keepdims=True)
        pre = dot32(x, wg_ref[0])
        up = dot32(x, wu_ref[0])
        back = dot32(dy_ref[rows, :], wd_ref[0], ((1,), (1,)))
        silu, slope = silu_parts(pre)
        hidden = (silu * up).astype(jnp.bfloat16).astype(jnp.float32)
        dg_ref[rows, :] += jnp.where(mine, jnp.sum(hidden * back, axis=1, keepdims=True), 0.0)
        hidden_low = (gate * hidden).astype(jnp.bfloat16)
        he_ref[rows, :] = hidden_low
        add(0, rows, dot32(hidden_low, wd_ref[0]))
        back = gate * back
        pre_low = (back * up * slope).astype(jnp.bfloat16)
        up_low = (back * silu).astype(jnp.bfloat16)
        da_ref[rows, :] = pre_low
        db_ref[rows, :] = up_low
        add(1, rows, dot32(pre_low, wg_ref[0], ((1,), (1,))) + dot32(up_low, wu_ref[0], ((1,), (1,))))

    @pl.loop(0, width // tall)
    def _(step):
        begin = pl.multiple_of(step * tall, tall)
        columns = pl.ds(begin, tall)
        lows = [
            dot32(left[:, columns], right[...], ((0,), (0,))).astype(jnp.bfloat16)
            for left, right in ((x_ref, da_ref), (x_ref, db_ref), (dy_ref, he_ref))
        ]
        for number, target in enumerate(targets):

            @pl.when(local == number)
            def _():
                if isinstance(target, tuple):
                    store_sides(lows, begin, target)
                else:
                    store_lines(lows, begin, target)

    if not final:
        return

    @pl.when(local == pl.num_programs(0) - 1)
    def _():
        shared = shared_ref.shape[1] // 3
        pair_w, down_w = slice(0, 2 * shared), slice(2 * shared, 3 * shared)
        for begin in range(0, total_rows, step_rows):
            rows = slice(begin, begin + step_rows)
            both = dot32(x_ref[rows, :], shared_ref[:, pair_w])
            pre, up = both[:, :shared], both[:, shared:]
            silu, slope = silu_parts(pre)
            hidden = (silu * up).astype(jnp.bfloat16)
            he_ref[rows, :shared] = hidden
            add(0, rows, dot32(hidden, shared_ref[:, down_w], ((1,), (1,))))
            back = dot32(dy_ref[rows, :], shared_ref[:, down_w])
            da_ref[rows, :shared] = (back * up * slope).astype(jnp.bfloat16)
            da_ref[rows, shared:] = (back * silu).astype(jnp.bfloat16)
            add(1, rows, dot32(da_ref[rows, :], shared_ref[:, pair_w], ((1,), (1,))))
        out_low_ref[...] = tail_ref[0].astype(jnp.bfloat16)
        dx_low_ref[...] = tail_ref[1].astype(jnp.bfloat16)

        @pl.loop(0, width // tall)
        def _(step):
            begin = pl.multiple_of(step * tall, tall)
            columns = pl.ds(begin, tall)
            pair_low = dot32(x_ref[:, columns], da_ref[...], ((0,), (0,))).astype(jnp.bfloat16)
            down_low = dot32(dy_ref[:, columns], he_ref[:, :shared], ((0,), (0,))).astype(jnp.bfloat16)
            store_sides((pair_low[:, :shared], pair_low[:, shared:], down_low), begin, pair_target)


def experts_call(at, x, dy, gates, weights, first, contexts, shared_w=None, carried=()):
    final = shared_w is not None
    gate_w, up_w, down_w = weights
    rows, width = 4 * x[0].shape[0], x[0].shape[1]
    hidden = gate_w.shape[2]
    per, lines, half = width // contexts, contexts // 2, rows // 2
    once = pl.Buffered(1)
    whole = lambda shape: pl.BlockSpec(shape, lambda e, *_: (0,) * len(shape), pipeline_mode=once)
    weight = lambda shape: pl.BlockSpec((1,) + shape, lambda e, *_: (first + e, 0, 0))
    apart = pl.BlockSpec(memory_space=pl.ANY)
    part = jax.ShapeDtypeStruct((half, width), jnp.float32)
    low = jax.ShapeDtypeStruct((half, width), jnp.bfloat16)
    tail = jax.ShapeDtypeStruct((2, half, width), jnp.float32)
    table = jax.ShapeDtypeStruct((rows, EXPERTS), jnp.float32)
    term = jax.ShapeDtypeStruct((lines, 3, per, hidden), jnp.bfloat16)
    both = jax.ShapeDtypeStruct((lines, 2, 3, per, hidden), jnp.bfloat16)
    scratch = [pltpu.VMEM((rows, width), jnp.bfloat16)] * 2 + [pltpu.VMEM((rows, hidden), jnp.bfloat16)] * 3
    if final:
        shared = shared_w.shape[1] // 3
        pair = jax.ShapeDtypeStruct((lines, 3, per, shared), jnp.bfloat16)
        extra_specs = [whole(shared_w.shape)] + [apart] * 4
        out_shape = (part, part, low, low, table, both, both, pair, pair)
        scratch.append(pltpu.VMEM(tail.shape, jnp.float32))
    else:
        shared = 0
        extra_specs = []
        out_shape = (part, part, tail, table, both, term, term)
    return pl.pallas_call(
        functools.partial(experts_kernel, final),
        grid_spec=pltpu.PrefetchScalarGridSpec(
            num_scalar_prefetch=1,
            grid=(2,),
            in_specs=[apart] * 8
            + [
                whole((rows, EXPERTS)),
                weight((width, hidden)),
                weight((width, hidden)),
                weight((hidden, width)),
            ]
            + extra_specs,
            out_specs=[whole(item.shape) for item in out_shape],
            scratch_shapes=scratch + [pltpu.SemaphoreType.DMA((12,))],
        ),
        out_shape=out_shape,
        compiler_params=pltpu.CompilerParams(vmem_limit_bytes=60 << 20),
        cost_estimate=pl.CostEstimate(flops=0, bytes_accessed=1 << 20, transcendentals=0),
        name="experts_final" if final else "experts",
    )(at, *x, *dy, gates, gate_w, up_w, down_w, *((shared_w,) if final else ()), *carried)


def dense_gates(logits, routes):
    chosen = jnp.any(
        routes[:, :, None] == jnp.arange(EXPERTS, dtype=jnp.int32)[None, None, :], axis=1
    )
    top = jnp.max(jnp.where(chosen, logits, large_negative), axis=-1, keepdims=True)
    expo = jnp.where(chosen, jnp.exp(logits - top), 0.0)
    return expo / jnp.sum(expo, axis=-1, keepdims=True)


def shards(
    tokens, doc_starts, routes, norm_gain_1, query_weight, key_matrix, value_matrix, out_weight,
    norm_gain_2, router_weight, shared_gate, shared_up, shared_down, expert_gate, expert_up,
    expert_down, out_grad,
):
    contexts, members = lax.axis_size("ctx"), lax.axis_size("wa")
    context, member = lax.axis_index("ctx"), lax.axis_index("wa")
    half_rows, width = tokens.shape[3], tokens.shape[4]
    rows = 2 * half_rows
    share = width // members
    each = share // contexts
    lines = contexts // 2
    kv_width = 2 * key_matrix.shape[1]
    starts = doc_starts[0]
    own = context[None].astype(jnp.int32)
    inputs = tokens.reshape(rows, width).astype(jnp.float32)
    grad_low = out_grad.reshape(rows, width)
    grad_rows = grad_low.astype(jnp.float32)

    beside = lambda k, v: jnp.stack(
        [k.reshape(-1, KEY_VALUE_HEADS, HEAD_DIM), v.reshape(-1, KEY_VALUE_HEADS, HEAD_DIM)], axis=2
    ).reshape(-1, kv_width)
    apart = lambda kv: jnp.moveaxis(
        kv.reshape(-1, KEY_VALUE_HEADS, 2, HEAD_DIM), 2, 0
    ).reshape(2, -1, kv_width // 2)
    small = jnp.concatenate([router_weight, norm_gain_1[:, None], norm_gain_2[:, None]], axis=1)
    small = jnp.pad(small, ((0, 0), (0, 128 - EXPERTS - 2)))
    kv_pieces = gather_pieces(jnp.concatenate([beside(key_matrix, value_matrix), small], axis=1))
    kv_across = kv_pieces[1]
    kv_full = ordered(kv_pieces, member)
    router_full = kv_full[:, kv_width : kv_width + EXPERTS]
    gain_one = kv_full[:, kv_width + EXPERTS].astype(jnp.float32)
    gain_two = kv_full[:, kv_width + EXPERTS + 1].astype(jnp.float32)
    kv_full = kv_full[:, :kv_width]
    query_full = lax.all_gather(after(query_weight, kv_across), "wa", axis=0, tiled=True)
    out_full = lax.all_gather(after(out_weight, kv_across), "wa", axis=0, tiled=False)

    inverse_one = lax.rsqrt(jnp.mean(inputs * inputs, axis=-1, keepdims=True) + epsilon)
    normed_one = inputs * inverse_one
    normed_low = (normed_one * gain_one).astype(jnp.bfloat16)
    kv_own = dot32(normed_low, kv_full).astype(jnp.bfloat16).reshape(2, half_rows, kv_width)
    ring, other = [kv_own], []
    for step in range(lines - 1):
        ring.append(shift(after(ring[-1], *other), 1))
        other.append(flip(ring[step], "ctx", 1))
    other.append(flip(ring[-1], "ctx", 1))
    kv_all = jnp.concatenate(ring + other, axis=0)
    queries = dot32(normed_low, query_full).astype(jnp.bfloat16)

    hidden_share = shared_gate.shape[1] // members
    routes_all = jnp.concatenate(gather_pieces(after(routes.reshape(rows, TOP), ring[1])), axis=0)
    grad_pieces = gather_pieces(after(grad_low, ring[1]))
    queries = after(queries, routes_all)
    shared_w = jnp.concatenate(
        [
            shared_gate.reshape(share, members, hidden_share),
            shared_up.reshape(share, members, hidden_share),
            shared_down.T.reshape(share, members, hidden_share),
        ],
        axis=2,
    ).transpose(1, 0, 2)
    shared_w = lax.all_to_all(after(shared_w, ring[-1]), "wa", 0, 0, tiled=True)
    shared_w = shared_w.reshape(width, 3 * hidden_share)
    by_share = lambda value: value.reshape(rows, contexts, members, each).transpose(2, 0, 1, 3).reshape(
        members, rows, share
    )

    attended, log_sums = attention_forward(starts, own, queries, kv_all)
    mixed = jnp.concatenate([dot32(attended, out_full[m]) for m in range(members)], axis=1)
    residual = inputs + mixed
    inverse_two = lax.rsqrt(jnp.mean(residual * residual, axis=-1, keepdims=True) + epsilon)
    normed_two = residual * inverse_two
    second_low = after((normed_two * gain_two).astype(jnp.bfloat16), shared_w, *grad_pieces)

    second_pieces = gather_pieces(second_low)
    logits = jnp.concatenate([dot32(piece, router_full) for piece in second_pieces], axis=0)
    gates_all = dense_gates(logits, routes_all)
    attended_across = flip(after(attended, second_pieces[3]), "wa", 2)
    local = expert_gate.shape[0]
    weights = (expert_gate, expert_up, expert_down)
    at = lambda first: jnp.stack([member * local + first, context % 2]).astype(jnp.int32)
    *carried, line_terms, keep_one, send_one = experts_call(
        at(0), second_pieces, grad_pieces, gates_all, weights, 0, contexts
    )
    line_sums = scatter_lines(line_terms)
    other_one = flip(send_one, "ctx", 1)
    (
        out_keep, dx_keep, out_send, dx_send, gate_back,
        keep_both, send_both, pair_keep, pair_send,
    ) = experts_call(
        at(2), second_pieces, grad_pieces, gates_all, weights, 2, contexts, shared_w, carried
    )
    other_both = flip(send_both, "ctx", 1)

    def side_sum(keep, received):
        return keep.astype(jnp.float32) + received.astype(jnp.float32)

    dx_near = dx_keep + flip(after(dx_send, other_one, attended_across), "wa", 1).astype(jnp.float32)
    dx_moved = flip(dx_near[rows:].astype(jnp.bfloat16), "wa", 2)
    dx_own = dx_near[:rows] + dx_moved.astype(jnp.float32)
    half = 2 * rows
    gate_back = reduce_rows(gate_back[:half], gate_back[half:], jnp.float32)

    gates = gates_all[:rows]
    logit_grad = gates * (gate_back - jnp.sum(gates * gate_back, axis=-1, keepdims=True))
    router_term = lax.dot_general(
        logit_grad, second_low.astype(jnp.float32), (((0,), (0,)), ((), ())), precision=highest
    )
    second_grad = dx_own + jnp.dot(logit_grad, router_full.astype(jnp.float32).T, precision=highest)
    gain_two_term, residual_back = rms_back(second_grad, normed_two, inverse_two, gain_two)
    residual_grad = grad_rows + residual_back
    mix_low = residual_grad.astype(jnp.bfloat16)

    def shared_out(extra):
        count = extra.shape[0]
        pieces = extra.reshape(count, contexts, members, each).transpose(2, 0, 1, 3)
        return exchange(pieces.reshape(members, count, share), member)

    def widened(term, pieces):
        total = sum(pieces)
        columns = jnp.pad(total, ((0, 128 - total.shape[0]), (0, 0))).T
        return jnp.concatenate([term, columns], axis=1).astype(jnp.bfloat16).reshape(contexts, each, -1)

    attended_grad = sum(
        dot32(mix_low[:, m * share : (m + 1) * share], out_full[m], ((1,), (1,)))
        for m in range(members)
    ).astype(jnp.bfloat16)
    small_terms = jnp.concatenate([router_term, gain_two_term[None]], axis=0)
    near_one = side_sum(keep_one, after(other_one, dx_moved)) + 0.0 * line_sums[0, 0, 0, 0].astype(jnp.float32)
    near_one = near_one.astype(jnp.bfloat16)
    sum_one = scatter_lines(near_one)
    attended_grad = after(attended_grad, near_one)
    query_low, kv_keep, kv_send = attention_backward(starts, own, queries, attended_grad, kv_all, log_sums)
    by_line = lambda parts: parts.reshape(lines, rows, kv_width)
    kv_send = after(by_line(kv_send), other_both)
    received = flip(kv_send, "ctx", 1)
    query_pieces = gather_pieces(query_low)
    mix_pieces = exchange(after(by_share(mix_low), query_low), member)
    small_pieces = shared_out(after(small_terms, query_low))
    normed_pieces = exchange(after(by_share(normed_low), query_low), member)
    attended_pieces = [attended, attended_across] + [
        flip(after(piece, query_low), "wa", 1) for piece in (attended, attended_across)
    ]
    out_near = out_keep + flip(after(out_send, query_low), "wa", 1).astype(jnp.float32)
    out_moved = flip(out_near[rows:].astype(jnp.bfloat16), "wa", 2)
    out_own = out_near[:rows] + out_moved.astype(jnp.float32)
    block_out = (residual + out_own).astype(jnp.bfloat16).reshape(tokens.shape)
    moved = mix_pieces[1:] + small_pieces[1:] + normed_pieces[1:] + attended_pieces[2:]
    received = after(received, out_moved, query_pieces[3], *moved)
    kv_near = by_line(kv_keep).astype(jnp.float32) + received.astype(jnp.float32)
    kv_parts = kv_near.astype(jnp.bfloat16)
    kv_moved = [shift(kv_parts[steps], -steps) for steps in range(1, lines)]
    near_both = side_sum(keep_both, after(other_both, kv_parts)).astype(jnp.bfloat16)
    sum_both = scatter_lines(near_both)
    kv_moved[0] = after(kv_moved[0], near_both)
    kv_low = (kv_near[0] + sum(moved.astype(jnp.float32) for moved in kv_moved)).astype(jnp.bfloat16)

    stacked = lambda pieces: jnp.concatenate(pieces, axis=0)
    normed_share = stacked(normed_pieces)
    query_term = dot32(normed_share, stacked(query_pieces), ((0,), (0,))).astype(jnp.bfloat16)
    out_term = dot32(stacked(mix_pieces), stacked(attended_pieces), ((0,), (0,)))
    out_term = widened(out_term, small_pieces)

    early_term = jnp.concatenate([query_term.reshape(contexts, each, width), out_term], axis=2)
    early_sides = to_side(after(early_term, kv_parts), context)
    other_pair = flip(after(pair_send, kv_parts), "ctx", 1)

    kv_low_pieces = gather_pieces(kv_low)
    early_sides = (early_sides[0], after(early_sides[1], kv_low_pieces[3]))
    kv_low_all = stacked(kv_low_pieces)
    kv_term = dot32(normed_share, kv_low_all, ((0,), (0,)))
    first_grad = dot32(query_low, query_full, ((1,), (1,))) + dot32(kv_low, kv_full, ((1,), (1,)))
    scaled = first_grad * gain_one
    input_back = inverse_one * (
        scaled - normed_one * jnp.mean(scaled * normed_one, axis=-1, keepdims=True)
    )
    tokens_grad = (residual_grad + input_back).astype(jnp.bfloat16).reshape(tokens.shape)
    kv_sides = to_side(kv_term.astype(jnp.bfloat16).reshape(contexts, each, kv_width), context)
    kv_sum = line_sum(side_sum(*kv_sides), context)
    early_sum = line_sum(side_sum(*early_sides), context)
    query_weight_grad, out_sum = early_sum[:, :width], early_sum[:, width:]
    out_weight_grad = out_sum[:, :width].T
    router_weight_grad = out_sum[:, width : width + EXPERTS]
    norm_gain_2_grad = out_sum[:, width + EXPERTS]
    key_weight_grad, value_weight_grad = apart(kv_sum)
    mine = lambda full: lax.dynamic_slice_in_dim(full, (context * members + member) * each, each, 0)
    norm_gain_1_grad = (
        jnp.sum(mine(query_full).astype(jnp.float32) * query_weight_grad, axis=1)
        + jnp.sum(mine(kv_full).astype(jnp.float32) * kv_sum, axis=1)
    ) / mine(gain_one)

    line_zero = flip(after(line_sums[1], kv_low_pieces[1]), "ctx", 1)
    sum_zero = line_sums[0].astype(jnp.float32) + line_zero.astype(jnp.float32)
    expert_sums = [sum_zero, sum_one, sum_both[0], sum_both[1]]
    expert_gate_grad = jnp.stack([total[0] for total in expert_sums]).astype(jnp.float32)
    expert_up_grad = jnp.stack([total[1] for total in expert_sums]).astype(jnp.float32)
    expert_down_grad = jnp.stack([total[2].T for total in expert_sums]).astype(jnp.float32)

    shared_sum = line_sum(side_sum(pair_keep, after(other_pair, kv_low_pieces[3])), context)
    shared_sum = shared_sum.reshape(3, members, each, hidden_share).transpose(1, 0, 2, 3)
    shared_sum = lax.all_to_all(shared_sum, "wa", 0, 0, tiled=True)
    shared_gate_grad = shared_sum[:, 0].transpose(1, 0, 2).reshape(each, members * hidden_share)
    shared_up_grad = shared_sum[:, 1].transpose(1, 0, 2).reshape(each, members * hidden_share)
    shared_down_grad = shared_sum[:, 2].transpose(0, 2, 1).reshape(members * hidden_share, each)
    return (
        block_out,
        tokens_grad,
        norm_gain_1_grad,
        query_weight_grad,
        key_weight_grad,
        value_weight_grad,
        out_weight_grad,
        norm_gain_2_grad,
        router_weight_grad,
        shared_gate_grad,
        shared_up_grad,
        shared_down_grad,
        expert_gate_grad,
        expert_up_grad,
        expert_down_grad,
    )


def solution(mesh):
    return jax.shard_map(
        shards,
        mesh=mesh,
        in_specs=(
            P("wa", "ctx", None, None, None),
            P("wa", None),
            P("wa", "ctx", None, None, None),
            P("wa"),
            P("wa", None),
            P("wa", None),
            P("wa", None),
            P(None, "wa"),
            P("wa"),
            P("wa", None),
            P("wa", None),
            P("wa", None),
            P(None, "wa"),
            P("wa", None, None),
            P("wa", None, None),
            P("wa", None, None),
            P("wa", "ctx", None, None, None),
        ),
        out_specs=(
            P("wa", "ctx", None, None, None),
            P("wa", "ctx", None, None, None),
            P(("ctx", "wa")),
            P(("ctx", "wa"), None),
            P(("ctx", "wa"), None),
            P(("ctx", "wa"), None),
            P(None, ("ctx", "wa")),
            P(("ctx", "wa")),
            P(("ctx", "wa"), None),
            P(("ctx", "wa"), None),
            P(("ctx", "wa"), None),
            P(None, ("ctx", "wa")),
            P("wa", "ctx", None),
            P("wa", "ctx", None),
            P("wa", None, "ctx"),
        ),
        check_vma=False,
    )
```

```python
import functools

import jax
import jax.numpy as jnp
from jax import lax
from jax.experimental import pallas as pl
from jax.experimental.pallas import tpu as pltpu
from jax.sharding import PartitionSpec as P

QUERY_HEADS = 12
KEY_VALUE_HEADS = 4
HEAD_DIM = 128
TOP = 6
EXPERTS = 16

epsilon = 1e-05
large_negative = -1e30
highest = lax.Precision.HIGHEST
ORDER = (0, 2, 1, 3)


def dot32(left, right, dims=None):
    if dims is None:
        return jnp.dot(left, right, preferred_element_type=jnp.float32)
    return lax.dot_general(left, right, (dims, ((), ())), preferred_element_type=jnp.float32)


def flip(value, axis, bits):
    count = lax.axis_size(axis)
    return lax.ppermute(value, axis, [(i, i ^ bits) for i in range(count)])


def shift(value, steps):
    count = lax.axis_size("ctx")
    return lax.ppermute(value, "ctx", [(i, (i + 2 * steps) % count) for i in range(count)])


def after(value, *earlier):
    return lax.optimization_barrier((value,) + earlier)[0]


def gather_pieces(value):
    across = flip(value, "wa", 2)
    return [value, across, flip(value, "wa", 1), flip(across, "wa", 1)]


def ordered(pieces, index):
    chip, core = index // 2, index % 2
    near = [jnp.where(core == i, pieces[0], pieces[2]) for i in range(2)]
    far = [jnp.where(core == i, pieces[1], pieces[3]) for i in range(2)]
    return jnp.concatenate(
        [jnp.where(chip == i // 2, near[i % 2], far[i % 2]) for i in range(4)], axis=0
    )


def exchange(pieces, index):
    received = []
    for bits in ORDER:
        piece = lax.dynamic_index_in_dim(pieces, index ^ bits, 0, keepdims=False)
        received.append(piece if bits == 0 else flip(piece, "wa", bits))
    return received


def reduce_rows(keep, send, kind):
    near = keep + flip(send, "wa", 1).astype(jnp.float32)
    quarter = keep.shape[0] // 2
    return near[:quarter] + flip(near[quarter:].astype(kind), "wa", 2).astype(jnp.float32)


def scatter_small(value):
    rows, width = value.shape
    contexts, members = lax.axis_size("ctx"), lax.axis_size("wa")
    each = width // (contexts * members)
    spread = value.reshape(rows, contexts, members, each).transpose(2, 0, 1, 3)
    spread = spread.reshape(members, rows, contexts * each)
    first = jnp.sum(lax.all_to_all(spread, "wa", 0, 0, tiled=True), axis=0)
    second = first.reshape(rows, contexts, each).transpose(1, 0, 2)
    return jnp.sum(lax.all_to_all(second, "ctx", 0, 0, tiled=True), axis=0)


def sides():
    count = lax.axis_size("ctx")
    return [list(range(side, count, 2)) for side in range(2)]


def to_side(value, index):
    pairs = value.reshape((value.shape[0] // 2, 2) + value.shape[1:])
    keep = lax.dynamic_index_in_dim(pairs, index % 2, 1, keepdims=False)
    return keep, flip(lax.dynamic_index_in_dim(pairs, 1 - index % 2, 1, keepdims=False), "ctx", 1)


def line_sum(near, index):
    lines, line = near.shape[0], index // 2
    low = near.astype(jnp.bfloat16)
    total = lax.dynamic_index_in_dim(near, line, 0, keepdims=False)
    for steps in range(1, lines):
        piece = lax.dynamic_index_in_dim(low, (line + lines - steps) % lines, 0, keepdims=False)
        total = total + shift(piece, -steps).astype(jnp.float32)
    return total


def scatter_lines(value):
    return lax.psum_scatter(
        value, "ctx", scatter_dimension=0, axis_index_groups=sides(), tiled=True
    )[0]


def silu_parts(values):
    sigmoid_of = jax.nn.sigmoid(values)
    return (values * sigmoid_of, sigmoid_of * (1.0 + values * (1.0 - sigmoid_of)))


def rms_back(grad_normed, normed, inverse, gain_values):
    scaled = grad_normed * gain_values
    return (
        jnp.sum(grad_normed * normed, axis=0),
        inverse * (scaled - normed * jnp.mean(scaled * normed, axis=-1, keepdims=True)),
    )


TOGETHER = 3


def attention_masks(starts_ref, block, half_rows, shape):
    rows = block * half_rows + lax.broadcasted_iota(jnp.int32, shape, 0) % half_rows
    first = jnp.zeros(shape, jnp.int32)
    for document in range(1, starts_ref.shape[0]):
        start = starts_ref[document]
        first = jnp.where(start <= rows, jnp.maximum(first, start), first)
    return first, rows


def block_bounds(starts_ref, block, half_rows):
    top = block * half_rows
    first = jnp.int32(0)
    for document in range(1, starts_ref.shape[0]):
        start = starts_ref[document]
        first = jnp.where(start <= top, jnp.maximum(first, start), first)
    return first // half_rows


def block_place(block, own, contexts):
    late = (block >= contexts).astype(jnp.int32)
    device = jnp.where(block < contexts, block, 2 * contexts - 1 - block)
    lines = contexts // 2
    behind = own // 2 - device // 2
    behind = jnp.where(behind < 0, behind + lines, behind)
    return (((own + device) % 2) * lines + behind) * 2 + late


def attention_forward_kernel(starts_ref, own_ref, q_ref, kv_ref, o_ref, lse_ref, s_ref):
    blocks, half_rows, _ = kv_ref.shape
    contexts = blocks // 2
    ratio = q_ref.shape[1] // HEAD_DIM
    rows = ratio * half_rows
    scale = HEAD_DIM ** (-0.5)
    for half in range(2):
        block = own_ref[0] if half == 0 else blocks - 1 - own_ref[0]
        queries = jnp.concatenate(
            [
                q_ref[half * half_rows : (half + 1) * half_rows, h * HEAD_DIM : (h + 1) * HEAD_DIM]
                for h in range(ratio)
            ],
            axis=0,
        )
        low = block_bounds(starts_ref, block, half_rows)
        first, position = attention_masks(starts_ref, block, half_rows, (rows, half_rows))
        column = lax.broadcasted_iota(jnp.int32, (rows, half_rows), 1)

        trips = (block - low + TOGETHER) // TOGETHER

        def score_step(trip, running):
            for part in range(TOGETHER):
                step = trip * TOGETHER + part
                place = block_place(jnp.minimum(low + step, block), own_ref[0], contexts)
                scores = dot32(queries, kv_ref[place, :, :HEAD_DIM], ((1,), (1,))) * scale
                at = column + (low + step) * half_rows
                scores = jnp.where((at >= first) & (at <= position), scores, large_negative)
                s_ref[step] = scores
                running = jnp.maximum(running, scores)
            return running

        running = lax.fori_loop(
            0, trips, score_step, jnp.full((rows, half_rows), large_negative, jnp.float32)
        )
        row_max = jnp.max(running, axis=1, keepdims=True)

        def sum_step(trip, total):
            for part in range(TOGETHER):
                step = trip * TOGETHER + part
                expo = jnp.exp(s_ref[step] - row_max)
                s_ref[step] = expo
                total = total + expo
            return total

        total = lax.fori_loop(0, trips, sum_step, jnp.zeros((rows, half_rows), jnp.float32))
        row_sum = jnp.sum(total, axis=1, keepdims=True)
        inverse = 1.0 / row_sum

        def value_step(trip, accum):
            for part in range(TOGETHER):
                step = trip * TOGETHER + part
                place = block_place(jnp.minimum(low + step, block), own_ref[0], contexts)
                weights = (s_ref[step] * inverse).astype(jnp.bfloat16)
                accum = accum + dot32(weights, kv_ref[place, :, HEAD_DIM:])
            return accum

        accum = lax.fori_loop(0, trips, value_step, jnp.zeros((rows, HEAD_DIM), jnp.float32))
        log_sum = row_max + jnp.log(row_sum)
        lse_ref[0, half] = jnp.broadcast_to(log_sum, (rows, half_rows))
        for h in range(ratio):
            o_ref[half * half_rows : (half + 1) * half_rows, h * HEAD_DIM : (h + 1) * HEAD_DIM] = (
                accum[h * half_rows : (h + 1) * half_rows].astype(jnp.bfloat16)
            )


def attention_forward(starts, own, queries, kv):
    rows, width = queries.shape
    blocks, half_rows, _ = kv.shape
    ratio = QUERY_HEADS // KEY_VALUE_HEADS
    stacked = ratio * half_rows
    kv_spec = pl.BlockSpec((blocks, half_rows, 2 * HEAD_DIM), lambda g, *_: (0, 0, g))
    q_spec = pl.BlockSpec((rows, ratio * HEAD_DIM), lambda g, *_: (0, g))
    return pl.pallas_call(
        attention_forward_kernel,
        grid_spec=pltpu.PrefetchScalarGridSpec(
            num_scalar_prefetch=2,
            grid=(KEY_VALUE_HEADS,),
            in_specs=[q_spec, kv_spec],
            out_specs=[
                q_spec,
                pl.BlockSpec((1, 2, stacked, half_rows), lambda g, *_: (g, 0, 0, 0)),
            ],
            scratch_shapes=[pltpu.VMEM((blocks + TOGETHER - 1, stacked, half_rows), jnp.float32)],
        ),
        out_shape=(
            jax.ShapeDtypeStruct((rows, width), jnp.bfloat16),
            jax.ShapeDtypeStruct((KEY_VALUE_HEADS, 2, stacked, half_rows), jnp.float32),
        ),
        compiler_params=pltpu.CompilerParams(vmem_limit_bytes=48 << 20),
        cost_estimate=pl.CostEstimate(flops=0, bytes_accessed=1 << 20, transcendentals=0),
        name="attention_forward",
    )(starts, own, queries, kv)


def attention_backward_kernel(
    starts_ref, own_ref, q_ref, do_ref, kv_ref, lse_ref, dq_ref, keep_ref, send_ref, p_ref, dp_ref, dka_ref, dva_ref
):
    blocks, half_rows, _ = kv_ref.shape
    contexts = blocks // 2
    ratio = q_ref.shape[1] // HEAD_DIM
    rows = ratio * half_rows
    scale = HEAD_DIM ** (-0.5)
    dka_ref[...] = jnp.zeros_like(dka_ref)
    dva_ref[...] = jnp.zeros_like(dva_ref)

    def stack(ref, half):
        return jnp.concatenate(
            [
                ref[half * half_rows : (half + 1) * half_rows, h * HEAD_DIM : (h + 1) * HEAD_DIM]
                for h in range(ratio)
            ],
            axis=0,
        )

    for half in range(2):
        block = own_ref[0] if half == 0 else blocks - 1 - own_ref[0]
        queries = stack(q_ref, half)
        grads = stack(do_ref, half)
        log_sum = lse_ref[0, half]
        low = block_bounds(starts_ref, block, half_rows)
        first, position = attention_masks(starts_ref, block, half_rows, (rows, half_rows))
        column = lax.broadcasted_iota(jnp.int32, (rows, half_rows), 1)

        trips = (block - low + TOGETHER) // TOGETHER

        def prob_step(trip, running):
            for part in range(TOGETHER):
                step = trip * TOGETHER + part
                place = block_place(jnp.minimum(low + step, block), own_ref[0], contexts)
                scores = dot32(queries, kv_ref[place, :, :HEAD_DIM], ((1,), (1,))) * scale
                at = column + (low + step) * half_rows
                probs = jnp.where(
                    (at >= first) & (at <= position), jnp.exp(scores - log_sum), 0.0
                )
                prob_grads = dot32(grads, kv_ref[place, :, HEAD_DIM:], ((1,), (1,)))
                p_ref[step] = probs
                dp_ref[step] = prob_grads
                running = running + probs * prob_grads
            return running

        running = lax.fori_loop(0, trips, prob_step, jnp.zeros((rows, half_rows), jnp.float32))
        delta = jnp.sum(running, axis=1, keepdims=True)

        def grad_step(trip, query_grad):
            for part in range(TOGETHER):
                step = trip * TOGETHER + part
                place = block_place(jnp.minimum(low + step, block), own_ref[0], contexts)
                probs = p_ref[step]
                score_low = (probs * (dp_ref[step] - delta)).astype(jnp.bfloat16)
                dka_ref[place] += dot32(score_low, queries, ((0,), (0,)))
                dva_ref[place] += dot32(probs.astype(jnp.bfloat16), grads, ((0,), (0,)))
                query_grad = query_grad + dot32(score_low, kv_ref[place, :, :HEAD_DIM])
            return query_grad

        query_grad = lax.fori_loop(0, trips, grad_step, jnp.zeros((rows, HEAD_DIM), jnp.float32))
        for h in range(ratio):
            dq_ref[half * half_rows : (half + 1) * half_rows, h * HEAD_DIM : (h + 1) * HEAD_DIM] = (
                query_grad[h * half_rows : (h + 1) * half_rows] * scale
            ).astype(jnp.bfloat16)
    for out_ref, places in ((keep_ref, slice(0, contexts)), (send_ref, slice(contexts, blocks))):
        out_ref[:, :, :HEAD_DIM] = (dka_ref[places] * scale).astype(jnp.bfloat16)
        out_ref[:, :, HEAD_DIM:] = dva_ref[places].astype(jnp.bfloat16)


def attention_backward(starts, own, queries, grads, kv, log_sums):
    rows, width = queries.shape
    blocks, half_rows, kv_width = kv.shape
    ratio = QUERY_HEADS // KEY_VALUE_HEADS
    stacked = ratio * half_rows
    kv_spec = pl.BlockSpec((blocks, half_rows, 2 * HEAD_DIM), lambda g, *_: (0, 0, g))
    part_spec = pl.BlockSpec((blocks // 2, half_rows, 2 * HEAD_DIM), lambda g, *_: (0, 0, g))
    q_spec = pl.BlockSpec((rows, ratio * HEAD_DIM), lambda g, *_: (0, g))
    return pl.pallas_call(
        attention_backward_kernel,
        grid_spec=pltpu.PrefetchScalarGridSpec(
            num_scalar_prefetch=2,
            grid=(KEY_VALUE_HEADS,),
            in_specs=[
                q_spec,
                q_spec,
                kv_spec,
                pl.BlockSpec((1, 2, stacked, half_rows), lambda g, *_: (g, 0, 0, 0)),
            ],
            out_specs=[q_spec, part_spec, part_spec],
            scratch_shapes=[
                pltpu.VMEM((blocks + TOGETHER - 1, stacked, half_rows), jnp.float32),
                pltpu.VMEM((blocks + TOGETHER - 1, stacked, half_rows), jnp.float32),
                pltpu.VMEM((blocks, half_rows, HEAD_DIM), jnp.float32),
                pltpu.VMEM((blocks, half_rows, HEAD_DIM), jnp.float32),
            ],
        ),
        out_shape=(
            jax.ShapeDtypeStruct((rows, width), jnp.bfloat16),
            jax.ShapeDtypeStruct((blocks // 2, half_rows, kv_width), jnp.bfloat16),
            jax.ShapeDtypeStruct((blocks // 2, half_rows, kv_width), jnp.bfloat16),
        ),
        compiler_params=pltpu.CompilerParams(vmem_limit_bytes=58 << 20),
        cost_estimate=pl.CostEstimate(flops=0, bytes_accessed=1 << 20, transcendentals=0),
        name="attention_backward",
    )(starts, own, queries, grads, kv, log_sums)


def experts_kernel(final, *refs):
    at_ref, *refs = refs
    parts, refs = refs[:8], refs[8:]
    g_ref, wg_ref, wu_ref, wd_ref, *refs = refs
    if final:
        shared_ref, out_in, dx_in, dg_in, *refs = refs
        out_hbm, dx_hbm, out_low_ref, dx_low_ref, dg_ref, *refs = refs
        targets = tuple((refs[0].at[:, number], refs[1].at[:, number]) for number in range(2))
        pair_target, refs = (refs[2], refs[3]), refs[4:]
        x_ref, dy_ref, he_ref, da_ref, db_ref, out_ref, dx_ref, sem = refs
    else:
        out_hbm, dx_hbm, dg_ref, line_hbm, *refs = refs
        x_ref, dy_ref, he_ref, da_ref, db_ref, out_ref, dx_ref, line_ref, sem = refs[2:]
        targets = (line_ref, (refs[0], refs[1]))
        line_copy = pltpu.make_async_copy(line_ref, line_hbm, sem.at[19])
    local = pl.program_id(0)
    expert = at_ref[0] + local
    side = at_ref[1]
    total_rows, width = x_ref.shape
    half = total_rows // 2
    step_rows = total_rows // 4
    tall = 384

    def loads(number):
        rows = pl.ds(number * step_rows, step_rows)
        moves = [(parts[number], x_ref.at[rows, :]), (parts[4 + number], dy_ref.at[rows, :])]
        if final:
            moves += [(out_in.at[rows, :], out_ref.at[rows, :]), (dx_in.at[rows, :], dx_ref.at[rows, :])]
            if number == 0:
                moves.append((dg_in, dg_ref))
        return [
            pltpu.make_async_copy(source, target, sem.at[number * 5 + place])
            for place, (source, target) in enumerate(moves)
        ]

    def results(number, count):
        rows = pl.ds(number * count, count)
        return [
            pltpu.make_async_copy(ref.at[rows, :], hbm.at[rows, :], sem.at[number * 2 + place])
            for place, (ref, hbm) in enumerate(((out_ref, out_hbm), (dx_ref, dx_hbm)))
        ]

    @pl.when(local == 0)
    def _():
        for number in range(4):
            for copy in loads(number):
                copy.start()
        if not final:
            for ref in (out_ref, dx_ref, dg_ref):
                ref[...] = jnp.zeros_like(ref)

    def add(number, rows, value):
        (out_ref, dx_ref)[number][rows, :] += value

    def store_sides(lows, begin, pair):
        per = pair[0].shape[2]
        for parity in range(2):

            @pl.when(side == parity)
            def _():
                for part in range(tall // per):
                    line = begin // (2 * per) + part // 2
                    for number, low in enumerate(lows):
                        pair[(part + parity) % 2][line, number] = low[part * per : (part + 1) * per]

    def store_lines(lows, begin, target):
        per = target.shape[3]
        for part in range(tall // per):
            line = begin // (2 * per) + part // 2
            for number, low in enumerate(lows):
                target[line, (side + part) % 2, number] = low[part * per : (part + 1) * per]

    for number in range(4):
        rows = slice(number * step_rows, (number + 1) * step_rows)

        @pl.when(local == 0)
        def _():
            for copy in loads(number):
                copy.wait()

        x = x_ref[rows, :]
        lane = lax.broadcasted_iota(jnp.int32, (step_rows, g_ref.shape[1]), 1)
        mine = lane == expert
        gate = jnp.sum(jnp.where(mine, g_ref[rows, :], 0.0), axis=1, keepdims=True)
        pre = dot32(x, wg_ref[0])
        up = dot32(x, wu_ref[0])
        back = dot32(dy_ref[rows, :], wd_ref[0], ((1,), (1,)))
        silu, slope = silu_parts(pre)
        hidden = (silu * up).astype(jnp.bfloat16).astype(jnp.float32)
        dg_ref[rows, :] += jnp.where(mine, jnp.sum(hidden * back, axis=1, keepdims=True), 0.0)
        hidden_low = (gate * hidden).astype(jnp.bfloat16)
        he_ref[rows, :] = hidden_low
        add(0, rows, dot32(hidden_low, wd_ref[0]))
        back = gate * back
        pre_low = (back * up * slope).astype(jnp.bfloat16)
        up_low = (back * silu).astype(jnp.bfloat16)
        da_ref[rows, :] = pre_low
        db_ref[rows, :] = up_low
        add(1, rows, dot32(pre_low, wg_ref[0], ((1,), (1,))) + dot32(up_low, wu_ref[0], ((1,), (1,))))
        if not final:

            @pl.when(local == 1)
            def _():
                for copy in results(number, step_rows):
                    copy.start()

    @pl.loop(0, width // tall)
    def _(step):
        begin = pl.multiple_of(step * tall, tall)
        columns = pl.ds(begin, tall)
        lows = [
            dot32(left[:, columns], right[...], ((0,), (0,))).astype(jnp.bfloat16)
            for left, right in ((x_ref, da_ref), (x_ref, db_ref), (dy_ref, he_ref))
        ]
        for number, target in enumerate(targets):

            @pl.when(local == number)
            def _():
                if isinstance(target, tuple):
                    store_sides(lows, begin, target)
                else:
                    store_lines(lows, begin, target)

    if not final:

        @pl.when(local == 0)
        def _():
            line_copy.start()

        @pl.when(local == 1)
        def _():
            line_copy.wait()
            for number in range(4):
                for copy in results(number, step_rows):
                    copy.wait()

        return

    @pl.when(local == pl.num_programs(0) - 1)
    def _():
        shared = shared_ref.shape[1] // 3
        pair_w, down_w = slice(0, 2 * shared), slice(2 * shared, 3 * shared)
        for begin in range(0, total_rows, step_rows):
            rows = slice(begin, begin + step_rows)
            both = dot32(x_ref[rows, :], shared_ref[:, pair_w])
            pre, up = both[:, :shared], both[:, shared:]
            silu, slope = silu_parts(pre)
            hidden = (silu * up).astype(jnp.bfloat16)
            he_ref[rows, :shared] = hidden
            add(0, rows, dot32(hidden, shared_ref[:, down_w], ((1,), (1,))))
            back = dot32(dy_ref[rows, :], shared_ref[:, down_w])
            da_ref[rows, :shared] = (back * up * slope).astype(jnp.bfloat16)
            da_ref[rows, shared:] = (back * silu).astype(jnp.bfloat16)
            add(1, rows, dot32(da_ref[rows, :], shared_ref[:, pair_w], ((1,), (1,))))
        for copy in results(0, half):
            copy.start()
        out_low_ref[...] = out_ref[half:, :].astype(jnp.bfloat16)
        dx_low_ref[...] = dx_ref[half:, :].astype(jnp.bfloat16)

        @pl.loop(0, width // tall)
        def _(step):
            begin = pl.multiple_of(step * tall, tall)
            columns = pl.ds(begin, tall)
            pair_low = dot32(x_ref[:, columns], da_ref[...], ((0,), (0,))).astype(jnp.bfloat16)
            down_low = dot32(dy_ref[:, columns], he_ref[:, :shared], ((0,), (0,))).astype(jnp.bfloat16)
            store_sides((pair_low[:, :shared], pair_low[:, shared:], down_low), begin, pair_target)

        for copy in results(0, half):
            copy.wait()


def experts_call(at, x, dy, gates, weights, first, contexts, shared_w=None, carried=()):
    final = shared_w is not None
    gate_w, up_w, down_w = weights
    rows, width = 4 * x[0].shape[0], x[0].shape[1]
    hidden = gate_w.shape[2]
    per, lines, half = width // contexts, contexts // 2, rows // 2
    once = pl.Buffered(1)
    whole = lambda shape: pl.BlockSpec(shape, lambda e, *_: (0,) * len(shape), pipeline_mode=once)
    weight = lambda shape: pl.BlockSpec((1,) + shape, lambda e, *_: (first + e, 0, 0))
    apart = pl.BlockSpec(memory_space=pl.ANY)
    part = jax.ShapeDtypeStruct((half, width), jnp.float32)
    low = jax.ShapeDtypeStruct((half, width), jnp.bfloat16)
    full = jax.ShapeDtypeStruct((rows, width), jnp.float32)
    table = jax.ShapeDtypeStruct((rows, EXPERTS), jnp.float32)
    term = jax.ShapeDtypeStruct((lines, 3, per, hidden), jnp.bfloat16)
    both = jax.ShapeDtypeStruct((lines, 2, 3, per, hidden), jnp.bfloat16)
    scratch = [pltpu.VMEM((rows, width), jnp.bfloat16)] * 2 + [pltpu.VMEM((rows, hidden), jnp.bfloat16)] * 3
    scratch += [pltpu.VMEM((rows, width), jnp.float32)] * 2
    if final:
        shared = shared_w.shape[1] // 3
        pair = jax.ShapeDtypeStruct((lines, 3, per, shared), jnp.bfloat16)
        extra_specs = [whole(shared_w.shape)] + [apart] * 3
        out_shape = (part, part, low, low, table, both, both, pair, pair)
        outside = (0, 1)
    else:
        shared = 0
        extra_specs = []
        out_shape = (full, full, table, both, term, term)
        outside = (0, 1, 3)
        scratch.append(pltpu.VMEM(both.shape, jnp.bfloat16))
    return pl.pallas_call(
        functools.partial(experts_kernel, final),
        grid_spec=pltpu.PrefetchScalarGridSpec(
            num_scalar_prefetch=1,
            grid=(2,),
            in_specs=[apart] * 8
            + [
                whole((rows, EXPERTS)),
                weight((width, hidden)),
                weight((width, hidden)),
                weight((hidden, width)),
            ]
            + extra_specs,
            out_specs=[apart if place in outside else whole(item.shape) for place, item in enumerate(out_shape)],
            scratch_shapes=scratch + [pltpu.SemaphoreType.DMA((20,))],
        ),
        out_shape=out_shape,
        compiler_params=pltpu.CompilerParams(vmem_limit_bytes=60 << 20),
        cost_estimate=pl.CostEstimate(flops=0, bytes_accessed=1 << 20, transcendentals=0),
        name="experts_final" if final else "experts",
    )(at, *x, *dy, gates, gate_w, up_w, down_w, *((shared_w,) if final else ()), *carried)


def dense_gates(logits, routes):
    chosen = jnp.any(
        routes[:, :, None] == jnp.arange(EXPERTS, dtype=jnp.int32)[None, None, :], axis=1
    )
    top = jnp.max(jnp.where(chosen, logits, large_negative), axis=-1, keepdims=True)
    expo = jnp.where(chosen, jnp.exp(logits - top), 0.0)
    return expo / jnp.sum(expo, axis=-1, keepdims=True)


def shards(
    tokens, doc_starts, routes, norm_gain_1, query_weight, key_matrix, value_matrix, out_weight,
    norm_gain_2, router_weight, shared_gate, shared_up, shared_down, expert_gate, expert_up,
    expert_down, out_grad,
):
    contexts, members = lax.axis_size("ctx"), lax.axis_size("wa")
    context, member = lax.axis_index("ctx"), lax.axis_index("wa")
    half_rows, width = tokens.shape[3], tokens.shape[4]
    rows = 2 * half_rows
    share = width // members
    each = share // contexts
    lines = contexts // 2
    kv_width = 2 * key_matrix.shape[1]
    starts = doc_starts[0]
    own = context[None].astype(jnp.int32)
    inputs = tokens.reshape(rows, width).astype(jnp.float32)
    grad_low = out_grad.reshape(rows, width)
    grad_rows = grad_low.astype(jnp.float32)

    beside = lambda k, v: jnp.stack(
        [k.reshape(-1, KEY_VALUE_HEADS, HEAD_DIM), v.reshape(-1, KEY_VALUE_HEADS, HEAD_DIM)], axis=2
    ).reshape(-1, kv_width)
    apart = lambda kv: jnp.moveaxis(
        kv.reshape(-1, KEY_VALUE_HEADS, 2, HEAD_DIM), 2, 0
    ).reshape(2, -1, kv_width // 2)
    small = jnp.concatenate([router_weight, norm_gain_1[:, None], norm_gain_2[:, None]], axis=1)
    small = jnp.pad(small, ((0, 0), (0, 128 - EXPERTS - 2)))
    kv_pieces = gather_pieces(jnp.concatenate([beside(key_matrix, value_matrix), small], axis=1))
    kv_across = kv_pieces[1]
    kv_full = ordered(kv_pieces, member)
    router_full = kv_full[:, kv_width : kv_width + EXPERTS]
    gain_one = kv_full[:, kv_width + EXPERTS].astype(jnp.float32)
    gain_two = kv_full[:, kv_width + EXPERTS + 1].astype(jnp.float32)
    kv_full = kv_full[:, :kv_width]
    query_full = lax.all_gather(after(query_weight, kv_across), "wa", axis=0, tiled=True)
    out_full = lax.all_gather(after(out_weight, kv_across), "wa", axis=0, tiled=False)

    inverse_one = lax.rsqrt(jnp.mean(inputs * inputs, axis=-1, keepdims=True) + epsilon)
    normed_one = inputs * inverse_one
    normed_low = (normed_one * gain_one).astype(jnp.bfloat16)
    kv_own = dot32(normed_low, kv_full).astype(jnp.bfloat16).reshape(2, half_rows, kv_width)
    ring, other = [kv_own], []
    for step in range(lines - 1):
        ring.append(shift(after(ring[-1], *other), 1))
        other.append(flip(ring[step], "ctx", 1))
    other.append(flip(ring[-1], "ctx", 1))
    kv_all = jnp.concatenate(ring + other, axis=0)
    queries = dot32(normed_low, query_full).astype(jnp.bfloat16)

    hidden_share = shared_gate.shape[1] // members
    routes_all = jnp.concatenate(gather_pieces(after(routes.reshape(rows, TOP), ring[1])), axis=0)
    grad_pieces = gather_pieces(after(grad_low, ring[1]))
    queries = after(queries, routes_all)
    shared_w = jnp.concatenate(
        [
            shared_gate.reshape(share, members, hidden_share),
            shared_up.reshape(share, members, hidden_share),
            shared_down.T.reshape(share, members, hidden_share),
        ],
        axis=2,
    ).transpose(1, 0, 2)
    shared_w = lax.all_to_all(after(shared_w, ring[-1]), "wa", 0, 0, tiled=True)
    shared_w = shared_w.reshape(width, 3 * hidden_share)
    by_share = lambda value: value.reshape(rows, contexts, members, each).transpose(2, 0, 1, 3).reshape(
        members, rows, share
    )

    attended, log_sums = attention_forward(starts, own, queries, kv_all)
    mixed = jnp.concatenate([dot32(attended, out_full[m]) for m in range(members)], axis=1)
    residual = inputs + mixed
    inverse_two = lax.rsqrt(jnp.mean(residual * residual, axis=-1, keepdims=True) + epsilon)
    normed_two = residual * inverse_two
    second_low = after((normed_two * gain_two).astype(jnp.bfloat16), shared_w, *grad_pieces)

    second_pieces = gather_pieces(second_low)
    logits = jnp.concatenate([dot32(piece, router_full) for piece in second_pieces], axis=0)
    gates_all = dense_gates(logits, routes_all)
    attended_across = flip(after(attended, second_pieces[3]), "wa", 2)
    local = expert_gate.shape[0]
    weights = (expert_gate, expert_up, expert_down)
    at = lambda first: jnp.stack([member * local + first, context % 2]).astype(jnp.int32)
    *carried, line_terms, keep_one, send_one = experts_call(
        at(0), second_pieces, grad_pieces, gates_all, weights, 0, contexts
    )
    line_sums = scatter_lines(line_terms)
    other_one = flip(send_one, "ctx", 1)
    (
        out_keep, dx_keep, out_send, dx_send, gate_back,
        keep_both, send_both, pair_keep, pair_send,
    ) = experts_call(
        at(2), second_pieces, grad_pieces, gates_all, weights, 2, contexts, shared_w, carried
    )
    other_both = flip(send_both, "ctx", 1)

    def nothing(arrived):
        return 0.0 * arrived[(0,) * arrived.ndim].astype(jnp.float32)

    def side_sum(keep, received):
        return keep.astype(jnp.float32) + received.astype(jnp.float32)

    dx_near = dx_keep + flip(after(dx_send, other_one, attended_across), "wa", 1).astype(jnp.float32)
    dx_moved = flip(dx_near[rows:].astype(jnp.bfloat16), "wa", 2)
    dx_own = dx_near[:rows] + dx_moved.astype(jnp.float32)
    half = 2 * rows
    gate_back = reduce_rows(gate_back[:half], gate_back[half:], jnp.float32)

    gates = gates_all[:rows]
    logit_grad = gates * (gate_back - jnp.sum(gates * gate_back, axis=-1, keepdims=True))
    router_term = lax.dot_general(
        logit_grad, second_low.astype(jnp.float32), (((0,), (0,)), ((), ())), precision=highest
    )
    second_grad = dx_own + jnp.dot(logit_grad, router_full.astype(jnp.float32).T, precision=highest)
    gain_two_term, residual_back = rms_back(second_grad, normed_two, inverse_two, gain_two)
    residual_grad = grad_rows + residual_back
    mix_low = residual_grad.astype(jnp.bfloat16)

    attended_grad = sum(
        dot32(mix_low[:, m * share : (m + 1) * share], out_full[m], ((1,), (1,)))
        for m in range(members)
    ).astype(jnp.bfloat16)
    small_terms = jnp.concatenate([router_term, gain_two_term[None]], axis=0)
    small_terms = jnp.pad(small_terms, ((0, 128 - small_terms.shape[0]), (0, 0)))
    small_terms = small_terms.reshape(-1, contexts, members, each).transpose(2, 0, 1, 3)
    small_terms = small_terms.reshape(members, -1, share).astype(jnp.bfloat16)
    near_one = side_sum(keep_one, after(other_one, dx_moved)) + nothing(line_sums)
    near_one = near_one.astype(jnp.bfloat16)
    sum_one = scatter_lines(near_one)
    attended_grad = after(attended_grad, near_one)
    query_low, kv_keep, kv_send = attention_backward(starts, own, queries, attended_grad, kv_all, log_sums)
    by_line = lambda parts: parts.reshape(lines, rows, kv_width)
    query_across = flip(query_low, "wa", 2)
    bundle = jnp.concatenate([by_share(mix_low), by_share(normed_low), small_terms], axis=1)
    bundle = exchange(after(bundle, query_low), member)
    attended_core = flip(after(jnp.concatenate([attended, attended_across], axis=0), query_low), "wa", 1)
    query_core = flip(jnp.concatenate([query_low, query_across], axis=0), "wa", 1)
    moved = bundle[1:] + [attended_core, query_core]
    kv_send = after(by_line(kv_send), other_both, *moved)
    received = flip(kv_send, "ctx", 1)
    out_near = out_keep + flip(after(out_send, query_core), "wa", 1).astype(jnp.float32)
    out_moved = flip(out_near[rows:].astype(jnp.bfloat16), "wa", 2)
    out_own = out_near[:rows] + out_moved.astype(jnp.float32)
    block_out = (residual + out_own).astype(jnp.bfloat16).reshape(tokens.shape)
    near_both = (side_sum(keep_both, other_both) + nothing(sum_one)).astype(jnp.bfloat16)
    sum_both = scatter_lines(near_both)
    received = after(received, near_both)
    kv_near = by_line(kv_keep).astype(jnp.float32) + received.astype(jnp.float32)
    kv_parts = kv_near.astype(jnp.bfloat16)
    kv_moved = [shift(kv_parts[steps], -steps) for steps in range(1, lines)]
    stacked = lambda pieces: jnp.concatenate(pieces, axis=0)
    mix_share = stacked([piece[:rows] for piece in bundle])
    normed_share = stacked([piece[rows : 2 * rows] for piece in bundle])
    small_share = sum(piece[2 * rows :].astype(jnp.float32) for piece in bundle)
    query_all = stacked([query_low, query_across, query_core])
    attended_all = stacked([attended, attended_across, attended_core])
    early_term = jnp.concatenate(
        [
            dot32(normed_share, query_all, ((0,), (0,))),
            dot32(mix_share, attended_all, ((0,), (0,))),
            small_share.T,
        ],
        axis=1,
    ).astype(jnp.bfloat16)
    early_sides = to_side(after(early_term.reshape(contexts, each, -1), kv_parts), context)
    other_pair = flip(after(pair_send, kv_parts), "ctx", 1)
    kv_moved[0] = after(kv_moved[0], early_sides[1], out_moved)
    kv_low = (kv_near[0] + sum(moved.astype(jnp.float32) for moved in kv_moved)).astype(jnp.bfloat16)

    kv_low_pieces = gather_pieces(kv_low)
    kv_low_all = stacked(kv_low_pieces)
    kv_term = dot32(normed_share, kv_low_all, ((0,), (0,)))
    first_grad = dot32(query_low, query_full, ((1,), (1,))) + dot32(kv_low, kv_full, ((1,), (1,)))
    scaled = first_grad * gain_one
    input_back = inverse_one * (
        scaled - normed_one * jnp.mean(scaled * normed_one, axis=-1, keepdims=True)
    )
    tokens_grad = (residual_grad + input_back).astype(jnp.bfloat16).reshape(tokens.shape)
    kv_sides = to_side(kv_term.astype(jnp.bfloat16).reshape(contexts, each, kv_width), context)
    kv_sum = line_sum(side_sum(*kv_sides), context)
    early_near = side_sum(early_sides[0], after(early_sides[1], kv_sides[1])) + nothing(sum_both)
    early_sum = line_sum(early_near, context)
    query_weight_grad, out_sum = early_sum[:, :width], early_sum[:, width:]
    out_weight_grad = out_sum[:, :width].T
    router_weight_grad = out_sum[:, width : width + EXPERTS]
    norm_gain_2_grad = out_sum[:, width + EXPERTS]
    key_weight_grad, value_weight_grad = apart(kv_sum)
    mine = lambda full: lax.dynamic_slice_in_dim(full, (context * members + member) * each, each, 0)
    norm_gain_1_grad = (
        jnp.sum(mine(query_full).astype(jnp.float32) * query_weight_grad, axis=1)
        + jnp.sum(mine(kv_full).astype(jnp.float32) * kv_sum, axis=1)
    ) / mine(gain_one)

    line_zero = flip(after(line_sums[1], kv_low_pieces[1]), "ctx", 1)
    sum_zero = line_sums[0].astype(jnp.float32) + line_zero.astype(jnp.float32)
    expert_sums = [sum_zero, sum_one, sum_both[0], sum_both[1]]
    expert_gate_grad = jnp.stack([total[0] for total in expert_sums]).astype(jnp.float32)
    expert_up_grad = jnp.stack([total[1] for total in expert_sums]).astype(jnp.float32)
    expert_down_grad = jnp.stack([total[2].T for total in expert_sums]).astype(jnp.float32)

    shared_sum = line_sum(side_sum(pair_keep, after(other_pair, *kv_moved)), context)
    shared_sum = shared_sum.reshape(3, members, each, hidden_share).transpose(1, 0, 2, 3)
    shared_sum = lax.all_to_all(shared_sum, "wa", 0, 0, tiled=True)
    shared_gate_grad = shared_sum[:, 0].transpose(1, 0, 2).reshape(each, members * hidden_share)
    shared_up_grad = shared_sum[:, 1].transpose(1, 0, 2).reshape(each, members * hidden_share)
    shared_down_grad = shared_sum[:, 2].transpose(0, 2, 1).reshape(members * hidden_share, each)
    return (
        block_out,
        tokens_grad,
        norm_gain_1_grad,
        query_weight_grad,
        key_weight_grad,
        value_weight_grad,
        out_weight_grad,
        norm_gain_2_grad,
        router_weight_grad,
        shared_gate_grad,
        shared_up_grad,
        shared_down_grad,
        expert_gate_grad,
        expert_up_grad,
        expert_down_grad,
    )


def solution(mesh):
    return jax.shard_map(
        shards,
        mesh=mesh,
        in_specs=(
            P("wa", "ctx", None, None, None),
            P("wa", None),
            P("wa", "ctx", None, None, None),
            P("wa"),
            P("wa", None),
            P("wa", None),
            P("wa", None),
            P(None, "wa"),
            P("wa"),
            P("wa", None),
            P("wa", None),
            P("wa", None),
            P(None, "wa"),
            P("wa", None, None),
            P("wa", None, None),
            P("wa", None, None),
            P("wa", "ctx", None, None, None),
        ),
        out_specs=(
            P("wa", "ctx", None, None, None),
            P("wa", "ctx", None, None, None),
            P(("ctx", "wa")),
            P(("ctx", "wa"), None),
            P(("ctx", "wa"), None),
            P(("ctx", "wa"), None),
            P(None, ("ctx", "wa")),
            P(("ctx", "wa")),
            P(("ctx", "wa"), None),
            P(("ctx", "wa"), None),
            P(("ctx", "wa"), None),
            P(None, ("ctx", "wa")),
            P("wa", "ctx", None),
            P("wa", "ctx", None),
            P("wa", None, "ctx"),
        ),
        check_vma=False,
    )
```

```python
import functools

import jax
import jax.numpy as jnp
from jax import lax
from jax.experimental import pallas as pl
from jax.experimental.pallas import tpu as pltpu
from jax.sharding import PartitionSpec as P

QUERY_HEADS = 12
KEY_VALUE_HEADS = 4
HEAD_DIM = 128
TOP = 6
EXPERTS = 16

epsilon = 1e-05
large_negative = -1e30
highest = lax.Precision.HIGHEST
ORDER = (0, 2, 1, 3)


def dot32(left, right, dims=None):
    if dims is None:
        return jnp.dot(left, right, preferred_element_type=jnp.float32)
    return lax.dot_general(left, right, (dims, ((), ())), preferred_element_type=jnp.float32)


def flip(value, axis, bits):
    count = lax.axis_size(axis)
    return lax.ppermute(value, axis, [(i, i ^ bits) for i in range(count)])


def shift(value, steps):
    count = lax.axis_size("ctx")
    return lax.ppermute(value, "ctx", [(i, (i + 2 * steps) % count) for i in range(count)])


def after(value, *earlier):
    return lax.optimization_barrier((value,) + earlier)[0]


def gather_pieces(value):
    across = flip(value, "wa", 2)
    return [value, across, flip(value, "wa", 1), flip(across, "wa", 1)]


def ordered(pieces, index):
    chip, core = index // 2, index % 2
    near = [jnp.where(core == i, pieces[0], pieces[2]) for i in range(2)]
    far = [jnp.where(core == i, pieces[1], pieces[3]) for i in range(2)]
    return jnp.concatenate(
        [jnp.where(chip == i // 2, near[i % 2], far[i % 2]) for i in range(4)], axis=0
    )


def exchange(pieces, index):
    received = []
    for bits in ORDER:
        piece = lax.dynamic_index_in_dim(pieces, index ^ bits, 0, keepdims=False)
        received.append(piece if bits == 0 else flip(piece, "wa", bits))
    return received


def reduce_rows(keep, send, kind):
    near = keep + flip(send, "wa", 1).astype(jnp.float32)
    quarter = keep.shape[0] // 2
    return near[:quarter] + flip(near[quarter:].astype(kind), "wa", 2).astype(jnp.float32)


def scatter_small(value):
    rows, width = value.shape
    contexts, members = lax.axis_size("ctx"), lax.axis_size("wa")
    each = width // (contexts * members)
    spread = value.reshape(rows, contexts, members, each).transpose(2, 0, 1, 3)
    spread = spread.reshape(members, rows, contexts * each)
    first = jnp.sum(lax.all_to_all(spread, "wa", 0, 0, tiled=True), axis=0)
    second = first.reshape(rows, contexts, each).transpose(1, 0, 2)
    return jnp.sum(lax.all_to_all(second, "ctx", 0, 0, tiled=True), axis=0)


def sides():
    count = lax.axis_size("ctx")
    return [list(range(side, count, 2)) for side in range(2)]


def to_side(value, index):
    pairs = value.reshape((value.shape[0] // 2, 2) + value.shape[1:])
    keep = lax.dynamic_index_in_dim(pairs, index % 2, 1, keepdims=False)
    return keep, flip(lax.dynamic_index_in_dim(pairs, 1 - index % 2, 1, keepdims=False), "ctx", 1)


def line_sum(near, index, *before):
    lines, line = near.shape[0], index // 2
    low = near.astype(jnp.bfloat16)
    total = lax.dynamic_index_in_dim(near, line, 0, keepdims=False)
    for steps in range(1, lines):
        piece = lax.dynamic_index_in_dim(low, (line + lines - steps) % lines, 0, keepdims=False)
        total = total + after(shift(piece, -steps), *before).astype(jnp.float32)
    return total


def scatter_lines(value):
    return lax.psum_scatter(
        value, "ctx", scatter_dimension=0, axis_index_groups=sides(), tiled=True
    )[0]


def silu_parts(values):
    sigmoid_of = jax.nn.sigmoid(values)
    return (values * sigmoid_of, sigmoid_of * (1.0 + values * (1.0 - sigmoid_of)))


def rms_back(grad_normed, normed, inverse, gain_values):
    scaled = grad_normed * gain_values
    return (
        jnp.sum(grad_normed * normed, axis=0),
        inverse * (scaled - normed * jnp.mean(scaled * normed, axis=-1, keepdims=True)),
    )


TOGETHER = 3


def attention_masks(starts_ref, block, half_rows, shape):
    rows = block * half_rows + lax.broadcasted_iota(jnp.int32, shape, 0) % half_rows
    first = jnp.zeros(shape, jnp.int32)
    for document in range(1, starts_ref.shape[0]):
        start = starts_ref[document]
        first = jnp.where(start <= rows, jnp.maximum(first, start), first)
    return first, rows


def block_bounds(starts_ref, block, half_rows):
    top = block * half_rows
    first = jnp.int32(0)
    for document in range(1, starts_ref.shape[0]):
        start = starts_ref[document]
        first = jnp.where(start <= top, jnp.maximum(first, start), first)
    return first // half_rows


def block_place(block, own, contexts):
    late = (block >= contexts).astype(jnp.int32)
    device = jnp.where(block < contexts, block, 2 * contexts - 1 - block)
    lines = contexts // 2
    behind = own // 2 - device // 2
    behind = jnp.where(behind < 0, behind + lines, behind)
    return (((own + device) % 2) * lines + behind) * 2 + late


def attention_forward_kernel(starts_ref, own_ref, q_ref, kv_ref, o_ref, lse_ref, s_ref):
    blocks, half_rows, _ = kv_ref.shape
    contexts = blocks // 2
    ratio = q_ref.shape[1] // HEAD_DIM
    rows = ratio * half_rows
    scale = HEAD_DIM ** (-0.5)
    for half in range(2):
        block = own_ref[0] if half == 0 else blocks - 1 - own_ref[0]
        queries = jnp.concatenate(
            [
                q_ref[half * half_rows : (half + 1) * half_rows, h * HEAD_DIM : (h + 1) * HEAD_DIM]
                for h in range(ratio)
            ],
            axis=0,
        )
        low = block_bounds(starts_ref, block, half_rows)
        first, position = attention_masks(starts_ref, block, half_rows, (rows, half_rows))
        column = lax.broadcasted_iota(jnp.int32, (rows, half_rows), 1)

        trips = (block - low + TOGETHER) // TOGETHER

        def score_step(trip, running):
            for part in range(TOGETHER):
                step = trip * TOGETHER + part
                place = block_place(jnp.minimum(low + step, block), own_ref[0], contexts)
                scores = dot32(queries, kv_ref[place, :, :HEAD_DIM], ((1,), (1,))) * scale
                at = column + (low + step) * half_rows
                scores = jnp.where((at >= first) & (at <= position), scores, large_negative)
                s_ref[step] = scores
                running = jnp.maximum(running, scores)
            return running

        running = lax.fori_loop(
            0, trips, score_step, jnp.full((rows, half_rows), large_negative, jnp.float32)
        )
        row_max = jnp.max(running, axis=1, keepdims=True)

        def sum_step(trip, total):
            for part in range(TOGETHER):
                step = trip * TOGETHER + part
                expo = jnp.exp(s_ref[step] - row_max)
                s_ref[step] = expo
                total = total + expo
            return total

        total = lax.fori_loop(0, trips, sum_step, jnp.zeros((rows, half_rows), jnp.float32))
        row_sum = jnp.sum(total, axis=1, keepdims=True)
        inverse = 1.0 / row_sum

        def value_step(trip, accum):
            for part in range(TOGETHER):
                step = trip * TOGETHER + part
                place = block_place(jnp.minimum(low + step, block), own_ref[0], contexts)
                weights = (s_ref[step] * inverse).astype(jnp.bfloat16)
                accum = accum + dot32(weights, kv_ref[place, :, HEAD_DIM:])
            return accum

        accum = lax.fori_loop(0, trips, value_step, jnp.zeros((rows, HEAD_DIM), jnp.float32))
        log_sum = row_max + jnp.log(row_sum)
        lse_ref[0, half] = jnp.broadcast_to(log_sum, (rows, half_rows))
        for h in range(ratio):
            o_ref[half * half_rows : (half + 1) * half_rows, h * HEAD_DIM : (h + 1) * HEAD_DIM] = (
                accum[h * half_rows : (h + 1) * half_rows].astype(jnp.bfloat16)
            )


def attention_forward(starts, own, queries, kv):
    rows, width = queries.shape
    blocks, half_rows, _ = kv.shape
    ratio = QUERY_HEADS // KEY_VALUE_HEADS
    stacked = ratio * half_rows
    kv_spec = pl.BlockSpec((blocks, half_rows, 2 * HEAD_DIM), lambda g, *_: (0, 0, g))
    q_spec = pl.BlockSpec((rows, ratio * HEAD_DIM), lambda g, *_: (0, g))
    return pl.pallas_call(
        attention_forward_kernel,
        grid_spec=pltpu.PrefetchScalarGridSpec(
            num_scalar_prefetch=2,
            grid=(KEY_VALUE_HEADS,),
            in_specs=[q_spec, kv_spec],
            out_specs=[
                q_spec,
                pl.BlockSpec((1, 2, stacked, half_rows), lambda g, *_: (g, 0, 0, 0)),
            ],
            scratch_shapes=[pltpu.VMEM((blocks + TOGETHER - 1, stacked, half_rows), jnp.float32)],
        ),
        out_shape=(
            jax.ShapeDtypeStruct((rows, width), jnp.bfloat16),
            jax.ShapeDtypeStruct((KEY_VALUE_HEADS, 2, stacked, half_rows), jnp.float32),
        ),
        compiler_params=pltpu.CompilerParams(vmem_limit_bytes=48 << 20),
        cost_estimate=pl.CostEstimate(flops=0, bytes_accessed=1 << 20, transcendentals=0),
        name="attention_forward",
    )(starts, own, queries, kv)


def attention_backward_kernel(
    starts_ref, own_ref, q_ref, do_ref, kv_ref, lse_ref, dq_ref, keep_ref, send_ref, p_ref, dp_ref, dka_ref, dva_ref
):
    blocks, half_rows, _ = kv_ref.shape
    contexts = blocks // 2
    ratio = q_ref.shape[1] // HEAD_DIM
    rows = ratio * half_rows
    scale = HEAD_DIM ** (-0.5)
    dka_ref[...] = jnp.zeros_like(dka_ref)
    dva_ref[...] = jnp.zeros_like(dva_ref)

    def stack(ref, half):
        return jnp.concatenate(
            [
                ref[half * half_rows : (half + 1) * half_rows, h * HEAD_DIM : (h + 1) * HEAD_DIM]
                for h in range(ratio)
            ],
            axis=0,
        )

    for half in range(2):
        block = own_ref[0] if half == 0 else blocks - 1 - own_ref[0]
        queries = stack(q_ref, half)
        grads = stack(do_ref, half)
        log_sum = lse_ref[0, half]
        low = block_bounds(starts_ref, block, half_rows)
        first, position = attention_masks(starts_ref, block, half_rows, (rows, half_rows))
        column = lax.broadcasted_iota(jnp.int32, (rows, half_rows), 1)

        trips = (block - low + TOGETHER) // TOGETHER

        def prob_step(trip, running):
            for part in range(TOGETHER):
                step = trip * TOGETHER + part
                place = block_place(jnp.minimum(low + step, block), own_ref[0], contexts)
                scores = dot32(queries, kv_ref[place, :, :HEAD_DIM], ((1,), (1,))) * scale
                at = column + (low + step) * half_rows
                probs = jnp.where(
                    (at >= first) & (at <= position), jnp.exp(scores - log_sum), 0.0
                )
                prob_grads = dot32(grads, kv_ref[place, :, HEAD_DIM:], ((1,), (1,)))
                p_ref[step] = probs
                dp_ref[step] = prob_grads
                running = running + probs * prob_grads
            return running

        running = lax.fori_loop(0, trips, prob_step, jnp.zeros((rows, half_rows), jnp.float32))
        delta = jnp.sum(running, axis=1, keepdims=True)

        def grad_step(trip, query_grad):
            for part in range(TOGETHER):
                step = trip * TOGETHER + part
                place = block_place(jnp.minimum(low + step, block), own_ref[0], contexts)
                probs = p_ref[step]
                score_low = (probs * (dp_ref[step] - delta)).astype(jnp.bfloat16)
                dka_ref[place] += dot32(score_low, queries, ((0,), (0,)))
                dva_ref[place] += dot32(probs.astype(jnp.bfloat16), grads, ((0,), (0,)))
                query_grad = query_grad + dot32(score_low, kv_ref[place, :, :HEAD_DIM])
            return query_grad

        query_grad = lax.fori_loop(0, trips, grad_step, jnp.zeros((rows, HEAD_DIM), jnp.float32))
        for h in range(ratio):
            dq_ref[half * half_rows : (half + 1) * half_rows, h * HEAD_DIM : (h + 1) * HEAD_DIM] = (
                query_grad[h * half_rows : (h + 1) * half_rows] * scale
            ).astype(jnp.bfloat16)
    for out_ref, places in ((keep_ref, slice(0, contexts)), (send_ref, slice(contexts, blocks))):
        out_ref[:, :, :HEAD_DIM] = (dka_ref[places] * scale).astype(jnp.bfloat16)
        out_ref[:, :, HEAD_DIM:] = dva_ref[places].astype(jnp.bfloat16)


def attention_backward(starts, own, queries, grads, kv, log_sums):
    rows, width = queries.shape
    blocks, half_rows, kv_width = kv.shape
    ratio = QUERY_HEADS // KEY_VALUE_HEADS
    stacked = ratio * half_rows
    kv_spec = pl.BlockSpec((blocks, half_rows, 2 * HEAD_DIM), lambda g, *_: (0, 0, g))
    part_spec = pl.BlockSpec((blocks // 2, half_rows, 2 * HEAD_DIM), lambda g, *_: (0, 0, g))
    q_spec = pl.BlockSpec((rows, ratio * HEAD_DIM), lambda g, *_: (0, g))
    return pl.pallas_call(
        attention_backward_kernel,
        grid_spec=pltpu.PrefetchScalarGridSpec(
            num_scalar_prefetch=2,
            grid=(KEY_VALUE_HEADS,),
            in_specs=[
                q_spec,
                q_spec,
                kv_spec,
                pl.BlockSpec((1, 2, stacked, half_rows), lambda g, *_: (g, 0, 0, 0)),
            ],
            out_specs=[q_spec, part_spec, part_spec],
            scratch_shapes=[
                pltpu.VMEM((blocks + TOGETHER - 1, stacked, half_rows), jnp.float32),
                pltpu.VMEM((blocks + TOGETHER - 1, stacked, half_rows), jnp.float32),
                pltpu.VMEM((blocks, half_rows, HEAD_DIM), jnp.float32),
                pltpu.VMEM((blocks, half_rows, HEAD_DIM), jnp.float32),
            ],
        ),
        out_shape=(
            jax.ShapeDtypeStruct((rows, width), jnp.bfloat16),
            jax.ShapeDtypeStruct((blocks // 2, half_rows, kv_width), jnp.bfloat16),
            jax.ShapeDtypeStruct((blocks // 2, half_rows, kv_width), jnp.bfloat16),
        ),
        compiler_params=pltpu.CompilerParams(vmem_limit_bytes=58 << 20),
        cost_estimate=pl.CostEstimate(flops=0, bytes_accessed=1 << 20, transcendentals=0),
        name="attention_backward",
    )(starts, own, queries, grads, kv, log_sums)


def experts_kernel(final, *refs):
    at_ref, *refs = refs
    parts, refs = refs[:8], refs[8:]
    g_ref, wg_ref, wu_ref, wd_ref, *refs = refs
    if final:
        shared_ref, out_in, dx_in, dg_in, *refs = refs
        out_hbm, dx_hbm, out_low_ref, dx_low_ref, dg_ref, *refs = refs
        targets = tuple((refs[0].at[:, number], refs[1].at[:, number]) for number in range(2))
        pair_target, refs = (refs[2], refs[3]), refs[4:]
        x_ref, dy_ref, he_ref, da_ref, db_ref, out_ref, dx_ref, sem = refs
    else:
        out_hbm, dx_hbm, dg_ref, line_hbm, *refs = refs
        x_ref, dy_ref, he_ref, da_ref, db_ref, out_ref, dx_ref, line_ref, sem = refs[2:]
        targets = (line_ref, (refs[0], refs[1]))
        line_copy = pltpu.make_async_copy(line_ref, line_hbm, sem.at[19])
    local = pl.program_id(0)
    expert = at_ref[0] + local
    side = at_ref[1]
    total_rows, width = x_ref.shape
    half = total_rows // 2
    step_rows = total_rows // 4
    tall = 384

    def loads(number):
        rows = pl.ds(number * step_rows, step_rows)
        moves = [(parts[number], x_ref.at[rows, :]), (parts[4 + number], dy_ref.at[rows, :])]
        if final:
            moves += [(out_in.at[rows, :], out_ref.at[rows, :]), (dx_in.at[rows, :], dx_ref.at[rows, :])]
            if number == 0:
                moves.append((dg_in, dg_ref))
        return [
            pltpu.make_async_copy(source, target, sem.at[number * 5 + place])
            for place, (source, target) in enumerate(moves)
        ]

    def results(number, count):
        rows = pl.ds(number * count, count)
        return [
            pltpu.make_async_copy(ref.at[rows, :], hbm.at[rows, :], sem.at[number * 2 + place])
            for place, (ref, hbm) in enumerate(((out_ref, out_hbm), (dx_ref, dx_hbm)))
        ]

    @pl.when(local == 0)
    def _():
        for number in range(4):
            for copy in loads(number):
                copy.start()
        if not final:
            for ref in (out_ref, dx_ref, dg_ref):
                ref[...] = jnp.zeros_like(ref)

    def add(number, rows, value):
        (out_ref, dx_ref)[number][rows, :] += value

    def store_sides(lows, begin, pair):
        per = pair[0].shape[2]
        for parity in range(2):

            @pl.when(side == parity)
            def _():
                for part in range(tall // per):
                    line = begin // (2 * per) + part // 2
                    for number, low in enumerate(lows):
                        pair[(part + parity) % 2][line, number] = low[part * per : (part + 1) * per]

    def store_lines(lows, begin, target):
        per = target.shape[3]
        for part in range(tall // per):
            line = begin // (2 * per) + part // 2
            for number, low in enumerate(lows):
                target[line, (side + part) % 2, number] = low[part * per : (part + 1) * per]

    for number in range(4):
        rows = slice(number * step_rows, (number + 1) * step_rows)

        @pl.when(local == 0)
        def _():
            for copy in loads(number):
                copy.wait()

        x = x_ref[rows, :]
        lane = lax.broadcasted_iota(jnp.int32, (step_rows, g_ref.shape[1]), 1)
        mine = lane == expert
        gate = jnp.sum(jnp.where(mine, g_ref[rows, :], 0.0), axis=1, keepdims=True)
        pre = dot32(x, wg_ref[0])
        up = dot32(x, wu_ref[0])
        back = dot32(dy_ref[rows, :], wd_ref[0], ((1,), (1,)))
        silu, slope = silu_parts(pre)
        hidden = (silu * up).astype(jnp.bfloat16).astype(jnp.float32)
        dg_ref[rows, :] += jnp.where(mine, jnp.sum(hidden * back, axis=1, keepdims=True), 0.0)
        hidden_low = (gate * hidden).astype(jnp.bfloat16)
        he_ref[rows, :] = hidden_low
        add(0, rows, dot32(hidden_low, wd_ref[0]))
        back = gate * back
        pre_low = (back * up * slope).astype(jnp.bfloat16)
        up_low = (back * silu).astype(jnp.bfloat16)
        da_ref[rows, :] = pre_low
        db_ref[rows, :] = up_low
        add(1, rows, dot32(pre_low, wg_ref[0], ((1,), (1,))) + dot32(up_low, wu_ref[0], ((1,), (1,))))
        if not final:

            @pl.when(local == 1)
            def _():
                for copy in results(number, step_rows):
                    copy.start()

    @pl.loop(0, width // tall)
    def _(step):
        begin = pl.multiple_of(step * tall, tall)
        columns = pl.ds(begin, tall)
        lows = [
            dot32(left[:, columns], right[...], ((0,), (0,))).astype(jnp.bfloat16)
            for left, right in ((x_ref, da_ref), (x_ref, db_ref), (dy_ref, he_ref))
        ]
        for number, target in enumerate(targets):

            @pl.when(local == number)
            def _():
                if isinstance(target, tuple):
                    store_sides(lows, begin, target)
                else:
                    store_lines(lows, begin, target)

    if not final:

        @pl.when(local == 0)
        def _():
            line_copy.start()

        @pl.when(local == 1)
        def _():
            line_copy.wait()
            for number in range(4):
                for copy in results(number, step_rows):
                    copy.wait()

        return

    @pl.when(local == pl.num_programs(0) - 1)
    def _():
        shared = shared_ref.shape[1] // 3
        pair_w, down_w = slice(0, 2 * shared), slice(2 * shared, 3 * shared)
        for begin in range(0, total_rows, step_rows):
            rows = slice(begin, begin + step_rows)
            both = dot32(x_ref[rows, :], shared_ref[:, pair_w])
            pre, up = both[:, :shared], both[:, shared:]
            silu, slope = silu_parts(pre)
            hidden = (silu * up).astype(jnp.bfloat16)
            he_ref[rows, :shared] = hidden
            add(0, rows, dot32(hidden, shared_ref[:, down_w], ((1,), (1,))))
            back = dot32(dy_ref[rows, :], shared_ref[:, down_w])
            da_ref[rows, :shared] = (back * up * slope).astype(jnp.bfloat16)
            da_ref[rows, shared:] = (back * silu).astype(jnp.bfloat16)
            add(1, rows, dot32(da_ref[rows, :], shared_ref[:, pair_w], ((1,), (1,))))
        for copy in results(0, half):
            copy.start()
        out_low_ref[...] = out_ref[half:, :].astype(jnp.bfloat16)
        dx_low_ref[...] = dx_ref[half:, :].astype(jnp.bfloat16)

        @pl.loop(0, width // tall)
        def _(step):
            begin = pl.multiple_of(step * tall, tall)
            columns = pl.ds(begin, tall)
            pair_low = dot32(x_ref[:, columns], da_ref[...], ((0,), (0,))).astype(jnp.bfloat16)
            down_low = dot32(dy_ref[:, columns], he_ref[:, :shared], ((0,), (0,))).astype(jnp.bfloat16)
            store_sides((pair_low[:, :shared], pair_low[:, shared:], down_low), begin, pair_target)

        for copy in results(0, half):
            copy.wait()


def experts_call(at, x, dy, gates, weights, first, contexts, shared_w=None, carried=()):
    final = shared_w is not None
    gate_w, up_w, down_w = weights
    rows, width = 4 * x[0].shape[0], x[0].shape[1]
    hidden = gate_w.shape[2]
    per, lines, half = width // contexts, contexts // 2, rows // 2
    once = pl.Buffered(1)
    whole = lambda shape: pl.BlockSpec(shape, lambda e, *_: (0,) * len(shape), pipeline_mode=once)
    weight = lambda shape: pl.BlockSpec((1,) + shape, lambda e, *_: (first + e, 0, 0))
    apart = pl.BlockSpec(memory_space=pl.ANY)
    part = jax.ShapeDtypeStruct((half, width), jnp.float32)
    low = jax.ShapeDtypeStruct((half, width), jnp.bfloat16)
    full = jax.ShapeDtypeStruct((rows, width), jnp.float32)
    table = jax.ShapeDtypeStruct((rows, EXPERTS), jnp.float32)
    term = jax.ShapeDtypeStruct((lines, 3, per, hidden), jnp.bfloat16)
    both = jax.ShapeDtypeStruct((lines, 2, 3, per, hidden), jnp.bfloat16)
    scratch = [pltpu.VMEM((rows, width), jnp.bfloat16)] * 2 + [pltpu.VMEM((rows, hidden), jnp.bfloat16)] * 3
    scratch += [pltpu.VMEM((rows, width), jnp.float32)] * 2
    if final:
        shared = shared_w.shape[1] // 3
        pair = jax.ShapeDtypeStruct((lines, 3, per, shared), jnp.bfloat16)
        extra_specs = [whole(shared_w.shape)] + [apart] * 3
        out_shape = (part, part, low, low, table, both, both, pair, pair)
        outside = (0, 1)
    else:
        shared = 0
        extra_specs = []
        out_shape = (full, full, table, both, term, term)
        outside = (0, 1, 3)
        scratch.append(pltpu.VMEM(both.shape, jnp.bfloat16))
    return pl.pallas_call(
        functools.partial(experts_kernel, final),
        grid_spec=pltpu.PrefetchScalarGridSpec(
            num_scalar_prefetch=1,
            grid=(2,),
            in_specs=[apart] * 8
            + [
                whole((rows, EXPERTS)),
                weight((width, hidden)),
                weight((width, hidden)),
                weight((hidden, width)),
            ]
            + extra_specs,
            out_specs=[apart if place in outside else whole(item.shape) for place, item in enumerate(out_shape)],
            scratch_shapes=scratch + [pltpu.SemaphoreType.DMA((20,))],
        ),
        out_shape=out_shape,
        compiler_params=pltpu.CompilerParams(vmem_limit_bytes=60 << 20),
        cost_estimate=pl.CostEstimate(flops=0, bytes_accessed=1 << 20, transcendentals=0),
        name="experts_final" if final else "experts",
    )(at, *x, *dy, gates, gate_w, up_w, down_w, *((shared_w,) if final else ()), *carried)


def dense_gates(logits, routes):
    chosen = jnp.any(
        routes[:, :, None] == jnp.arange(EXPERTS, dtype=jnp.int32)[None, None, :], axis=1
    )
    top = jnp.max(jnp.where(chosen, logits, large_negative), axis=-1, keepdims=True)
    expo = jnp.where(chosen, jnp.exp(logits - top), 0.0)
    return expo / jnp.sum(expo, axis=-1, keepdims=True)


def shards(
    tokens, doc_starts, routes, norm_gain_1, query_weight, key_matrix, value_matrix, out_weight,
    norm_gain_2, router_weight, shared_gate, shared_up, shared_down, expert_gate, expert_up,
    expert_down, out_grad,
):
    contexts, members = lax.axis_size("ctx"), lax.axis_size("wa")
    context, member = lax.axis_index("ctx"), lax.axis_index("wa")
    half_rows, width = tokens.shape[3], tokens.shape[4]
    rows = 2 * half_rows
    share = width // members
    each = share // contexts
    lines = contexts // 2
    kv_width = 2 * key_matrix.shape[1]
    starts = doc_starts[0]
    own = context[None].astype(jnp.int32)
    inputs = tokens.reshape(rows, width).astype(jnp.float32)
    grad_low = out_grad.reshape(rows, width)
    grad_rows = grad_low.astype(jnp.float32)

    beside = lambda k, v: jnp.stack(
        [k.reshape(-1, KEY_VALUE_HEADS, HEAD_DIM), v.reshape(-1, KEY_VALUE_HEADS, HEAD_DIM)], axis=2
    ).reshape(-1, kv_width)
    apart = lambda kv: jnp.moveaxis(
        kv.reshape(-1, KEY_VALUE_HEADS, 2, HEAD_DIM), 2, 0
    ).reshape(2, -1, kv_width // 2)
    small = jnp.concatenate([router_weight, norm_gain_1[:, None], norm_gain_2[:, None]], axis=1)
    small = jnp.pad(small, ((0, 0), (0, 128 - EXPERTS - 2)))
    kv_pieces = gather_pieces(jnp.concatenate([beside(key_matrix, value_matrix), small], axis=1))
    kv_across = kv_pieces[1]
    kv_full = ordered(kv_pieces, member)
    router_full = kv_full[:, kv_width : kv_width + EXPERTS]
    gain_one = kv_full[:, kv_width + EXPERTS].astype(jnp.float32)
    gain_two = kv_full[:, kv_width + EXPERTS + 1].astype(jnp.float32)
    kv_full = kv_full[:, :kv_width]
    query_full = lax.all_gather(after(query_weight, kv_across), "wa", axis=0, tiled=True)
    out_full = lax.all_gather(after(out_weight, kv_across), "wa", axis=0, tiled=False)

    inverse_one = lax.rsqrt(jnp.mean(inputs * inputs, axis=-1, keepdims=True) + epsilon)
    normed_one = inputs * inverse_one
    normed_low = (normed_one * gain_one).astype(jnp.bfloat16)
    kv_own = dot32(normed_low, kv_full).astype(jnp.bfloat16).reshape(2, half_rows, kv_width)
    ring, other = [kv_own], []
    for step in range(lines - 1):
        ring.append(shift(after(ring[-1], *other), 1))
        other.append(flip(ring[step], "ctx", 1))
    other.append(flip(ring[-1], "ctx", 1))
    kv_all = jnp.concatenate(ring + other, axis=0)
    queries = dot32(normed_low, query_full).astype(jnp.bfloat16)

    hidden_share = shared_gate.shape[1] // members
    routes_all = jnp.concatenate(gather_pieces(after(routes.reshape(rows, TOP), ring[1])), axis=0)
    grad_pieces = gather_pieces(after(grad_low, ring[1]))
    queries = after(queries, routes_all)
    shared_w = jnp.concatenate(
        [
            shared_gate.reshape(share, members, hidden_share),
            shared_up.reshape(share, members, hidden_share),
            shared_down.T.reshape(share, members, hidden_share),
        ],
        axis=2,
    ).transpose(1, 0, 2)
    shared_w = lax.all_to_all(after(shared_w, ring[-1]), "wa", 0, 0, tiled=True)
    shared_w = shared_w.reshape(width, 3 * hidden_share)
    by_share = lambda value: value.reshape(rows, contexts, members, each).transpose(2, 0, 1, 3).reshape(
        members, rows, share
    )

    attended, log_sums = attention_forward(starts, own, queries, kv_all)
    mixed = jnp.concatenate([dot32(attended, out_full[m]) for m in range(members)], axis=1)
    residual = inputs + mixed
    inverse_two = lax.rsqrt(jnp.mean(residual * residual, axis=-1, keepdims=True) + epsilon)
    normed_two = residual * inverse_two
    second_low = after((normed_two * gain_two).astype(jnp.bfloat16), shared_w, *grad_pieces)

    second_pieces = gather_pieces(second_low)
    logits = jnp.concatenate([dot32(piece, router_full) for piece in second_pieces], axis=0)
    gates_all = dense_gates(logits, routes_all)
    attended_across = flip(after(attended, second_pieces[3]), "wa", 2)
    local = expert_gate.shape[0]
    weights = (expert_gate, expert_up, expert_down)
    at = lambda first: jnp.stack([member * local + first, context % 2]).astype(jnp.int32)
    *carried, line_terms, keep_one, send_one = experts_call(
        at(0), second_pieces, grad_pieces, gates_all, weights, 0, contexts
    )
    line_sums = scatter_lines(line_terms)
    other_one = flip(send_one, "ctx", 1)
    (
        out_keep, dx_keep, out_send, dx_send, gate_back,
        keep_both, send_both, pair_keep, pair_send,
    ) = experts_call(
        at(2), second_pieces, grad_pieces, gates_all, weights, 2, contexts, shared_w, carried
    )
    other_both = flip(send_both, "ctx", 1)

    def nothing(arrived):
        return 0.0 * arrived[(0,) * arrived.ndim].astype(jnp.float32)

    def side_sum(keep, received):
        return keep.astype(jnp.float32) + received.astype(jnp.float32)

    dx_near = dx_keep + flip(after(dx_send, other_one, attended_across), "wa", 1).astype(jnp.float32)
    dx_moved = flip(dx_near[rows:].astype(jnp.bfloat16), "wa", 2)
    dx_own = dx_near[:rows] + dx_moved.astype(jnp.float32)
    half = 2 * rows
    gate_back = reduce_rows(gate_back[:half], gate_back[half:], jnp.float32)

    gates = gates_all[:rows]
    logit_grad = gates * (gate_back - jnp.sum(gates * gate_back, axis=-1, keepdims=True))
    router_term = lax.dot_general(
        logit_grad, second_low.astype(jnp.float32), (((0,), (0,)), ((), ())), precision=highest
    )
    second_grad = dx_own + jnp.dot(logit_grad, router_full.astype(jnp.float32).T, precision=highest)
    gain_two_term, residual_back = rms_back(second_grad, normed_two, inverse_two, gain_two)
    residual_grad = grad_rows + residual_back
    mix_low = residual_grad.astype(jnp.bfloat16)

    attended_grad = sum(
        dot32(mix_low[:, m * share : (m + 1) * share], out_full[m], ((1,), (1,)))
        for m in range(members)
    ).astype(jnp.bfloat16)
    small_terms = jnp.concatenate([router_term, gain_two_term[None]], axis=0)
    small_terms = jnp.pad(small_terms, ((0, 128 - small_terms.shape[0]), (0, 0)))
    small_terms = small_terms.reshape(-1, contexts, members, each).transpose(2, 0, 1, 3)
    small_terms = small_terms.reshape(members, -1, share).astype(jnp.bfloat16)
    near_one = side_sum(keep_one, after(other_one, dx_moved)) + nothing(line_sums)
    near_one = near_one.astype(jnp.bfloat16)
    sum_one = scatter_lines(near_one)
    attended_grad = after(attended_grad, near_one)
    query_low, kv_keep, kv_send = attention_backward(starts, own, queries, attended_grad, kv_all, log_sums)
    by_line = lambda parts: parts.reshape(lines, rows, kv_width)
    query_across = flip(query_low, "wa", 2)
    bundle = jnp.concatenate([by_share(mix_low), by_share(normed_low), small_terms], axis=1)
    bundle = exchange(after(bundle, query_low), member)
    attended_core = flip(after(jnp.concatenate([attended, attended_across], axis=0), query_low), "wa", 1)
    query_core = flip(jnp.concatenate([query_low, query_across], axis=0), "wa", 1)
    moved = bundle[1:] + [attended_core, query_core]
    kv_send = after(by_line(kv_send), other_both, *moved)
    received = flip(kv_send, "ctx", 1)
    out_near = out_keep + flip(after(out_send, query_core), "wa", 1).astype(jnp.float32)
    out_moved = flip(out_near[rows:].astype(jnp.bfloat16), "wa", 2)
    out_own = out_near[:rows] + out_moved.astype(jnp.float32)
    block_out = (residual + out_own).astype(jnp.bfloat16).reshape(tokens.shape)
    near_both = (side_sum(keep_both, other_both) + nothing(sum_one)).astype(jnp.bfloat16)
    sum_both = scatter_lines(near_both)
    received = after(received, near_both)
    kv_near = by_line(kv_keep).astype(jnp.float32) + received.astype(jnp.float32)
    kv_parts = kv_near.astype(jnp.bfloat16)
    kv_moved = [shift(kv_parts[steps], -steps) for steps in range(1, lines)]
    stacked = lambda pieces: jnp.concatenate(pieces, axis=0)
    mix_share = stacked([piece[:rows] for piece in bundle])
    normed_share = stacked([piece[rows : 2 * rows] for piece in bundle])
    small_share = sum(piece[2 * rows :].astype(jnp.float32) for piece in bundle)
    query_all = stacked([query_low, query_across, query_core])
    attended_all = stacked([attended, attended_across, attended_core])
    early_term = jnp.concatenate(
        [
            dot32(normed_share, query_all, ((0,), (0,))),
            dot32(mix_share, attended_all, ((0,), (0,))),
            small_share.T,
        ],
        axis=1,
    ).astype(jnp.bfloat16)
    early_sides = to_side(after(early_term.reshape(contexts, each, -1), kv_parts), context)
    other_pair = flip(after(pair_send, kv_parts), "ctx", 1)
    kv_moved[0] = after(kv_moved[0], early_sides[1], out_moved)
    kv_low = (kv_near[0] + sum(moved.astype(jnp.float32) for moved in kv_moved)).astype(jnp.bfloat16)

    kv_across = flip(kv_low, "wa", 2)
    kv_pair = jnp.concatenate([kv_low, kv_across], axis=0)
    kv_low_all = jnp.concatenate([kv_pair, flip(kv_pair, "wa", 1)], axis=0)
    kv_term = dot32(normed_share, kv_low_all, ((0,), (0,)))
    first_grad = dot32(query_low, query_full, ((1,), (1,))) + dot32(kv_low, kv_full, ((1,), (1,)))
    scaled = first_grad * gain_one
    input_back = inverse_one * (
        scaled - normed_one * jnp.mean(scaled * normed_one, axis=-1, keepdims=True)
    )
    tokens_grad = (residual_grad + input_back).astype(jnp.bfloat16).reshape(tokens.shape)
    kv_sides = to_side(kv_term.astype(jnp.bfloat16).reshape(contexts, each, kv_width), context)
    kv_sum = line_sum(side_sum(*kv_sides), context)
    early_near = side_sum(early_sides[0], after(early_sides[1], *kv_moved))
    early_sum = line_sum(early_near, context, kv_sides[1])
    query_weight_grad, out_sum = early_sum[:, :width], early_sum[:, width:]
    out_weight_grad = out_sum[:, :width].T
    router_weight_grad = out_sum[:, width : width + EXPERTS]
    norm_gain_2_grad = out_sum[:, width + EXPERTS]
    key_weight_grad, value_weight_grad = apart(kv_sum)
    mine = lambda full: lax.dynamic_slice_in_dim(full, (context * members + member) * each, each, 0)
    norm_gain_1_grad = (
        jnp.sum(mine(query_full).astype(jnp.float32) * query_weight_grad, axis=1)
        + jnp.sum(mine(kv_full).astype(jnp.float32) * kv_sum, axis=1)
    ) / mine(gain_one)

    line_zero = flip((line_sums[1].astype(jnp.float32) + nothing(sum_both)).astype(jnp.bfloat16), "ctx", 1)
    sum_zero = line_sums[0].astype(jnp.float32) + line_zero.astype(jnp.float32)
    expert_sums = [sum_zero, sum_one, sum_both[0], sum_both[1]]
    expert_gate_grad = jnp.stack([total[0] for total in expert_sums]).astype(jnp.float32)
    expert_up_grad = jnp.stack([total[1] for total in expert_sums]).astype(jnp.float32)
    expert_down_grad = jnp.stack([total[2].T for total in expert_sums]).astype(jnp.float32)

    shared_sum = line_sum(side_sum(pair_keep, after(other_pair, kv_sides[1])), context)
    shared_sum = shared_sum.reshape(3, members, each, hidden_share).transpose(1, 0, 2, 3)
    shared_sum = lax.all_to_all(shared_sum, "wa", 0, 0, tiled=True)
    shared_gate_grad = shared_sum[:, 0].transpose(1, 0, 2).reshape(each, members * hidden_share)
    shared_up_grad = shared_sum[:, 1].transpose(1, 0, 2).reshape(each, members * hidden_share)
    shared_down_grad = shared_sum[:, 2].transpose(0, 2, 1).reshape(members * hidden_share, each)
    return (
        block_out,
        tokens_grad,
        norm_gain_1_grad,
        query_weight_grad,
        key_weight_grad,
        value_weight_grad,
        out_weight_grad,
        norm_gain_2_grad,
        router_weight_grad,
        shared_gate_grad,
        shared_up_grad,
        shared_down_grad,
        expert_gate_grad,
        expert_up_grad,
        expert_down_grad,
    )


def solution(mesh):
    return jax.shard_map(
        shards,
        mesh=mesh,
        in_specs=(
            P("wa", "ctx", None, None, None),
            P("wa", None),
            P("wa", "ctx", None, None, None),
            P("wa"),
            P("wa", None),
            P("wa", None),
            P("wa", None),
            P(None, "wa"),
            P("wa"),
            P("wa", None),
            P("wa", None),
            P("wa", None),
            P(None, "wa"),
            P("wa", None, None),
            P("wa", None, None),
            P("wa", None, None),
            P("wa", "ctx", None, None, None),
        ),
        out_specs=(
            P("wa", "ctx", None, None, None),
            P("wa", "ctx", None, None, None),
            P(("ctx", "wa")),
            P(("ctx", "wa"), None),
            P(("ctx", "wa"), None),
            P(("ctx", "wa"), None),
            P(None, ("ctx", "wa")),
            P(("ctx", "wa")),
            P(("ctx", "wa"), None),
            P(("ctx", "wa"), None),
            P(("ctx", "wa"), None),
            P(None, ("ctx", "wa")),
            P("wa", "ctx", None),
            P("wa", "ctx", None),
            P("wa", None, "ctx"),
        ),
        check_vma=False,
    )
```

```python
import functools

import jax
import jax.numpy as jnp
from jax import lax
from jax.experimental import pallas as pl
from jax.experimental.pallas import tpu as pltpu
from jax.sharding import PartitionSpec as P

QUERY_HEADS = 12
KEY_VALUE_HEADS = 4
HEAD_DIM = 128
TOP = 6
EXPERTS = 16

epsilon = 1e-05
large_negative = -1e30
highest = lax.Precision.HIGHEST
ORDER = (0, 2, 1, 3)


def dot32(left, right, dims=None):
    if dims is None:
        return jnp.dot(left, right, preferred_element_type=jnp.float32)
    return lax.dot_general(left, right, (dims, ((), ())), preferred_element_type=jnp.float32)


def flip(value, axis, bits):
    count = lax.axis_size(axis)
    return lax.ppermute(value, axis, [(i, i ^ bits) for i in range(count)])


def shift(value, steps):
    count = lax.axis_size("ctx")
    return lax.ppermute(value, "ctx", [(i, (i + 2 * steps) % count) for i in range(count)])


def after(value, *earlier):
    return lax.optimization_barrier((value,) + earlier)[0]


def gather_pieces(value):
    across = flip(value, "wa", 2)
    return [value, across, flip(value, "wa", 1), flip(across, "wa", 1)]


def ordered(pieces, index):
    chip, core = index // 2, index % 2
    near = [jnp.where(core == i, pieces[0], pieces[2]) for i in range(2)]
    far = [jnp.where(core == i, pieces[1], pieces[3]) for i in range(2)]
    return jnp.concatenate(
        [jnp.where(chip == i // 2, near[i % 2], far[i % 2]) for i in range(4)], axis=0
    )


def exchange(pieces, index):
    received = []
    for bits in ORDER:
        piece = lax.dynamic_index_in_dim(pieces, index ^ bits, 0, keepdims=False)
        received.append(piece if bits == 0 else flip(piece, "wa", bits))
    return received


def reduce_rows(keep, send, kind):
    near = keep + flip(send, "wa", 1).astype(jnp.float32)
    quarter = keep.shape[0] // 2
    return near[:quarter] + flip(near[quarter:].astype(kind), "wa", 2).astype(jnp.float32)


def scatter_small(value):
    rows, width = value.shape
    contexts, members = lax.axis_size("ctx"), lax.axis_size("wa")
    each = width // (contexts * members)
    spread = value.reshape(rows, contexts, members, each).transpose(2, 0, 1, 3)
    spread = spread.reshape(members, rows, contexts * each)
    first = jnp.sum(lax.all_to_all(spread, "wa", 0, 0, tiled=True), axis=0)
    second = first.reshape(rows, contexts, each).transpose(1, 0, 2)
    return jnp.sum(lax.all_to_all(second, "ctx", 0, 0, tiled=True), axis=0)


def sides():
    count = lax.axis_size("ctx")
    return [list(range(side, count, 2)) for side in range(2)]


def to_side(value, index):
    pairs = value.reshape((value.shape[0] // 2, 2) + value.shape[1:])
    keep = lax.dynamic_index_in_dim(pairs, index % 2, 1, keepdims=False)
    return keep, flip(lax.dynamic_index_in_dim(pairs, 1 - index % 2, 1, keepdims=False), "ctx", 1)


def line_sum(near, index, *before):
    lines, line = near.shape[0], index // 2
    low = near.astype(jnp.bfloat16)
    total = lax.dynamic_index_in_dim(near, line, 0, keepdims=False)
    for steps in range(1, lines):
        piece = lax.dynamic_index_in_dim(low, (line + lines - steps) % lines, 0, keepdims=False)
        total = total + after(shift(piece, -steps), *before).astype(jnp.float32)
    return total


def scatter_lines(value):
    return lax.psum_scatter(
        value, "ctx", scatter_dimension=0, axis_index_groups=sides(), tiled=True
    )[0]


def silu_parts(values):
    sigmoid_of = jax.nn.sigmoid(values)
    return (values * sigmoid_of, sigmoid_of * (1.0 + values * (1.0 - sigmoid_of)))


def rms_back(grad_normed, normed, inverse, gain_values):
    scaled = grad_normed * gain_values
    return (
        jnp.sum(grad_normed * normed, axis=0),
        inverse * (scaled - normed * jnp.mean(scaled * normed, axis=-1, keepdims=True)),
    )


TOGETHER = 3


def attention_masks(starts_ref, block, half_rows, shape):
    rows = block * half_rows + lax.broadcasted_iota(jnp.int32, shape, 0) % half_rows
    first = jnp.zeros(shape, jnp.int32)
    for document in range(1, starts_ref.shape[0]):
        start = starts_ref[document]
        first = jnp.where(start <= rows, jnp.maximum(first, start), first)
    return first, rows


def block_bounds(starts_ref, block, half_rows):
    top = block * half_rows
    first = jnp.int32(0)
    for document in range(1, starts_ref.shape[0]):
        start = starts_ref[document]
        first = jnp.where(start <= top, jnp.maximum(first, start), first)
    return first // half_rows


def block_place(block, own, contexts):
    late = (block >= contexts).astype(jnp.int32)
    device = jnp.where(block < contexts, block, 2 * contexts - 1 - block)
    lines = contexts // 2
    behind = own // 2 - device // 2
    behind = jnp.where(behind < 0, behind + lines, behind)
    return (((own + device) % 2) * lines + behind) * 2 + late


def attention_forward_kernel(starts_ref, own_ref, q_ref, kv_ref, o_ref, lse_ref, s_ref):
    blocks, half_rows, _ = kv_ref.shape
    contexts = blocks // 2
    ratio = q_ref.shape[1] // HEAD_DIM
    rows = ratio * half_rows
    scale = HEAD_DIM ** (-0.5)
    for half in range(2):
        block = own_ref[0] if half == 0 else blocks - 1 - own_ref[0]
        queries = jnp.concatenate(
            [
                q_ref[half * half_rows : (half + 1) * half_rows, h * HEAD_DIM : (h + 1) * HEAD_DIM]
                for h in range(ratio)
            ],
            axis=0,
        )
        low = block_bounds(starts_ref, block, half_rows)
        first, position = attention_masks(starts_ref, block, half_rows, (rows, half_rows))
        column = lax.broadcasted_iota(jnp.int32, (rows, half_rows), 1)

        trips = (block - low + TOGETHER) // TOGETHER

        def score_step(trip, running):
            for part in range(TOGETHER):
                step = trip * TOGETHER + part
                place = block_place(jnp.minimum(low + step, block), own_ref[0], contexts)
                scores = dot32(queries, kv_ref[place, :, :HEAD_DIM], ((1,), (1,))) * scale
                at = column + (low + step) * half_rows
                scores = jnp.where((at >= first) & (at <= position), scores, large_negative)
                s_ref[step] = scores
                running = jnp.maximum(running, scores)
            return running

        running = lax.fori_loop(
            0, trips, score_step, jnp.full((rows, half_rows), large_negative, jnp.float32)
        )
        row_max = jnp.max(running, axis=1, keepdims=True)

        def sum_step(trip, total):
            for part in range(TOGETHER):
                step = trip * TOGETHER + part
                expo = jnp.exp(s_ref[step] - row_max)
                s_ref[step] = expo
                total = total + expo
            return total

        total = lax.fori_loop(0, trips, sum_step, jnp.zeros((rows, half_rows), jnp.float32))
        row_sum = jnp.sum(total, axis=1, keepdims=True)
        inverse = 1.0 / row_sum

        def value_step(trip, accum):
            for part in range(TOGETHER):
                step = trip * TOGETHER + part
                place = block_place(jnp.minimum(low + step, block), own_ref[0], contexts)
                weights = (s_ref[step] * inverse).astype(jnp.bfloat16)
                accum = accum + dot32(weights, kv_ref[place, :, HEAD_DIM:])
            return accum

        accum = lax.fori_loop(0, trips, value_step, jnp.zeros((rows, HEAD_DIM), jnp.float32))
        log_sum = row_max + jnp.log(row_sum)
        lse_ref[0, half] = jnp.broadcast_to(log_sum, (rows, half_rows))
        for h in range(ratio):
            o_ref[half * half_rows : (half + 1) * half_rows, h * HEAD_DIM : (h + 1) * HEAD_DIM] = (
                accum[h * half_rows : (h + 1) * half_rows].astype(jnp.bfloat16)
            )


def attention_forward(starts, own, queries, kv):
    rows, width = queries.shape
    blocks, half_rows, _ = kv.shape
    ratio = QUERY_HEADS // KEY_VALUE_HEADS
    stacked = ratio * half_rows
    kv_spec = pl.BlockSpec((blocks, half_rows, 2 * HEAD_DIM), lambda g, *_: (0, 0, g))
    q_spec = pl.BlockSpec((rows, ratio * HEAD_DIM), lambda g, *_: (0, g))
    return pl.pallas_call(
        attention_forward_kernel,
        grid_spec=pltpu.PrefetchScalarGridSpec(
            num_scalar_prefetch=2,
            grid=(KEY_VALUE_HEADS,),
            in_specs=[q_spec, kv_spec],
            out_specs=[
                q_spec,
                pl.BlockSpec((1, 2, stacked, half_rows), lambda g, *_: (g, 0, 0, 0)),
            ],
            scratch_shapes=[pltpu.VMEM((blocks + TOGETHER - 1, stacked, half_rows), jnp.float32)],
        ),
        out_shape=(
            jax.ShapeDtypeStruct((rows, width), jnp.bfloat16),
            jax.ShapeDtypeStruct((KEY_VALUE_HEADS, 2, stacked, half_rows), jnp.float32),
        ),
        compiler_params=pltpu.CompilerParams(vmem_limit_bytes=48 << 20),
        cost_estimate=pl.CostEstimate(flops=0, bytes_accessed=1 << 20, transcendentals=0),
        name="attention_forward",
    )(starts, own, queries, kv)


def attention_backward_kernel(
    starts_ref, own_ref, q_ref, do_ref, kv_ref, lse_ref, dq_ref, keep_ref, send_ref, p_ref, dp_ref, dka_ref, dva_ref
):
    blocks, half_rows, _ = kv_ref.shape
    contexts = blocks // 2
    ratio = q_ref.shape[1] // HEAD_DIM
    rows = ratio * half_rows
    scale = HEAD_DIM ** (-0.5)
    dka_ref[...] = jnp.zeros_like(dka_ref)
    dva_ref[...] = jnp.zeros_like(dva_ref)

    def stack(ref, half):
        return jnp.concatenate(
            [
                ref[half * half_rows : (half + 1) * half_rows, h * HEAD_DIM : (h + 1) * HEAD_DIM]
                for h in range(ratio)
            ],
            axis=0,
        )

    for half in range(2):
        block = own_ref[0] if half == 0 else blocks - 1 - own_ref[0]
        queries = stack(q_ref, half)
        grads = stack(do_ref, half)
        log_sum = lse_ref[0, half]
        low = block_bounds(starts_ref, block, half_rows)
        first, position = attention_masks(starts_ref, block, half_rows, (rows, half_rows))
        column = lax.broadcasted_iota(jnp.int32, (rows, half_rows), 1)

        trips = (block - low + TOGETHER) // TOGETHER

        def prob_step(trip, running):
            for part in range(TOGETHER):
                step = trip * TOGETHER + part
                place = block_place(jnp.minimum(low + step, block), own_ref[0], contexts)
                scores = dot32(queries, kv_ref[place, :, :HEAD_DIM], ((1,), (1,))) * scale
                at = column + (low + step) * half_rows
                probs = jnp.where(
                    (at >= first) & (at <= position), jnp.exp(scores - log_sum), 0.0
                )
                prob_grads = dot32(grads, kv_ref[place, :, HEAD_DIM:], ((1,), (1,)))
                p_ref[step] = probs
                dp_ref[step] = prob_grads
                running = running + probs * prob_grads
            return running

        running = lax.fori_loop(0, trips, prob_step, jnp.zeros((rows, half_rows), jnp.float32))
        delta = jnp.sum(running, axis=1, keepdims=True)

        def grad_step(trip, query_grad):
            for part in range(TOGETHER):
                step = trip * TOGETHER + part
                place = block_place(jnp.minimum(low + step, block), own_ref[0], contexts)
                probs = p_ref[step]
                score_low = (probs * (dp_ref[step] - delta)).astype(jnp.bfloat16)
                dka_ref[place] += dot32(score_low, queries, ((0,), (0,)))
                dva_ref[place] += dot32(probs.astype(jnp.bfloat16), grads, ((0,), (0,)))
                query_grad = query_grad + dot32(score_low, kv_ref[place, :, :HEAD_DIM])
            return query_grad

        query_grad = lax.fori_loop(0, trips, grad_step, jnp.zeros((rows, HEAD_DIM), jnp.float32))
        for h in range(ratio):
            dq_ref[half * half_rows : (half + 1) * half_rows, h * HEAD_DIM : (h + 1) * HEAD_DIM] = (
                query_grad[h * half_rows : (h + 1) * half_rows] * scale
            ).astype(jnp.bfloat16)
    for out_ref, places in ((keep_ref, slice(0, contexts)), (send_ref, slice(contexts, blocks))):
        out_ref[:, :, :HEAD_DIM] = (dka_ref[places] * scale).astype(jnp.bfloat16)
        out_ref[:, :, HEAD_DIM:] = dva_ref[places].astype(jnp.bfloat16)


def attention_backward(starts, own, queries, grads, kv, log_sums):
    rows, width = queries.shape
    blocks, half_rows, kv_width = kv.shape
    ratio = QUERY_HEADS // KEY_VALUE_HEADS
    stacked = ratio * half_rows
    kv_spec = pl.BlockSpec((blocks, half_rows, 2 * HEAD_DIM), lambda g, *_: (0, 0, g))
    part_spec = pl.BlockSpec((blocks // 2, half_rows, 2 * HEAD_DIM), lambda g, *_: (0, 0, g))
    q_spec = pl.BlockSpec((rows, ratio * HEAD_DIM), lambda g, *_: (0, g))
    return pl.pallas_call(
        attention_backward_kernel,
        grid_spec=pltpu.PrefetchScalarGridSpec(
            num_scalar_prefetch=2,
            grid=(KEY_VALUE_HEADS,),
            in_specs=[
                q_spec,
                q_spec,
                kv_spec,
                pl.BlockSpec((1, 2, stacked, half_rows), lambda g, *_: (g, 0, 0, 0)),
            ],
            out_specs=[q_spec, part_spec, part_spec],
            scratch_shapes=[
                pltpu.VMEM((blocks + TOGETHER - 1, stacked, half_rows), jnp.float32),
                pltpu.VMEM((blocks + TOGETHER - 1, stacked, half_rows), jnp.float32),
                pltpu.VMEM((blocks, half_rows, HEAD_DIM), jnp.float32),
                pltpu.VMEM((blocks, half_rows, HEAD_DIM), jnp.float32),
            ],
        ),
        out_shape=(
            jax.ShapeDtypeStruct((rows, width), jnp.bfloat16),
            jax.ShapeDtypeStruct((blocks // 2, half_rows, kv_width), jnp.bfloat16),
            jax.ShapeDtypeStruct((blocks // 2, half_rows, kv_width), jnp.bfloat16),
        ),
        compiler_params=pltpu.CompilerParams(vmem_limit_bytes=58 << 20),
        cost_estimate=pl.CostEstimate(flops=0, bytes_accessed=1 << 20, transcendentals=0),
        name="attention_backward",
    )(starts, own, queries, grads, kv, log_sums)


def experts_kernel(final, *refs):
    at_ref, *refs = refs
    parts, refs = refs[:8], refs[8:]
    g_ref, wg_ref, wu_ref, wd_ref, *refs = refs
    if final:
        shared_ref, out_in, dx_in, dg_in, *refs = refs
        out_hbm, dx_hbm, out_low_ref, dx_low_ref, dg_ref, *refs = refs
        targets = ((refs[0], refs[1]), (refs[2], refs[3]))
        pair_target, refs = (refs[4], refs[5]), refs[6:]
        x_ref, dy_ref, he_ref, da_ref, db_ref, out_ref, dx_ref, sem = refs
    else:
        out_hbm, dx_hbm, dg_ref, line_hbm, *refs = refs
        x_ref, dy_ref, he_ref, da_ref, db_ref, out_ref, dx_ref, line_ref, sem = refs[2:]
        targets = (line_ref, (refs[0], refs[1]))
        line_copy = pltpu.make_async_copy(line_ref, line_hbm, sem.at[19])
    local = pl.program_id(0)
    expert = at_ref[0] + local
    side = at_ref[1]
    total_rows, width = x_ref.shape
    half = total_rows // 2
    step_rows = total_rows // 4
    tall = 384

    def loads(number):
        rows = pl.ds(number * step_rows, step_rows)
        moves = [(parts[number], x_ref.at[rows, :]), (parts[4 + number], dy_ref.at[rows, :])]
        if final:
            moves += [(out_in.at[rows, :], out_ref.at[rows, :]), (dx_in.at[rows, :], dx_ref.at[rows, :])]
            if number == 0:
                moves.append((dg_in, dg_ref))
        return [
            pltpu.make_async_copy(source, target, sem.at[number * 5 + place])
            for place, (source, target) in enumerate(moves)
        ]

    def results(number, count):
        rows = pl.ds(number * count, count)
        return [
            pltpu.make_async_copy(ref.at[rows, :], hbm.at[rows, :], sem.at[number * 2 + place])
            for place, (ref, hbm) in enumerate(((out_ref, out_hbm), (dx_ref, dx_hbm)))
        ]

    @pl.when(local == 0)
    def _():
        for number in range(4):
            for copy in loads(number):
                copy.start()
        if not final:
            for ref in (out_ref, dx_ref, dg_ref):
                ref[...] = jnp.zeros_like(ref)

    def add(number, rows, value):
        (out_ref, dx_ref)[number][rows, :] += value

    def store_sides(lows, begin, pair):
        per = pair[0].shape[2]
        for parity in range(2):

            @pl.when(side == parity)
            def _():
                for part in range(tall // per):
                    line = begin // (2 * per) + part // 2
                    for number, low in enumerate(lows):
                        pair[(part + parity) % 2][line, number] = low[part * per : (part + 1) * per]

    def store_lines(lows, begin, target):
        per = target.shape[3]
        for part in range(tall // per):
            line = begin // (2 * per) + part // 2
            for number, low in enumerate(lows):
                target[line, (side + part) % 2, number] = low[part * per : (part + 1) * per]

    for number in range(4):
        rows = slice(number * step_rows, (number + 1) * step_rows)

        @pl.when(local == 0)
        def _():
            for copy in loads(number):
                copy.wait()

        x = x_ref[rows, :]
        lane = lax.broadcasted_iota(jnp.int32, (step_rows, g_ref.shape[1]), 1)
        mine = lane == expert
        gate = jnp.sum(jnp.where(mine, g_ref[rows, :], 0.0), axis=1, keepdims=True)
        pre = dot32(x, wg_ref[0])
        up = dot32(x, wu_ref[0])
        back = dot32(dy_ref[rows, :], wd_ref[0], ((1,), (1,)))
        silu, slope = silu_parts(pre)
        hidden = (silu * up).astype(jnp.bfloat16).astype(jnp.float32)
        dg_ref[rows, :] += jnp.where(mine, jnp.sum(hidden * back, axis=1, keepdims=True), 0.0)
        hidden_low = (gate * hidden).astype(jnp.bfloat16)
        he_ref[rows, :] = hidden_low
        add(0, rows, dot32(hidden_low, wd_ref[0]))
        back = gate * back
        pre_low = (back * up * slope).astype(jnp.bfloat16)
        up_low = (back * silu).astype(jnp.bfloat16)
        da_ref[rows, :] = pre_low
        db_ref[rows, :] = up_low
        add(1, rows, dot32(pre_low, wg_ref[0], ((1,), (1,))) + dot32(up_low, wu_ref[0], ((1,), (1,))))
        if not final:

            @pl.when(local == 1)
            def _():
                for copy in results(number, step_rows):
                    copy.start()

    @pl.loop(0, width // tall)
    def _(step):
        begin = pl.multiple_of(step * tall, tall)
        columns = pl.ds(begin, tall)
        lows = [
            dot32(left[:, columns], right[...], ((0,), (0,))).astype(jnp.bfloat16)
            for left, right in ((x_ref, da_ref), (x_ref, db_ref), (dy_ref, he_ref))
        ]
        for number, target in enumerate(targets):

            @pl.when(local == number)
            def _():
                if isinstance(target, tuple):
                    store_sides(lows, begin, target)
                else:
                    store_lines(lows, begin, target)

    if not final:

        @pl.when(local == 0)
        def _():
            line_copy.start()

        @pl.when(local == 1)
        def _():
            line_copy.wait()
            for number in range(4):
                for copy in results(number, step_rows):
                    copy.wait()

        return

    @pl.when(local == pl.num_programs(0) - 1)
    def _():
        shared = shared_ref.shape[1] // 3
        pair_w, down_w = slice(0, 2 * shared), slice(2 * shared, 3 * shared)
        for begin in range(0, total_rows, step_rows):
            rows = slice(begin, begin + step_rows)
            both = dot32(x_ref[rows, :], shared_ref[:, pair_w])
            pre, up = both[:, :shared], both[:, shared:]
            silu, slope = silu_parts(pre)
            hidden = (silu * up).astype(jnp.bfloat16)
            he_ref[rows, :shared] = hidden
            add(0, rows, dot32(hidden, shared_ref[:, down_w], ((1,), (1,))))
            back = dot32(dy_ref[rows, :], shared_ref[:, down_w])
            da_ref[rows, :shared] = (back * up * slope).astype(jnp.bfloat16)
            da_ref[rows, shared:] = (back * silu).astype(jnp.bfloat16)
            add(1, rows, dot32(da_ref[rows, :], shared_ref[:, pair_w], ((1,), (1,))))
        for copy in results(0, half):
            copy.start()
        out_low_ref[...] = out_ref[half:, :].astype(jnp.bfloat16)
        dx_low_ref[...] = dx_ref[half:, :].astype(jnp.bfloat16)

        @pl.loop(0, width // tall)
        def _(step):
            begin = pl.multiple_of(step * tall, tall)
            columns = pl.ds(begin, tall)
            pair_low = dot32(x_ref[:, columns], da_ref[...], ((0,), (0,))).astype(jnp.bfloat16)
            down_low = dot32(dy_ref[:, columns], he_ref[:, :shared], ((0,), (0,))).astype(jnp.bfloat16)
            store_sides((pair_low[:, :shared], pair_low[:, shared:], down_low), begin, pair_target)

        for copy in results(0, half):
            copy.wait()


def experts_call(at, x, dy, gates, weights, first, contexts, shared_w=None, carried=()):
    final = shared_w is not None
    gate_w, up_w, down_w = weights
    rows, width = 4 * x[0].shape[0], x[0].shape[1]
    hidden = gate_w.shape[2]
    per, lines, half = width // contexts, contexts // 2, rows // 2
    once = pl.Buffered(1)
    whole = lambda shape: pl.BlockSpec(shape, lambda e, *_: (0,) * len(shape), pipeline_mode=once)
    weight = lambda shape: pl.BlockSpec((1,) + shape, lambda e, *_: (first + e, 0, 0))
    apart = pl.BlockSpec(memory_space=pl.ANY)
    part = jax.ShapeDtypeStruct((half, width), jnp.float32)
    low = jax.ShapeDtypeStruct((half, width), jnp.bfloat16)
    full = jax.ShapeDtypeStruct((rows, width), jnp.float32)
    table = jax.ShapeDtypeStruct((rows, EXPERTS), jnp.float32)
    term = jax.ShapeDtypeStruct((lines, 3, per, hidden), jnp.bfloat16)
    both = jax.ShapeDtypeStruct((lines, 2, 3, per, hidden), jnp.bfloat16)
    scratch = [pltpu.VMEM((rows, width), jnp.bfloat16)] * 2 + [pltpu.VMEM((rows, hidden), jnp.bfloat16)] * 3
    scratch += [pltpu.VMEM((rows, width), jnp.float32)] * 2
    if final:
        shared = shared_w.shape[1] // 3
        pair = jax.ShapeDtypeStruct((lines, 3, per, shared), jnp.bfloat16)
        extra_specs = [whole(shared_w.shape)] + [apart] * 3
        out_shape = (part, part, low, low, table, term, term, term, term, pair, pair)
        outside = (0, 1)
    else:
        shared = 0
        extra_specs = []
        out_shape = (full, full, table, both, term, term)
        outside = (0, 1, 3)
        scratch.append(pltpu.VMEM(both.shape, jnp.bfloat16))
    return pl.pallas_call(
        functools.partial(experts_kernel, final),
        grid_spec=pltpu.PrefetchScalarGridSpec(
            num_scalar_prefetch=1,
            grid=(2,),
            in_specs=[apart] * 8
            + [
                whole((rows, EXPERTS)),
                weight((width, hidden)),
                weight((width, hidden)),
                weight((hidden, width)),
            ]
            + extra_specs,
            out_specs=[apart if place in outside else whole(item.shape) for place, item in enumerate(out_shape)],
            scratch_shapes=scratch + [pltpu.SemaphoreType.DMA((20,))],
        ),
        out_shape=out_shape,
        compiler_params=pltpu.CompilerParams(vmem_limit_bytes=60 << 20),
        cost_estimate=pl.CostEstimate(flops=0, bytes_accessed=1 << 20, transcendentals=0),
        name="experts_final" if final else "experts",
    )(at, *x, *dy, gates, gate_w, up_w, down_w, *((shared_w,) if final else ()), *carried)


def dense_gates(logits, routes):
    chosen = jnp.any(
        routes[:, :, None] == jnp.arange(EXPERTS, dtype=jnp.int32)[None, None, :], axis=1
    )
    top = jnp.max(jnp.where(chosen, logits, large_negative), axis=-1, keepdims=True)
    expo = jnp.where(chosen, jnp.exp(logits - top), 0.0)
    return expo / jnp.sum(expo, axis=-1, keepdims=True)


def shards(
    tokens, doc_starts, routes, norm_gain_1, query_weight, key_matrix, value_matrix, out_weight,
    norm_gain_2, router_weight, shared_gate, shared_up, shared_down, expert_gate, expert_up,
    expert_down, out_grad,
):
    contexts, members = lax.axis_size("ctx"), lax.axis_size("wa")
    context, member = lax.axis_index("ctx"), lax.axis_index("wa")
    half_rows, width = tokens.shape[3], tokens.shape[4]
    rows = 2 * half_rows
    share = width // members
    each = share // contexts
    lines = contexts // 2
    kv_width = 2 * key_matrix.shape[1]
    starts = doc_starts[0]
    own = context[None].astype(jnp.int32)
    inputs = tokens.reshape(rows, width).astype(jnp.float32)
    grad_low = out_grad.reshape(rows, width)
    grad_rows = grad_low.astype(jnp.float32)

    beside = lambda k, v: jnp.stack(
        [k.reshape(-1, KEY_VALUE_HEADS, HEAD_DIM), v.reshape(-1, KEY_VALUE_HEADS, HEAD_DIM)], axis=2
    ).reshape(-1, kv_width)
    apart = lambda kv: jnp.moveaxis(
        kv.reshape(-1, KEY_VALUE_HEADS, 2, HEAD_DIM), 2, 0
    ).reshape(2, -1, kv_width // 2)
    small = jnp.concatenate([router_weight, norm_gain_1[:, None], norm_gain_2[:, None]], axis=1)
    small = jnp.pad(small, ((0, 0), (0, 128 - EXPERTS - 2)))
    kv_pieces = gather_pieces(jnp.concatenate([beside(key_matrix, value_matrix), small], axis=1))
    kv_across = kv_pieces[1]
    kv_full = ordered(kv_pieces, member)
    router_full = kv_full[:, kv_width : kv_width + EXPERTS]
    gain_one = kv_full[:, kv_width + EXPERTS].astype(jnp.float32)
    gain_two = kv_full[:, kv_width + EXPERTS + 1].astype(jnp.float32)
    kv_full = kv_full[:, :kv_width]
    query_full = lax.all_gather(after(query_weight, kv_across), "wa", axis=0, tiled=True)
    out_full = lax.all_gather(after(out_weight, kv_across), "wa", axis=0, tiled=False)

    inverse_one = lax.rsqrt(jnp.mean(inputs * inputs, axis=-1, keepdims=True) + epsilon)
    normed_one = inputs * inverse_one
    normed_low = (normed_one * gain_one).astype(jnp.bfloat16)
    kv_own = dot32(normed_low, kv_full).astype(jnp.bfloat16).reshape(2, half_rows, kv_width)
    ring, other = [kv_own], []
    for step in range(lines - 1):
        ring.append(shift(after(ring[-1], *other), 1))
        other.append(flip(ring[step], "ctx", 1))
    other.append(flip(ring[-1], "ctx", 1))
    kv_all = jnp.concatenate(ring + other, axis=0)
    queries = dot32(normed_low, query_full).astype(jnp.bfloat16)

    hidden_share = shared_gate.shape[1] // members
    routes_all = jnp.concatenate(gather_pieces(after(routes.reshape(rows, TOP), ring[1])), axis=0)
    grad_pieces = gather_pieces(after(grad_low, ring[1]))
    queries = after(queries, routes_all)
    shared_w = jnp.concatenate(
        [
            shared_gate.reshape(share, members, hidden_share),
            shared_up.reshape(share, members, hidden_share),
            shared_down.T.reshape(share, members, hidden_share),
        ],
        axis=2,
    ).transpose(1, 0, 2)
    shared_w = lax.all_to_all(after(shared_w, ring[-1]), "wa", 0, 0, tiled=True)
    shared_w = shared_w.reshape(width, 3 * hidden_share)
    by_share = lambda value: value.reshape(rows, contexts, members, each).transpose(2, 0, 1, 3).reshape(
        members, rows, share
    )

    attended, log_sums = attention_forward(starts, own, queries, kv_all)
    mixed = jnp.concatenate([dot32(attended, out_full[m]) for m in range(members)], axis=1)
    residual = inputs + mixed
    inverse_two = lax.rsqrt(jnp.mean(residual * residual, axis=-1, keepdims=True) + epsilon)
    normed_two = residual * inverse_two
    second_low = after((normed_two * gain_two).astype(jnp.bfloat16), shared_w, *grad_pieces)

    second_pieces = gather_pieces(second_low)
    logits = jnp.concatenate([dot32(piece, router_full) for piece in second_pieces], axis=0)
    gates_all = dense_gates(logits, routes_all)
    attended_across = flip(after(attended, second_pieces[3]), "wa", 2)
    local = expert_gate.shape[0]
    weights = (expert_gate, expert_up, expert_down)
    at = lambda first: jnp.stack([member * local + first, context % 2]).astype(jnp.int32)
    *carried, line_terms, keep_one, send_one = experts_call(
        at(0), second_pieces, grad_pieces, gates_all, weights, 0, contexts
    )
    line_sums = scatter_lines(line_terms)
    other_one = flip(send_one, "ctx", 1)
    (
        out_keep, dx_keep, out_send, dx_send, gate_back,
        keep_two, send_two, keep_three, send_three, pair_keep, pair_send,
    ) = experts_call(
        at(2), second_pieces, grad_pieces, gates_all, weights, 2, contexts, shared_w, carried
    )
    other_two = flip(send_two, "ctx", 1)

    def nothing(arrived):
        return 0.0 * arrived[(0,) * arrived.ndim].astype(jnp.float32)

    def side_sum(keep, received):
        return keep.astype(jnp.float32) + received.astype(jnp.float32)

    dx_near = dx_keep + flip(after(dx_send, other_one, attended_across), "wa", 1).astype(jnp.float32)
    dx_moved = flip(dx_near[rows:].astype(jnp.bfloat16), "wa", 2)
    other_three = flip(after(send_three, dx_moved), "ctx", 1)
    dx_own = dx_near[:rows] + after(dx_moved, other_two).astype(jnp.float32)
    half = 2 * rows
    gate_back = reduce_rows(gate_back[:half], gate_back[half:], jnp.float32)

    gates = gates_all[:rows]
    logit_grad = gates * (gate_back - jnp.sum(gates * gate_back, axis=-1, keepdims=True))
    router_term = lax.dot_general(
        logit_grad, second_low.astype(jnp.float32), (((0,), (0,)), ((), ())), precision=highest
    )
    second_grad = dx_own + jnp.dot(logit_grad, router_full.astype(jnp.float32).T, precision=highest)
    gain_two_term, residual_back = rms_back(second_grad, normed_two, inverse_two, gain_two)
    residual_grad = grad_rows + residual_back
    mix_low = residual_grad.astype(jnp.bfloat16)

    attended_grad = sum(
        dot32(mix_low[:, m * share : (m + 1) * share], out_full[m], ((1,), (1,)))
        for m in range(members)
    ).astype(jnp.bfloat16)
    small_terms = jnp.concatenate([router_term, gain_two_term[None]], axis=0)
    small_terms = jnp.pad(small_terms, ((0, 128 - small_terms.shape[0]), (0, 0)))
    small_terms = small_terms.reshape(-1, contexts, members, each).transpose(2, 0, 1, 3)
    small_terms = small_terms.reshape(members, -1, share).astype(jnp.bfloat16)
    near_one = side_sum(keep_one, after(other_one, dx_moved)) + nothing(line_sums)
    near_one = near_one.astype(jnp.bfloat16)
    sum_one = scatter_lines(near_one)
    attended_grad = after(attended_grad, near_one)
    query_low, kv_keep, kv_send = attention_backward(starts, own, queries, attended_grad, kv_all, log_sums)
    by_line = lambda parts: parts.reshape(lines, rows, kv_width)
    query_across = flip(query_low, "wa", 2)
    bundle = jnp.concatenate([by_share(mix_low), by_share(normed_low), small_terms], axis=1)
    bundle = exchange(after(bundle, query_low), member)
    attended_core = flip(after(jnp.concatenate([attended, attended_across], axis=0), query_low), "wa", 1)
    query_core = flip(jnp.concatenate([query_low, query_across], axis=0), "wa", 1)
    moved = bundle[1:] + [attended_core, query_core]
    near_two = (side_sum(keep_two, after(other_two, query_low)) + nothing(sum_one)).astype(jnp.bfloat16)
    sum_two = scatter_lines(near_two)
    kv_send = after(by_line(kv_send), other_three, near_two, *moved)
    received = flip(kv_send, "ctx", 1)
    out_near = out_keep + flip(after(out_send, query_core), "wa", 1).astype(jnp.float32)
    out_moved = flip(out_near[rows:].astype(jnp.bfloat16), "wa", 2)
    out_own = out_near[:rows] + out_moved.astype(jnp.float32)
    block_out = (residual + out_own).astype(jnp.bfloat16).reshape(tokens.shape)
    near_three = side_sum(keep_three, other_three) + 0.0 * near_two[0, 0, 0, 0].astype(jnp.float32)
    near_three = near_three.astype(jnp.bfloat16)
    sum_three = scatter_lines(near_three)
    received = after(received, near_three)
    kv_near = by_line(kv_keep).astype(jnp.float32) + received.astype(jnp.float32)
    kv_parts = kv_near.astype(jnp.bfloat16)
    kv_moved = [shift(kv_parts[steps], -steps) for steps in range(1, lines)]
    stacked = lambda pieces: jnp.concatenate(pieces, axis=0)
    mix_share = stacked([piece[:rows] for piece in bundle])
    normed_share = stacked([piece[rows : 2 * rows] for piece in bundle])
    small_share = sum(piece[2 * rows :].astype(jnp.float32) for piece in bundle)
    query_all = stacked([query_low, query_across, query_core])
    attended_all = stacked([attended, attended_across, attended_core])
    early_term = jnp.concatenate(
        [
            dot32(normed_share, query_all, ((0,), (0,))),
            dot32(mix_share, attended_all, ((0,), (0,))),
            small_share.T,
        ],
        axis=1,
    ).astype(jnp.bfloat16)
    early_sides = to_side(after(early_term.reshape(contexts, each, -1), kv_parts), context)
    other_pair = flip(after(pair_send, kv_parts), "ctx", 1)
    kv_moved[0] = after(kv_moved[0], early_sides[1], out_moved)
    kv_low = (kv_near[0] + sum(moved.astype(jnp.float32) for moved in kv_moved)).astype(jnp.bfloat16)

    kv_across = flip(kv_low, "wa", 2)
    kv_pair = jnp.concatenate([kv_low, kv_across], axis=0)
    kv_low_all = jnp.concatenate([kv_pair, flip(kv_pair, "wa", 1)], axis=0)
    kv_term = dot32(normed_share, kv_low_all, ((0,), (0,)))
    first_grad = dot32(query_low, query_full, ((1,), (1,))) + dot32(kv_low, kv_full, ((1,), (1,)))
    scaled = first_grad * gain_one
    input_back = inverse_one * (
        scaled - normed_one * jnp.mean(scaled * normed_one, axis=-1, keepdims=True)
    )
    tokens_grad = (residual_grad + input_back).astype(jnp.bfloat16).reshape(tokens.shape)
    kv_sides = to_side(kv_term.astype(jnp.bfloat16).reshape(contexts, each, kv_width), context)
    kv_sum = line_sum(side_sum(*kv_sides), context)
    early_near = side_sum(early_sides[0], after(early_sides[1], *kv_moved))
    early_sum = line_sum(early_near, context, kv_sides[1])
    query_weight_grad, out_sum = early_sum[:, :width], early_sum[:, width:]
    out_weight_grad = out_sum[:, :width].T
    router_weight_grad = out_sum[:, width : width + EXPERTS]
    norm_gain_2_grad = out_sum[:, width + EXPERTS]
    key_weight_grad, value_weight_grad = apart(kv_sum)
    mine = lambda full: lax.dynamic_slice_in_dim(full, (context * members + member) * each, each, 0)
    norm_gain_1_grad = (
        jnp.sum(mine(query_full).astype(jnp.float32) * query_weight_grad, axis=1)
        + jnp.sum(mine(kv_full).astype(jnp.float32) * kv_sum, axis=1)
    ) / mine(gain_one)

    line_zero = flip((line_sums[1].astype(jnp.float32) + nothing(sum_three)).astype(jnp.bfloat16), "ctx", 1)
    sum_zero = line_sums[0].astype(jnp.float32) + line_zero.astype(jnp.float32)
    expert_sums = [sum_zero, sum_one, sum_two, sum_three]
    expert_gate_grad = jnp.stack([total[0] for total in expert_sums]).astype(jnp.float32)
    expert_up_grad = jnp.stack([total[1] for total in expert_sums]).astype(jnp.float32)
    expert_down_grad = jnp.stack([total[2].T for total in expert_sums]).astype(jnp.float32)

    shared_sum = line_sum(side_sum(pair_keep, after(other_pair, kv_sides[1])), context)
    shared_sum = shared_sum.reshape(3, members, each, hidden_share).transpose(1, 0, 2, 3)
    shared_sum = lax.all_to_all(shared_sum, "wa", 0, 0, tiled=True)
    shared_gate_grad = shared_sum[:, 0].transpose(1, 0, 2).reshape(each, members * hidden_share)
    shared_up_grad = shared_sum[:, 1].transpose(1, 0, 2).reshape(each, members * hidden_share)
    shared_down_grad = shared_sum[:, 2].transpose(0, 2, 1).reshape(members * hidden_share, each)
    return (
        block_out,
        tokens_grad,
        norm_gain_1_grad,
        query_weight_grad,
        key_weight_grad,
        value_weight_grad,
        out_weight_grad,
        norm_gain_2_grad,
        router_weight_grad,
        shared_gate_grad,
        shared_up_grad,
        shared_down_grad,
        expert_gate_grad,
        expert_up_grad,
        expert_down_grad,
    )


def solution(mesh):
    return jax.shard_map(
        shards,
        mesh=mesh,
        in_specs=(
            P("wa", "ctx", None, None, None),
            P("wa", None),
            P("wa", "ctx", None, None, None),
            P("wa"),
            P("wa", None),
            P("wa", None),
            P("wa", None),
            P(None, "wa"),
            P("wa"),
            P("wa", None),
            P("wa", None),
            P("wa", None),
            P(None, "wa"),
            P("wa", None, None),
            P("wa", None, None),
            P("wa", None, None),
            P("wa", "ctx", None, None, None),
        ),
        out_specs=(
            P("wa", "ctx", None, None, None),
            P("wa", "ctx", None, None, None),
            P(("ctx", "wa")),
            P(("ctx", "wa"), None),
            P(("ctx", "wa"), None),
            P(("ctx", "wa"), None),
            P(None, ("ctx", "wa")),
            P(("ctx", "wa")),
            P(("ctx", "wa"), None),
            P(("ctx", "wa"), None),
            P(("ctx", "wa"), None),
            P(None, ("ctx", "wa")),
            P("wa", "ctx", None),
            P("wa", "ctx", None),
            P("wa", None, "ctx"),
        ),
        check_vma=False,
    )
```

```python
import functools

import jax
import jax.numpy as jnp
from jax import lax
from jax.experimental import pallas as pl
from jax.experimental.pallas import tpu as pltpu
from jax.sharding import PartitionSpec as P

QUERY_HEADS = 12
KEY_VALUE_HEADS = 4
HEAD_DIM = 128
TOP = 6
EXPERTS = 16

epsilon = 1e-05
large_negative = -1e30
highest = lax.Precision.HIGHEST
ORDER = (0, 2, 1, 3)


def dot32(left, right, dims=None):
    if dims is None:
        return jnp.dot(left, right, preferred_element_type=jnp.float32)
    return lax.dot_general(left, right, (dims, ((), ())), preferred_element_type=jnp.float32)


def flip(value, axis, bits):
    count = lax.axis_size(axis)
    return lax.ppermute(value, axis, [(i, i ^ bits) for i in range(count)])


def shift(value, steps):
    count = lax.axis_size("ctx")
    return lax.ppermute(value, "ctx", [(i, (i + 2 * steps) % count) for i in range(count)])


def after(value, *earlier):
    return lax.optimization_barrier((value,) + earlier)[0]


def gather_pieces(value):
    across = flip(value, "wa", 2)
    return [value, across, flip(value, "wa", 1), flip(across, "wa", 1)]


def ordered(pieces, index):
    chip, core = index // 2, index % 2
    near = [jnp.where(core == i, pieces[0], pieces[2]) for i in range(2)]
    far = [jnp.where(core == i, pieces[1], pieces[3]) for i in range(2)]
    return jnp.concatenate(
        [jnp.where(chip == i // 2, near[i % 2], far[i % 2]) for i in range(4)], axis=0
    )


def exchange(pieces, index):
    received = []
    for bits in ORDER:
        piece = lax.dynamic_index_in_dim(pieces, index ^ bits, 0, keepdims=False)
        received.append(piece if bits == 0 else flip(piece, "wa", bits))
    return received


def reduce_rows(keep, send, kind):
    near = keep + flip(send, "wa", 1).astype(jnp.float32)
    quarter = keep.shape[0] // 2
    return near[:quarter] + flip(near[quarter:].astype(kind), "wa", 2).astype(jnp.float32)


def scatter_small(value):
    rows, width = value.shape
    contexts, members = lax.axis_size("ctx"), lax.axis_size("wa")
    each = width // (contexts * members)
    spread = value.reshape(rows, contexts, members, each).transpose(2, 0, 1, 3)
    spread = spread.reshape(members, rows, contexts * each)
    first = jnp.sum(lax.all_to_all(spread, "wa", 0, 0, tiled=True), axis=0)
    second = first.reshape(rows, contexts, each).transpose(1, 0, 2)
    return jnp.sum(lax.all_to_all(second, "ctx", 0, 0, tiled=True), axis=0)


def sides():
    count = lax.axis_size("ctx")
    return [list(range(side, count, 2)) for side in range(2)]


def to_side(value, index):
    pairs = value.reshape((value.shape[0] // 2, 2) + value.shape[1:])
    keep = lax.dynamic_index_in_dim(pairs, index % 2, 1, keepdims=False)
    return keep, flip(lax.dynamic_index_in_dim(pairs, 1 - index % 2, 1, keepdims=False), "ctx", 1)


def line_sum(near, index, *before):
    lines, line = near.shape[0], index // 2
    low = near.astype(jnp.bfloat16)
    total = lax.dynamic_index_in_dim(near, line, 0, keepdims=False)
    for steps in range(1, lines):
        piece = lax.dynamic_index_in_dim(low, (line + lines - steps) % lines, 0, keepdims=False)
        total = total + after(shift(piece, -steps), *before).astype(jnp.float32)
    return total


def scatter_lines(value):
    return lax.psum_scatter(
        value, "ctx", scatter_dimension=0, axis_index_groups=sides(), tiled=True
    )[0]


def silu_parts(values):
    sigmoid_of = jax.nn.sigmoid(values)
    return (values * sigmoid_of, sigmoid_of * (1.0 + values * (1.0 - sigmoid_of)))


def rms_back(grad_normed, normed, inverse, gain_values):
    scaled = grad_normed * gain_values
    return (
        jnp.sum(grad_normed * normed, axis=0),
        inverse * (scaled - normed * jnp.mean(scaled * normed, axis=-1, keepdims=True)),
    )


TOGETHER = 3


def attention_masks(starts_ref, block, half_rows, shape):
    rows = block * half_rows + lax.broadcasted_iota(jnp.int32, shape, 0) % half_rows
    first = jnp.zeros(shape, jnp.int32)
    for document in range(1, starts_ref.shape[0]):
        start = starts_ref[document]
        first = jnp.where(start <= rows, jnp.maximum(first, start), first)
    return first, rows


def block_bounds(starts_ref, block, half_rows):
    top = block * half_rows
    first = jnp.int32(0)
    for document in range(1, starts_ref.shape[0]):
        start = starts_ref[document]
        first = jnp.where(start <= top, jnp.maximum(first, start), first)
    return first // half_rows


def block_place(block, own, contexts):
    late = (block >= contexts).astype(jnp.int32)
    device = jnp.where(block < contexts, block, 2 * contexts - 1 - block)
    lines = contexts // 2
    behind = own // 2 - device // 2
    behind = jnp.where(behind < 0, behind + lines, behind)
    return (((own + device) % 2) * lines + behind) * 2 + late


def attention_forward_kernel(starts_ref, own_ref, q_ref, kv_ref, o_ref, lse_ref, s_ref):
    blocks, half_rows, _ = kv_ref.shape
    contexts = blocks // 2
    ratio = q_ref.shape[1] // HEAD_DIM
    rows = ratio * half_rows
    scale = HEAD_DIM ** (-0.5)
    for half in range(2):
        block = own_ref[0] if half == 0 else blocks - 1 - own_ref[0]
        queries = jnp.concatenate(
            [
                q_ref[half * half_rows : (half + 1) * half_rows, h * HEAD_DIM : (h + 1) * HEAD_DIM]
                for h in range(ratio)
            ],
            axis=0,
        )
        low = block_bounds(starts_ref, block, half_rows)
        first, position = attention_masks(starts_ref, block, half_rows, (rows, half_rows))
        column = lax.broadcasted_iota(jnp.int32, (rows, half_rows), 1)

        trips = (block - low + TOGETHER) // TOGETHER

        def score_step(trip, running):
            for part in range(TOGETHER):
                step = trip * TOGETHER + part
                place = block_place(jnp.minimum(low + step, block), own_ref[0], contexts)
                scores = dot32(queries, kv_ref[place, :, :HEAD_DIM], ((1,), (1,))) * scale
                at = column + (low + step) * half_rows
                scores = jnp.where((at >= first) & (at <= position), scores, large_negative)
                s_ref[step] = scores
                running = jnp.maximum(running, scores)
            return running

        running = lax.fori_loop(
            0, trips, score_step, jnp.full((rows, half_rows), large_negative, jnp.float32)
        )
        row_max = jnp.max(running, axis=1, keepdims=True)

        def sum_step(trip, total):
            for part in range(TOGETHER):
                step = trip * TOGETHER + part
                expo = jnp.exp(s_ref[step] - row_max)
                s_ref[step] = expo
                total = total + expo
            return total

        total = lax.fori_loop(0, trips, sum_step, jnp.zeros((rows, half_rows), jnp.float32))
        row_sum = jnp.sum(total, axis=1, keepdims=True)
        inverse = 1.0 / row_sum

        def value_step(trip, accum):
            for part in range(TOGETHER):
                step = trip * TOGETHER + part
                place = block_place(jnp.minimum(low + step, block), own_ref[0], contexts)
                weights = (s_ref[step] * inverse).astype(jnp.bfloat16)
                accum = accum + dot32(weights, kv_ref[place, :, HEAD_DIM:])
            return accum

        accum = lax.fori_loop(0, trips, value_step, jnp.zeros((rows, HEAD_DIM), jnp.float32))
        log_sum = row_max + jnp.log(row_sum)
        lse_ref[0, half] = jnp.broadcast_to(log_sum, (rows, half_rows))
        for h in range(ratio):
            o_ref[half * half_rows : (half + 1) * half_rows, h * HEAD_DIM : (h + 1) * HEAD_DIM] = (
                accum[h * half_rows : (h + 1) * half_rows].astype(jnp.bfloat16)
            )


def attention_forward(starts, own, queries, kv):
    rows, width = queries.shape
    blocks, half_rows, _ = kv.shape
    ratio = QUERY_HEADS // KEY_VALUE_HEADS
    stacked = ratio * half_rows
    kv_spec = pl.BlockSpec((blocks, half_rows, 2 * HEAD_DIM), lambda g, *_: (0, 0, g))
    q_spec = pl.BlockSpec((rows, ratio * HEAD_DIM), lambda g, *_: (0, g))
    return pl.pallas_call(
        attention_forward_kernel,
        grid_spec=pltpu.PrefetchScalarGridSpec(
            num_scalar_prefetch=2,
            grid=(KEY_VALUE_HEADS,),
            in_specs=[q_spec, kv_spec],
            out_specs=[
                q_spec,
                pl.BlockSpec((1, 2, stacked, half_rows), lambda g, *_: (g, 0, 0, 0)),
            ],
            scratch_shapes=[pltpu.VMEM((blocks + TOGETHER - 1, stacked, half_rows), jnp.float32)],
        ),
        out_shape=(
            jax.ShapeDtypeStruct((rows, width), jnp.bfloat16),
            jax.ShapeDtypeStruct((KEY_VALUE_HEADS, 2, stacked, half_rows), jnp.float32),
        ),
        compiler_params=pltpu.CompilerParams(vmem_limit_bytes=48 << 20),
        cost_estimate=pl.CostEstimate(flops=0, bytes_accessed=1 << 20, transcendentals=0),
        name="attention_forward",
    )(starts, own, queries, kv)


def attention_backward_kernel(
    starts_ref, own_ref, q_ref, do_ref, kv_ref, lse_ref, dq_ref, keep_ref, send_ref, p_ref, dp_ref, dka_ref, dva_ref
):
    blocks, half_rows, _ = kv_ref.shape
    contexts = blocks // 2
    ratio = q_ref.shape[1] // HEAD_DIM
    rows = ratio * half_rows
    scale = HEAD_DIM ** (-0.5)
    dka_ref[...] = jnp.zeros_like(dka_ref)
    dva_ref[...] = jnp.zeros_like(dva_ref)

    def stack(ref, half):
        return jnp.concatenate(
            [
                ref[half * half_rows : (half + 1) * half_rows, h * HEAD_DIM : (h + 1) * HEAD_DIM]
                for h in range(ratio)
            ],
            axis=0,
        )

    for half in range(2):
        block = own_ref[0] if half == 0 else blocks - 1 - own_ref[0]
        queries = stack(q_ref, half)
        grads = stack(do_ref, half)
        log_sum = lse_ref[0, half]
        low = block_bounds(starts_ref, block, half_rows)
        first, position = attention_masks(starts_ref, block, half_rows, (rows, half_rows))
        column = lax.broadcasted_iota(jnp.int32, (rows, half_rows), 1)

        trips = (block - low + TOGETHER) // TOGETHER

        def prob_step(trip, running):
            for part in range(TOGETHER):
                step = trip * TOGETHER + part
                place = block_place(jnp.minimum(low + step, block), own_ref[0], contexts)
                scores = dot32(queries, kv_ref[place, :, :HEAD_DIM], ((1,), (1,))) * scale
                at = column + (low + step) * half_rows
                probs = jnp.where(
                    (at >= first) & (at <= position), jnp.exp(scores - log_sum), 0.0
                )
                prob_grads = dot32(grads, kv_ref[place, :, HEAD_DIM:], ((1,), (1,)))
                p_ref[step] = probs
                dp_ref[step] = prob_grads
                running = running + probs * prob_grads
            return running

        running = lax.fori_loop(0, trips, prob_step, jnp.zeros((rows, half_rows), jnp.float32))
        delta = jnp.sum(running, axis=1, keepdims=True)

        def grad_step(trip, query_grad):
            for part in range(TOGETHER):
                step = trip * TOGETHER + part
                place = block_place(jnp.minimum(low + step, block), own_ref[0], contexts)
                probs = p_ref[step]
                score_low = (probs * (dp_ref[step] - delta)).astype(jnp.bfloat16)
                dka_ref[place] += dot32(score_low, queries, ((0,), (0,)))
                dva_ref[place] += dot32(probs.astype(jnp.bfloat16), grads, ((0,), (0,)))
                query_grad = query_grad + dot32(score_low, kv_ref[place, :, :HEAD_DIM])
            return query_grad

        query_grad = lax.fori_loop(0, trips, grad_step, jnp.zeros((rows, HEAD_DIM), jnp.float32))
        for h in range(ratio):
            dq_ref[half * half_rows : (half + 1) * half_rows, h * HEAD_DIM : (h + 1) * HEAD_DIM] = (
                query_grad[h * half_rows : (h + 1) * half_rows] * scale
            ).astype(jnp.bfloat16)
    for out_ref, places in ((keep_ref, slice(0, contexts)), (send_ref, slice(contexts, blocks))):
        out_ref[:, :, :HEAD_DIM] = (dka_ref[places] * scale).astype(jnp.bfloat16)
        out_ref[:, :, HEAD_DIM:] = dva_ref[places].astype(jnp.bfloat16)


def attention_backward(starts, own, queries, grads, kv, log_sums):
    rows, width = queries.shape
    blocks, half_rows, kv_width = kv.shape
    ratio = QUERY_HEADS // KEY_VALUE_HEADS
    stacked = ratio * half_rows
    kv_spec = pl.BlockSpec((blocks, half_rows, 2 * HEAD_DIM), lambda g, *_: (0, 0, g))
    part_spec = pl.BlockSpec((blocks // 2, half_rows, 2 * HEAD_DIM), lambda g, *_: (0, 0, g))
    q_spec = pl.BlockSpec((rows, ratio * HEAD_DIM), lambda g, *_: (0, g))
    return pl.pallas_call(
        attention_backward_kernel,
        grid_spec=pltpu.PrefetchScalarGridSpec(
            num_scalar_prefetch=2,
            grid=(KEY_VALUE_HEADS,),
            in_specs=[
                q_spec,
                q_spec,
                kv_spec,
                pl.BlockSpec((1, 2, stacked, half_rows), lambda g, *_: (g, 0, 0, 0)),
            ],
            out_specs=[q_spec, part_spec, part_spec],
            scratch_shapes=[
                pltpu.VMEM((blocks + TOGETHER - 1, stacked, half_rows), jnp.float32),
                pltpu.VMEM((blocks + TOGETHER - 1, stacked, half_rows), jnp.float32),
                pltpu.VMEM((blocks, half_rows, HEAD_DIM), jnp.float32),
                pltpu.VMEM((blocks, half_rows, HEAD_DIM), jnp.float32),
            ],
        ),
        out_shape=(
            jax.ShapeDtypeStruct((rows, width), jnp.bfloat16),
            jax.ShapeDtypeStruct((blocks // 2, half_rows, kv_width), jnp.bfloat16),
            jax.ShapeDtypeStruct((blocks // 2, half_rows, kv_width), jnp.bfloat16),
        ),
        compiler_params=pltpu.CompilerParams(vmem_limit_bytes=58 << 20),
        cost_estimate=pl.CostEstimate(flops=0, bytes_accessed=1 << 20, transcendentals=0),
        name="attention_backward",
    )(starts, own, queries, grads, kv, log_sums)


def experts_kernel(final, *refs):
    at_ref, *refs = refs
    parts, refs = refs[:8], refs[8:]
    g_ref, wg_ref, wu_ref, wd_ref, *refs = refs
    if final:
        shared_ref, out_in, dx_in, dg_in, *refs = refs
        out_hbm, dx_hbm, out_low_ref, dx_low_ref, dg_ref, *refs = refs
        targets = ((refs[0], refs[1]), (refs[2], refs[3]))
        pair_target, refs = (refs[4], refs[5]), refs[6:]
        x_ref, dy_ref, he_ref, da_ref, db_ref, out_ref, dx_ref, sem = refs
    else:
        out_hbm, dx_hbm, dg_ref, line_hbm, *refs = refs
        x_ref, dy_ref, he_ref, da_ref, db_ref, out_ref, dx_ref, line_ref, sem = refs[2:]
        targets = (line_ref, (refs[0], refs[1]))
        line_copy = pltpu.make_async_copy(line_ref, line_hbm, sem.at[19])
    local = pl.program_id(0)
    expert = at_ref[0] + local
    side = at_ref[1]
    total_rows, width = x_ref.shape
    half = total_rows // 2
    step_rows = total_rows // 4
    tall = 384

    def loads(number):
        rows = pl.ds(number * step_rows, step_rows)
        moves = [(parts[number], x_ref.at[rows, :]), (parts[4 + number], dy_ref.at[rows, :])]
        if final:
            moves += [(out_in.at[rows, :], out_ref.at[rows, :]), (dx_in.at[rows, :], dx_ref.at[rows, :])]
            if number == 0:
                moves.append((dg_in, dg_ref))
        return [
            pltpu.make_async_copy(source, target, sem.at[number * 5 + place])
            for place, (source, target) in enumerate(moves)
        ]

    def results(number, count):
        rows = pl.ds(number * count, count)
        return [
            pltpu.make_async_copy(ref.at[rows, :], hbm.at[rows, :], sem.at[number * 2 + place])
            for place, (ref, hbm) in enumerate(((out_ref, out_hbm), (dx_ref, dx_hbm)))
        ]

    @pl.when(local == 0)
    def _():
        for number in range(4):
            for copy in loads(number):
                copy.start()
        if not final:
            for ref in (out_ref, dx_ref, dg_ref):
                ref[...] = jnp.zeros_like(ref)

    def add(number, rows, value):
        (out_ref, dx_ref)[number][rows, :] += value

    def store_sides(lows, begin, pair):
        per = pair[0].shape[2]
        for parity in range(2):

            @pl.when(side == parity)
            def _():
                for part in range(tall // per):
                    line = begin // (2 * per) + part // 2
                    for number, low in enumerate(lows):
                        pair[(part + parity) % 2][line, number] = low[part * per : (part + 1) * per]

    def store_lines(lows, begin, target):
        per = target.shape[3]
        for part in range(tall // per):
            line = begin // (2 * per) + part // 2
            for number, low in enumerate(lows):
                target[line, (side + part) % 2, number] = low[part * per : (part + 1) * per]

    for number in range(4):
        rows = slice(number * step_rows, (number + 1) * step_rows)

        @pl.when(local == 0)
        def _():
            for copy in loads(number):
                copy.wait()

        x = x_ref[rows, :]
        lane = lax.broadcasted_iota(jnp.int32, (step_rows, g_ref.shape[1]), 1)
        mine = lane == expert
        gate = jnp.sum(jnp.where(mine, g_ref[rows, :], 0.0), axis=1, keepdims=True)
        pre = dot32(x, wg_ref[0])
        up = dot32(x, wu_ref[0])
        back = dot32(dy_ref[rows, :], wd_ref[0], ((1,), (1,)))
        silu, slope = silu_parts(pre)
        hidden = (silu * up).astype(jnp.bfloat16).astype(jnp.float32)
        dg_ref[rows, :] += jnp.where(mine, jnp.sum(hidden * back, axis=1, keepdims=True), 0.0)
        hidden_low = (gate * hidden).astype(jnp.bfloat16)
        he_ref[rows, :] = hidden_low
        add(0, rows, dot32(hidden_low, wd_ref[0]))
        back = gate * back
        pre_low = (back * up * slope).astype(jnp.bfloat16)
        up_low = (back * silu).astype(jnp.bfloat16)
        da_ref[rows, :] = pre_low
        db_ref[rows, :] = up_low
        add(1, rows, dot32(pre_low, wg_ref[0], ((1,), (1,))) + dot32(up_low, wu_ref[0], ((1,), (1,))))
        if not final:

            @pl.when(local == 1)
            def _():
                for copy in results(number, step_rows):
                    copy.start()

    @pl.loop(0, width // tall)
    def _(step):
        begin = pl.multiple_of(step * tall, tall)
        columns = pl.ds(begin, tall)
        lows = [
            dot32(left[:, columns], right[...], ((0,), (0,))).astype(jnp.bfloat16)
            for left, right in ((x_ref, da_ref), (x_ref, db_ref), (dy_ref, he_ref))
        ]
        for number, target in enumerate(targets):

            @pl.when(local == number)
            def _():
                if isinstance(target, tuple):
                    store_sides(lows, begin, target)
                else:
                    store_lines(lows, begin, target)

    if not final:

        @pl.when(local == 0)
        def _():
            line_copy.start()

        @pl.when(local == 1)
        def _():
            line_copy.wait()
            for number in range(4):
                for copy in results(number, step_rows):
                    copy.wait()

        return

    @pl.when(local == pl.num_programs(0) - 1)
    def _():
        shared = shared_ref.shape[1] // 3
        pair_w, down_w = slice(0, 2 * shared), slice(2 * shared, 3 * shared)
        for begin in range(0, total_rows, step_rows):
            rows = slice(begin, begin + step_rows)
            both = dot32(x_ref[rows, :], shared_ref[:, pair_w])
            pre, up = both[:, :shared], both[:, shared:]
            silu, slope = silu_parts(pre)
            hidden = (silu * up).astype(jnp.bfloat16)
            he_ref[rows, :shared] = hidden
            add(0, rows, dot32(hidden, shared_ref[:, down_w], ((1,), (1,))))
            back = dot32(dy_ref[rows, :], shared_ref[:, down_w])
            da_ref[rows, :shared] = (back * up * slope).astype(jnp.bfloat16)
            da_ref[rows, shared:] = (back * silu).astype(jnp.bfloat16)
            add(1, rows, dot32(da_ref[rows, :], shared_ref[:, pair_w], ((1,), (1,))))
        for copy in results(0, half):
            copy.start()
        out_low_ref[...] = out_ref[half:, :].astype(jnp.bfloat16)
        dx_low_ref[...] = dx_ref[half:, :].astype(jnp.bfloat16)

        @pl.loop(0, width // tall)
        def _(step):
            begin = pl.multiple_of(step * tall, tall)
            columns = pl.ds(begin, tall)
            pair_low = dot32(x_ref[:, columns], da_ref[...], ((0,), (0,))).astype(jnp.bfloat16)
            down_low = dot32(dy_ref[:, columns], he_ref[:, :shared], ((0,), (0,))).astype(jnp.bfloat16)
            store_sides((pair_low[:, :shared], pair_low[:, shared:], down_low), begin, pair_target)

        for copy in results(0, half):
            copy.wait()


def experts_call(at, x, dy, gates, weights, first, contexts, shared_w=None, carried=()):
    final = shared_w is not None
    gate_w, up_w, down_w = weights
    rows, width = 4 * x[0].shape[0], x[0].shape[1]
    hidden = gate_w.shape[2]
    per, lines, half = width // contexts, contexts // 2, rows // 2
    once = pl.Buffered(1)
    whole = lambda shape: pl.BlockSpec(shape, lambda e, *_: (0,) * len(shape), pipeline_mode=once)
    weight = lambda shape: pl.BlockSpec((1,) + shape, lambda e, *_: (first + e, 0, 0))
    apart = pl.BlockSpec(memory_space=pl.ANY)
    part = jax.ShapeDtypeStruct((half, width), jnp.float32)
    low = jax.ShapeDtypeStruct((half, width), jnp.bfloat16)
    full = jax.ShapeDtypeStruct((rows, width), jnp.float32)
    table = jax.ShapeDtypeStruct((rows, EXPERTS), jnp.float32)
    term = jax.ShapeDtypeStruct((lines, 3, per, hidden), jnp.bfloat16)
    both = jax.ShapeDtypeStruct((lines, 2, 3, per, hidden), jnp.bfloat16)
    scratch = [pltpu.VMEM((rows, width), jnp.bfloat16)] * 2 + [pltpu.VMEM((rows, hidden), jnp.bfloat16)] * 3
    scratch += [pltpu.VMEM((rows, width), jnp.float32)] * 2
    if final:
        shared = shared_w.shape[1] // 3
        pair = jax.ShapeDtypeStruct((lines, 3, per, shared), jnp.bfloat16)
        extra_specs = [whole(shared_w.shape)] + [apart] * 3
        out_shape = (part, part, low, low, table, term, term, term, term, pair, pair)
        outside = (0, 1)
    else:
        shared = 0
        extra_specs = []
        out_shape = (full, full, table, both, term, term)
        outside = (0, 1, 3)
        scratch.append(pltpu.VMEM(both.shape, jnp.bfloat16))
    return pl.pallas_call(
        functools.partial(experts_kernel, final),
        grid_spec=pltpu.PrefetchScalarGridSpec(
            num_scalar_prefetch=1,
            grid=(2,),
            in_specs=[apart] * 8
            + [
                whole((rows, EXPERTS)),
                weight((width, hidden)),
                weight((width, hidden)),
                weight((hidden, width)),
            ]
            + extra_specs,
            out_specs=[apart if place in outside else whole(item.shape) for place, item in enumerate(out_shape)],
            scratch_shapes=scratch + [pltpu.SemaphoreType.DMA((20,))],
        ),
        out_shape=out_shape,
        compiler_params=pltpu.CompilerParams(vmem_limit_bytes=60 << 20),
        cost_estimate=pl.CostEstimate(flops=0, bytes_accessed=1 << 20, transcendentals=0),
        name="experts_final" if final else "experts",
    )(at, *x, *dy, gates, gate_w, up_w, down_w, *((shared_w,) if final else ()), *carried)


def dense_gates(logits, routes):
    chosen = jnp.any(
        routes[:, :, None] == jnp.arange(EXPERTS, dtype=jnp.int32)[None, None, :], axis=1
    )
    top = jnp.max(jnp.where(chosen, logits, large_negative), axis=-1, keepdims=True)
    expo = jnp.where(chosen, jnp.exp(logits - top), 0.0)
    return expo / jnp.sum(expo, axis=-1, keepdims=True)


def shards(
    tokens, doc_starts, routes, norm_gain_1, query_weight, key_matrix, value_matrix, out_weight,
    norm_gain_2, router_weight, shared_gate, shared_up, shared_down, expert_gate, expert_up,
    expert_down, out_grad,
):
    contexts, members = lax.axis_size("ctx"), lax.axis_size("wa")
    context, member = lax.axis_index("ctx"), lax.axis_index("wa")
    half_rows, width = tokens.shape[3], tokens.shape[4]
    rows = 2 * half_rows
    share = width // members
    each = share // contexts
    lines = contexts // 2
    kv_width = 2 * key_matrix.shape[1]
    starts = doc_starts[0]
    own = context[None].astype(jnp.int32)
    inputs = tokens.reshape(rows, width).astype(jnp.float32)
    grad_low = out_grad.reshape(rows, width)
    grad_rows = grad_low.astype(jnp.float32)

    beside = lambda k, v: jnp.stack(
        [k.reshape(-1, KEY_VALUE_HEADS, HEAD_DIM), v.reshape(-1, KEY_VALUE_HEADS, HEAD_DIM)], axis=2
    ).reshape(-1, kv_width)
    apart = lambda kv: jnp.moveaxis(
        kv.reshape(-1, KEY_VALUE_HEADS, 2, HEAD_DIM), 2, 0
    ).reshape(2, -1, kv_width // 2)
    small = jnp.concatenate([router_weight, norm_gain_1[:, None], norm_gain_2[:, None]], axis=1)
    small = jnp.pad(small, ((0, 0), (0, 128 - EXPERTS - 2)))
    kv_pieces = gather_pieces(jnp.concatenate([beside(key_matrix, value_matrix), small], axis=1))
    kv_across = kv_pieces[1]
    kv_full = ordered(kv_pieces, member)
    router_full = kv_full[:, kv_width : kv_width + EXPERTS]
    gain_one = kv_full[:, kv_width + EXPERTS].astype(jnp.float32)
    gain_two = kv_full[:, kv_width + EXPERTS + 1].astype(jnp.float32)
    kv_full = kv_full[:, :kv_width]
    query_full = lax.all_gather(after(query_weight, kv_across), "wa", axis=0, tiled=True)
    out_full = lax.all_gather(after(out_weight, kv_across), "wa", axis=0, tiled=False)

    inverse_one = lax.rsqrt(jnp.mean(inputs * inputs, axis=-1, keepdims=True) + epsilon)
    normed_one = inputs * inverse_one
    normed_low = (normed_one * gain_one).astype(jnp.bfloat16)
    kv_own = dot32(normed_low, kv_full).astype(jnp.bfloat16).reshape(2, half_rows, kv_width)
    ring, other = [kv_own], []
    for step in range(lines - 1):
        ring.append(shift(after(ring[-1], *other), 1))
        other.append(flip(ring[step], "ctx", 1))
    other.append(flip(ring[-1], "ctx", 1))
    kv_all = jnp.concatenate(ring + other, axis=0)
    queries = dot32(normed_low, query_full).astype(jnp.bfloat16)

    hidden_share = shared_gate.shape[1] // members
    routes_all = jnp.concatenate(gather_pieces(after(routes.reshape(rows, TOP), ring[1])), axis=0)
    grad_pieces = gather_pieces(after(grad_low, ring[1]))
    queries = after(queries, routes_all)
    shared_w = jnp.concatenate(
        [
            shared_gate.reshape(share, members, hidden_share),
            shared_up.reshape(share, members, hidden_share),
            shared_down.T.reshape(share, members, hidden_share),
        ],
        axis=2,
    ).transpose(1, 0, 2)
    shared_w = lax.all_to_all(after(shared_w, ring[-1]), "wa", 0, 0, tiled=True)
    shared_w = shared_w.reshape(width, 3 * hidden_share)
    by_share = lambda value: value.reshape(rows, contexts, members, each).transpose(2, 0, 1, 3).reshape(
        members, rows, share
    )

    attended, log_sums = attention_forward(starts, own, queries, kv_all)
    mixed = jnp.concatenate([dot32(attended, out_full[m]) for m in range(members)], axis=1)
    residual = inputs + mixed
    inverse_two = lax.rsqrt(jnp.mean(residual * residual, axis=-1, keepdims=True) + epsilon)
    normed_two = residual * inverse_two
    second_low = after((normed_two * gain_two).astype(jnp.bfloat16), shared_w, *grad_pieces)

    second_pieces = gather_pieces(second_low)
    logits = jnp.concatenate([dot32(piece, router_full) for piece in second_pieces], axis=0)
    gates_all = dense_gates(logits, routes_all)
    attended_across = flip(after(attended, second_pieces[3]), "wa", 2)
    local = expert_gate.shape[0]
    weights = (expert_gate, expert_up, expert_down)
    at = lambda first: jnp.stack([member * local + first, context % 2]).astype(jnp.int32)
    *carried, line_terms, keep_one, send_one = experts_call(
        at(0), second_pieces, grad_pieces, gates_all, weights, 0, contexts
    )
    line_sums = scatter_lines(line_terms)
    other_one = flip(send_one, "ctx", 1)
    (
        out_keep, dx_keep, out_send, dx_send, gate_back,
        keep_two, send_two, keep_three, send_three, pair_keep, pair_send,
    ) = experts_call(
        at(2), second_pieces, grad_pieces, gates_all, weights, 2, contexts, shared_w, carried
    )
    other_two = flip(send_two, "ctx", 1)

    def nothing(arrived):
        return 0.0 * arrived[(0,) * arrived.ndim].astype(jnp.float32)

    def side_sum(keep, received):
        return keep.astype(jnp.float32) + received.astype(jnp.float32)

    dx_near = dx_keep + flip(after(dx_send, other_one, attended_across), "wa", 1).astype(jnp.float32)
    dx_moved = flip(dx_near[rows:].astype(jnp.bfloat16), "wa", 2)
    other_three = flip(after(send_three, dx_moved), "ctx", 1)
    dx_own = dx_near[:rows] + after(dx_moved, other_two).astype(jnp.float32)
    half = 2 * rows
    gate_back = reduce_rows(gate_back[:half], gate_back[half:], jnp.float32)

    gates = gates_all[:rows]
    logit_grad = gates * (gate_back - jnp.sum(gates * gate_back, axis=-1, keepdims=True))
    router_term = lax.dot_general(
        logit_grad, second_low.astype(jnp.float32), (((0,), (0,)), ((), ())), precision=highest
    )
    second_grad = dx_own + jnp.dot(logit_grad, router_full.astype(jnp.float32).T, precision=highest)
    gain_two_term, residual_back = rms_back(second_grad, normed_two, inverse_two, gain_two)
    residual_grad = grad_rows + residual_back
    mix_low = residual_grad.astype(jnp.bfloat16)

    attended_grad = sum(
        dot32(mix_low[:, m * share : (m + 1) * share], out_full[m], ((1,), (1,)))
        for m in range(members)
    ).astype(jnp.bfloat16)
    small_terms = jnp.concatenate([router_term, gain_two_term[None]], axis=0)
    small_terms = jnp.pad(small_terms, ((0, 128 - small_terms.shape[0]), (0, 0)))
    small_terms = small_terms.reshape(-1, contexts, members, each).transpose(2, 0, 1, 3)
    small_terms = small_terms.reshape(members, -1, share).astype(jnp.bfloat16)
    near_one = side_sum(keep_one, after(other_one, dx_moved)) + nothing(line_sums)
    near_one = near_one.astype(jnp.bfloat16)
    sum_one = scatter_lines(near_one)
    attended_grad = after(attended_grad, near_one)
    query_low, kv_keep, kv_send = attention_backward(starts, own, queries, attended_grad, kv_all, log_sums)
    by_line = lambda parts: parts.reshape(lines, rows, kv_width)
    query_across = flip(query_low, "wa", 2)
    bundle = jnp.concatenate([by_share(mix_low), by_share(normed_low), small_terms], axis=1)
    bundle = exchange(after(bundle, query_low), member)
    attended_core = flip(after(jnp.concatenate([attended, attended_across], axis=0), query_low), "wa", 1)
    query_core = flip(jnp.concatenate([query_low, query_across], axis=0), "wa", 1)
    moved = bundle[1:] + [attended_core, query_core]
    near_two = (side_sum(keep_two, after(other_two, query_low)) + nothing(sum_one)).astype(jnp.bfloat16)
    sum_two = scatter_lines(near_two)
    kv_send = after(by_line(kv_send), other_three, *moved)
    received = flip(kv_send, "ctx", 1)
    out_core = flip(after(out_send, query_core), "wa", 1)
    out_near = out_keep + out_core.astype(jnp.float32)
    out_moved = flip(out_near[rows:].astype(jnp.bfloat16), "wa", 2)
    out_own = out_near[:rows] + out_moved.astype(jnp.float32)
    block_out = (residual + out_own).astype(jnp.bfloat16).reshape(tokens.shape)
    near_three = side_sum(keep_three, after(other_three, out_core)) + 0.0 * near_two[0, 0, 0, 0].astype(jnp.float32)
    near_three = near_three.astype(jnp.bfloat16)
    sum_three = scatter_lines(near_three)
    received = after(received, near_three)
    kv_near = by_line(kv_keep).astype(jnp.float32) + received.astype(jnp.float32)
    kv_parts = kv_near.astype(jnp.bfloat16)
    kv_moved = [shift(kv_parts[steps], -steps) for steps in range(1, lines)]
    stacked = lambda pieces: jnp.concatenate(pieces, axis=0)
    mix_share = stacked([piece[:rows] for piece in bundle])
    normed_share = stacked([piece[rows : 2 * rows] for piece in bundle])
    small_share = sum(piece[2 * rows :].astype(jnp.float32) for piece in bundle)
    query_all = stacked([query_low, query_across, query_core])
    attended_all = stacked([attended, attended_across, attended_core])
    early_term = jnp.concatenate(
        [
            dot32(normed_share, query_all, ((0,), (0,))),
            dot32(mix_share, attended_all, ((0,), (0,))),
            small_share.T,
        ],
        axis=1,
    ).astype(jnp.bfloat16)
    early_sides = to_side(after(early_term.reshape(contexts, each, -1), kv_parts), context)
    other_pair = flip(after(pair_send, kv_parts), "ctx", 1)
    kv_moved[0] = after(kv_moved[0], early_sides[1], out_moved)
    kv_low = (kv_near[0] + sum(moved.astype(jnp.float32) for moved in kv_moved)).astype(jnp.bfloat16)

    kv_across = flip(kv_low, "wa", 2)
    kv_pair = jnp.concatenate([kv_low, kv_across], axis=0)
    kv_low_all = jnp.concatenate([kv_pair, flip(kv_pair, "wa", 1)], axis=0)
    kv_term = dot32(normed_share, kv_low_all, ((0,), (0,)))
    first_grad = dot32(query_low, query_full, ((1,), (1,))) + dot32(kv_low, kv_full, ((1,), (1,)))
    scaled = first_grad * gain_one
    input_back = inverse_one * (
        scaled - normed_one * jnp.mean(scaled * normed_one, axis=-1, keepdims=True)
    )
    tokens_grad = (residual_grad + input_back).astype(jnp.bfloat16).reshape(tokens.shape)
    kv_sides = to_side(kv_term.astype(jnp.bfloat16).reshape(contexts, each, kv_width), context)
    kv_sum = line_sum(side_sum(*kv_sides), context)
    early_near = side_sum(early_sides[0], after(early_sides[1], *kv_moved))
    early_sum = line_sum(early_near, context, kv_sides[1])
    query_weight_grad, out_sum = early_sum[:, :width], early_sum[:, width:]
    out_weight_grad = out_sum[:, :width].T
    router_weight_grad = out_sum[:, width : width + EXPERTS]
    norm_gain_2_grad = out_sum[:, width + EXPERTS]
    key_weight_grad, value_weight_grad = apart(kv_sum)
    mine = lambda full: lax.dynamic_slice_in_dim(full, (context * members + member) * each, each, 0)
    norm_gain_1_grad = (
        jnp.sum(mine(query_full).astype(jnp.float32) * query_weight_grad, axis=1)
        + jnp.sum(mine(kv_full).astype(jnp.float32) * kv_sum, axis=1)
    ) / mine(gain_one)

    line_zero = flip((line_sums[1].astype(jnp.float32) + nothing(sum_three)).astype(jnp.bfloat16), "ctx", 1)
    sum_zero = line_sums[0].astype(jnp.float32) + line_zero.astype(jnp.float32)
    expert_sums = [sum_zero, sum_one, sum_two, sum_three]
    expert_gate_grad = jnp.stack([total[0] for total in expert_sums]).astype(jnp.float32)
    expert_up_grad = jnp.stack([total[1] for total in expert_sums]).astype(jnp.float32)
    expert_down_grad = jnp.stack([total[2].T for total in expert_sums]).astype(jnp.float32)

    shared_sum = line_sum(side_sum(pair_keep, after(other_pair, kv_sides[1])), context)
    shared_sum = shared_sum.reshape(3, members, each, hidden_share).transpose(1, 0, 2, 3)
    shared_sum = lax.all_to_all(shared_sum, "wa", 0, 0, tiled=True)
    shared_gate_grad = shared_sum[:, 0].transpose(1, 0, 2).reshape(each, members * hidden_share)
    shared_up_grad = shared_sum[:, 1].transpose(1, 0, 2).reshape(each, members * hidden_share)
    shared_down_grad = shared_sum[:, 2].transpose(0, 2, 1).reshape(members * hidden_share, each)
    return (
        block_out,
        tokens_grad,
        norm_gain_1_grad,
        query_weight_grad,
        key_weight_grad,
        value_weight_grad,
        out_weight_grad,
        norm_gain_2_grad,
        router_weight_grad,
        shared_gate_grad,
        shared_up_grad,
        shared_down_grad,
        expert_gate_grad,
        expert_up_grad,
        expert_down_grad,
    )


def solution(mesh):
    return jax.shard_map(
        shards,
        mesh=mesh,
        in_specs=(
            P("wa", "ctx", None, None, None),
            P("wa", None),
            P("wa", "ctx", None, None, None),
            P("wa"),
            P("wa", None),
            P("wa", None),
            P("wa", None),
            P(None, "wa"),
            P("wa"),
            P("wa", None),
            P("wa", None),
            P("wa", None),
            P(None, "wa"),
            P("wa", None, None),
            P("wa", None, None),
            P("wa", None, None),
            P("wa", "ctx", None, None, None),
        ),
        out_specs=(
            P("wa", "ctx", None, None, None),
            P("wa", "ctx", None, None, None),
            P(("ctx", "wa")),
            P(("ctx", "wa"), None),
            P(("ctx", "wa"), None),
            P(("ctx", "wa"), None),
            P(None, ("ctx", "wa")),
            P(("ctx", "wa")),
            P(("ctx", "wa"), None),
            P(("ctx", "wa"), None),
            P(("ctx", "wa"), None),
            P(None, ("ctx", "wa")),
            P("wa", "ctx", None),
            P("wa", "ctx", None),
            P("wa", None, "ctx"),
        ),
        check_vma=False,
    )
```
